256 devices in a mesh: aa: 16 (over x_lo, y, core), ba: 16 (over z, x_hi).
Axes of the slice: x: 4 (x_hi: 2, x_lo: 2; x = x_hi * 2 + x_lo), y: 4, z: 8, core: 2. Of those that a mesh axis runs over, the one named last changes fastest.
Arguments:
- query: bfloat16 [6144, 4096], P('aa', 'ba'), may hold values from -28 to 28
- keys: bfloat16 [6144, 2048], P('aa', 'ba'), may hold values from -6 to 6
- values: bfloat16 [6144, 2048], P('aa', 'ba'), may hold values from -6 to 6
- grad_out: bfloat16 [6144, 5376], P('aa', 'ba'), may hold values from -6 to 6
- segment_ids: int32 [6144], P('aa'), may hold values from 0 to 5, never falling along the last dimension, each value on 1 to 3456 neighbouring positions
- w_query: bfloat16 [5376, 4096], P(None, 'ba'), may hold values from -0.125 to 0.125
- w_key: bfloat16 [5376, 2048], P(None, 'ba'), may hold values from -0.1875 to 0.1875
- w_value: bfloat16 [5376, 2048], P(None, 'ba'), may hold values from -0.1875 to 0.1875
- w_out: bfloat16 [4096, 5376], P('ba'), may hold values from -0.078125 to 0.078125
Outputs:
- grad_input: bfloat16 [6144, 5376], P('aa', 'ba')
The draws below stay inside these ranges and needn't reach their ends.
Inputs may be any that keep to these rules, and one draw needn't show every extreme that they name: `segment_ids`: never falls along the sequence; each document has at most 3456 positions.
All inputs are finite; a program needn't handle non-finite values.
Results may differ from the reference program's by a relative error of at most 0.019.
Values may be sent and summed in bfloat16 or wider, within the bound.
No kernel may reach another device: no remote copies, remote signals or barrier semaphores. Data moves between devices by JAX's collectives and lax.ppermute only.
A program may use at most 128 MiB of HBM per device.

```python
import math
import jax
import jax.numpy as jnp
import numpy as np
from jax import lax

D = 5376
HQ = 32
KVH = 16
HD = 128
DOCS = 6
TOKENS = 6144
DOC_MOST = 3456


def query_key_pair(key):
    base = jax.random.fold_in(key, 4111)
    key_q, key_k = jax.random.split(base, 2)
    query = jax.random.truncated_normal(key_q, -6.0, 6.0, (TOKENS, KVH, 2, HD), jnp.float32)
    keys = jax.random.truncated_normal(key_k, -6.0, 6.0, (TOKENS, KVH, HD), jnp.float32)
    return (query.reshape(TOKENS, HQ * HD), keys.reshape(TOKENS, KVH * HD))


def draw_query(key, part):
    return query_key_pair(key)[0].astype(jnp.bfloat16)


def draw_keys(key, part):
    return query_key_pair(key)[1].astype(jnp.bfloat16)


def spiked(array, key, source, target, parts, factor):
    def block_of(dim):
        return (jnp.arange(array.shape[dim]) // (array.shape[dim] // parts)).reshape((-1,) + (1,) * (array.ndim - 1 - dim))

    first = jax.random.permutation(key, parts)[block_of(target)]
    far = (block_of(target) + parts // 2) % parts
    return jnp.where((block_of(source) == first) | (block_of(source) == far), factor * array, array)


def shard_levels(stream_key, dims, cuts, smallest, largest):
    def one(axis_at, blocks):
        heights = jax.random.uniform(jax.random.fold_in(jax.random.fold_in(stream_key, 6), axis_at), (blocks,), jnp.float32, smallest / len(cuts), largest / len(cuts))
        return jnp.repeat(jnp.exp(heights), dims[axis_at] // blocks).reshape((-1,) + (1,) * (len(dims) - axis_at - 1))

    gain = one(*cuts[0])
    for cut in cuts[1:]:
        gain = gain * one(*cut)
    return gain


def split_up(number_of, total, limit, lean):
    weights = [(1 << 20) // math.isqrt(rank ** lean) + 1 for rank in range(2, number_of + 1)]
    spare, counts = total - limit - (number_of - 1), [1] * (number_of - 1)
    while spare > 0:
        movable = [i for i in range(number_of - 1) if counts[i] < limit]
        pool, remaining = sum([weights[i] for i in movable]), spare
        for i in movable:
            extra = min(limit - counts[i], max(1, remaining * weights[i] // pool), spare)
            counts[i] = counts[i] + extra
            spare = spare - extra
    return np.array([limit] + counts)


def uneven_parts(own_key, amount, total, most, lean):
    if amount == 2:
        one = jax.random.randint(own_key, (), max(1, total - most), min(most, total - 1) + 1)
        return jnp.stack([one, total - one])
    tallies = jnp.asarray(split_up(amount, total, most, lean), jnp.int32)
    twos = (amount - 1) // 2
    giver, receiver = tallies[1:1 + 2 * twos:2], tallies[2:2 + 2 * twos:2]
    room = jnp.minimum(giver - 1, most - receiver)
    moved = jax.random.randint(jax.random.fold_in(own_key, 1), (twos,), 0, 1 << 20) % (room + 1)
    tallies = tallies.at[1:1 + 2 * twos:2].set(giver - moved).at[2:2 + 2 * twos:2].set(receiver + moved)
    return tallies[jax.random.permutation(jax.random.fold_in(own_key, 2), amount)]


def noise(own_key, extent, width, limit, cuts=(), held_as=jnp.bfloat16):
    drawn = jax.random.normal(own_key, extent, jnp.float32) * width
    if len(cuts) > 0:
        drawn = shard_levels(own_key, extent, cuts, -0.22, 0.18) * drawn
    return jnp.clip(drawn, min=-limit, max=limit).astype(held_as)


def noise_with(key, shape, width, reach, cuts, heavy, kind=jnp.bfloat16):
    entries = width * jax.random.normal(key, shape, jnp.float32)
    if cuts:
        entries = entries * shard_levels(key, shape, cuts, -0.22, 0.18)
    return jnp.clip(spiked(entries, jax.random.fold_in(key, 3), *heavy), -reach, reach).astype(kind)


def setup_inputs(seed: int = 0) -> dict:
    key_of = jax.random.split(jax.random.key(seed), 10)
    return {
        "query": draw_query(jax.random.fold_in(key_of[9], 71), 0),
        "keys": draw_keys(jax.random.fold_in(key_of[9], 71), 0),
        "values": noise(key_of[2], (TOKENS, KVH * HD), 1.0, 6.0, ((0, 16), (1, 16))),
        "grad_out": noise(key_of[3], (TOKENS, D), 1.0, 6.0, ((0, 16), (1, 16))),
        "segment_ids": jnp.searchsorted(jnp.cumsum(uneven_parts(key_of[4], DOCS, TOKENS, DOC_MOST, 1)), jnp.arange(TOKENS), side="right").astype(jnp.int32),
        "w_query": noise_with(key_of[5], (D, HQ * HD), (HQ * HD) ** -0.5, 0.125, ((1, 16),), (1, 0, 16, 2.0)),
        "w_key": noise_with(key_of[6], (D, KVH * HD), (KVH * HD) ** -0.5, 0.1875, ((1, 16),), (1, 0, 16, 2.0)),
        "w_value": noise_with(key_of[7], (D, KVH * HD), (KVH * HD) ** -0.5, 0.1875, ((1, 16),), (1, 0, 16, 2.0)),
        "w_out": noise(key_of[8], (HQ * HD, D), D ** -0.5, 0.078125, ((0, 16),)),
    }


NEG_FILL = -1e30


def back_project(grad, weight):
    return lax.dot_general(grad, weight, (((1,), (1,)), ((), ())), preferred_element_type=jnp.float32)


def reference(query, keys, values, grad_out, segment_ids, w_query, w_key, w_value, w_out):
    scaling = (D / HQ) ** -0.5
    dout = back_project(grad_out, w_out).astype(jnp.bfloat16)
    position = jnp.arange(TOKENS, dtype=jnp.int32)
    allowed = (position[None, :] <= position[:, None]) & (segment_ids[None, :] == segment_ids[:, None])
    query_grp = query.reshape(TOKENS, KVH, 2, HD).transpose(1, 0, 2, 3)
    dout_grp = dout.reshape(TOKENS, KVH, 2, HD).transpose(1, 0, 2, 3)
    keys_grp = keys.reshape(TOKENS, KVH, HD).transpose(1, 0, 2)
    values_grp = values.reshape(TOKENS, KVH, HD).transpose(1, 0, 2)
    highest = lax.Precision.HIGHEST

    def one_group(items):
        query_four, dout_four, key_three, value_three = items
        query_f = query_four.astype(jnp.float32)
        dout_f = dout_four.astype(jnp.float32)
        key_f = key_three.astype(jnp.float32)
        value_f = value_three.astype(jnp.float32)
        scores = jnp.einsum("igd,jd->gij", query_f, key_f, precision=highest) * scaling
        masked = jnp.where(allowed, scores, NEG_FILL)
        top_val = jnp.max(masked, axis=-1)
        expo = jnp.where(allowed, jnp.exp(scores - top_val[..., None]), 0.0)
        lse = top_val + jnp.log(jnp.sum(expo, axis=-1))
        probs = jnp.where(allowed, jnp.exp(scores - lse[..., None]), 0.0)
        dprobs = jnp.einsum("igd,jd->gij", dout_f, value_f, precision=highest)
        delta = jnp.sum(probs * dprobs, axis=-1)
        dscores = probs * (dprobs - delta[..., None])
        probs_low = lax.optimization_barrier(probs.astype(jnp.bfloat16)).astype(jnp.float32)
        dscores_low = lax.optimization_barrier(dscores.astype(jnp.bfloat16)).astype(jnp.float32)
        grad_v = jnp.einsum("gij,igd->jd", probs_low, dout_f, precision=highest)
        grad_k = jnp.einsum("gij,igd->jd", dscores_low, query_f, precision=highest) * scaling
        grad_q = jnp.einsum("gij,jd->igd", dscores_low, key_f, precision=highest) * scaling
        return grad_q, grad_k, grad_v

    grad_q, grad_k, grad_v = lax.map(one_group, (query_grp, dout_grp, keys_grp, values_grp))
    grad_q = grad_q.transpose(1, 0, 2, 3).reshape(TOKENS, HQ * HD).astype(jnp.bfloat16)
    grad_k = grad_k.transpose(1, 0, 2).reshape(TOKENS, KVH * HD).astype(jnp.bfloat16)
    grad_v = grad_v.transpose(1, 0, 2).reshape(TOKENS, KVH * HD).astype(jnp.bfloat16)
    total = back_project(grad_q, w_query) + back_project(grad_k, w_key) + back_project(grad_v, w_value)
    return total.astype(jnp.bfloat16)
```

```python
import math

import jax
import jax.numpy as jnp
from jax import lax
from jax.experimental import pallas as pl
from jax.experimental.pallas import tpu as pltpu
from jax.sharding import Mesh
from jax.sharding import PartitionSpec as P

D = 5376
HQ = 32
HD = 128
DOCS = 6
DOC_MOST = 3456
BA = ("ba_0", "ba_1")
NEG_FILL = -1e30
SCALE = (D / HQ) ** (-0.5)
SCALE2 = SCALE * math.log2(math.e)
F32 = jnp.float32
BF16 = jnp.bfloat16


def dot(a, b):
    return lax.dot_general(a, b, (((1,), (0,)), ((), ())), preferred_element_type=F32)


def row_limits(info, qseg_ref, rows):
    seg = qseg_ref[...]
    start = jnp.zeros((1, rows), jnp.int32)
    for s in range(DOCS):
        start = jnp.where(seg == s, info[2 + s], start)
    pos = info[1] + lax.broadcasted_iota(jnp.int32, (1, rows), 1)
    return start, pos


def stats_kernel(reach, info, qseg_ref, q_ref, *refs):
    kv_refs = refs[: reach + 1]
    lse_ref, out_ref, qt_ref, m_ref, l_ref = refs[reach + 1 :]
    rows = q_ref.shape[0]
    start, pos = row_limits(info, qseg_ref, rows)
    qt_ref[...] = q_ref[...].T
    m_ref[...] = jnp.full(m_ref.shape, NEG_FILL, F32)
    l_ref[...] = jnp.zeros(l_ref.shape, F32)
    out_ref[...] = jnp.zeros(out_ref.shape, F32)
    key_at = lax.broadcasted_iota(jnp.int32, (rows, rows), 0)
    for b in range(reach + 1):

        @pl.when(b >= info[0])
        def _(b=b):
            first = info[1] + (b - reach) * rows
            allowed = (key_at >= start - first) & (key_at <= pos - first)
            kb = kv_refs[b][:, :HD]
            vt = kv_refs[b][:, HD:].T
            for h in range(2):
                qt = qt_ref[h * HD : (h + 1) * HD, :]
                s = jnp.where(allowed, dot(kb, qt) * SCALE2, NEG_FILL)
                m_old = m_ref[h : h + 1, :]
                m_new = jnp.maximum(m_old, jnp.max(s, axis=0, keepdims=True))
                p = jnp.where(allowed, jnp.exp2(s - m_new), 0.0)
                back = jnp.exp2(m_old - m_new)
                l_ref[h : h + 1, :] = l_ref[h : h + 1, :] * back + jnp.sum(p, axis=0, keepdims=True)
                m_ref[h : h + 1, :] = m_new
                high = p.astype(BF16)
                low = (p - high.astype(F32)).astype(BF16)
                o = out_ref[h * HD : (h + 1) * HD, :]
                out_ref[h * HD : (h + 1) * HD, :] = o * back + (dot(vt, high) + dot(vt, low))

    lse_ref[...] = m_ref[...] + jnp.log2(l_ref[...])
    for h in range(2):
        out_ref[h * HD : (h + 1) * HD, :] = out_ref[h * HD : (h + 1) * HD, :] / l_ref[h : h + 1, :]


def grads_kernel(reach, info, qseg_ref, q_ref, doutt_ref, lse_ref, out_ref, *refs):
    kv_refs = refs[: reach + 1]
    gqt_ref = refs[reach + 1]
    gkv_refs = refs[reach + 2 : 2 * reach + 3]
    qt_ref, dout_ref, delta_ref, acc_ref = refs[2 * reach + 3 :]
    rows = q_ref.shape[0]
    start, pos = row_limits(info, qseg_ref, rows)
    qt_ref[...] = q_ref[...].T
    dout_ref[...] = doutt_ref[...].T
    for h in range(2):
        part = slice(h * HD, (h + 1) * HD)
        delta_ref[h : h + 1, :] = jnp.sum(
            doutt_ref[part, :].astype(F32) * out_ref[part, :], axis=0, keepdims=True
        )
    acc_ref[...] = jnp.zeros(acc_ref.shape, F32)
    key_at = lax.broadcasted_iota(jnp.int32, (rows, rows), 0)
    for b in range(reach + 1):

        @pl.when(b >= info[0])
        def _(b=b):
            first = info[1] + (b - reach) * rows
            allowed = (key_at >= start - first) & (key_at <= pos - first)
            kb = kv_refs[b][:, :HD]
            vb = kv_refs[b][:, HD:]
            kt = kb.T
            gk = gv = None
            for h in range(2):
                part = slice(h * HD, (h + 1) * HD)
                s = dot(kb, qt_ref[part, :]) * SCALE2
                dp = dot(vb, doutt_ref[part, :])
                p = jnp.where(allowed, jnp.exp2(s - lse_ref[h : h + 1, :]), 0.0)
                ds = (p * (dp - delta_ref[h : h + 1, :])).astype(BF16)
                add_v = dot(p.astype(BF16), dout_ref[:, part])
                add_k = dot(ds, q_ref[:, part])
                gv = add_v if h == 0 else gv + add_v
                gk = add_k if h == 0 else gk + add_k
                acc_ref[part, :] += dot(kt, ds)
            gkv_refs[b][:, :HD] = (gk * SCALE).astype(BF16)
            gkv_refs[b][:, HD:] = gv.astype(BF16)

        @pl.when(b < info[0])
        def _(b=b):
            gkv_refs[b][...] = jnp.zeros(gkv_refs[b].shape, BF16)

    gqt_ref[...] = (acc_ref[...] * SCALE).astype(BF16)


def attention_stats(info, qseg, query, window):
    reach = len(window) - 1
    rows = query.shape[0]
    vmem = pl.BlockSpec(memory_space=pltpu.VMEM)
    return pl.pallas_call(
        lambda *refs: stats_kernel(reach, *refs),
        name="attention_stats",
        out_shape=(
            jax.ShapeDtypeStruct((2, rows), F32),
            jax.ShapeDtypeStruct((2 * HD, rows), F32),
        ),
        in_specs=[pl.BlockSpec(memory_space=pltpu.SMEM)] + [vmem] * (reach + 3),
        out_specs=(vmem, vmem),
        scratch_shapes=[
            pltpu.VMEM((2 * HD, rows), BF16),
            pltpu.VMEM((2, rows), F32),
            pltpu.VMEM((2, rows), F32),
        ],
    )(info, qseg, query, *window)


def attention_grads(info, qseg, query, doutt, lse, out, window):
    reach = len(window) - 1
    rows = query.shape[0]
    vmem = pl.BlockSpec(memory_space=pltpu.VMEM)
    result = pl.pallas_call(
        lambda *refs: grads_kernel(reach, *refs),
        name="attention_grads",
        out_shape=(jax.ShapeDtypeStruct((2 * HD, rows), BF16),)
        + (jax.ShapeDtypeStruct((rows, 2 * HD), BF16),) * (reach + 1),
        in_specs=[pl.BlockSpec(memory_space=pltpu.SMEM)] + [vmem] * (reach + 6),
        out_specs=(vmem,) * (reach + 2),
        scratch_shapes=[
            pltpu.VMEM((2 * HD, rows), BF16),
            pltpu.VMEM((rows, 2 * HD), BF16),
            pltpu.VMEM((2, rows), F32),
            pltpu.VMEM((2 * HD, rows), F32),
        ],
    )(info, qseg, query, doutt, lse, out, *window)
    return result[0], result[1:]


def sent_to_all(x, axis):
    copies = jnp.broadcast_to(x, (lax.axis_size(axis), *x.shape))
    return lax.all_to_all(copies, axis, split_axis=0, concat_axis=0, tiled=True)


def local(query, keys, values, grad_out, segment_ids, w_query, w_key, w_value, w_out):
    count = lax.axis_size("aa")
    own = lax.axis_index("aa")
    rows = query.shape[0]
    reach = min(count - 1, -(-(DOC_MOST - 1) // rows))
    all_seg = sent_to_all(segment_ids, "aa").reshape(-1)
    block = jnp.concatenate((keys, values), axis=1)
    window = [
        lax.ppermute(block, "aa", [(i, i + d) for i in range(count - d)])
        for d in range(reach, 0, -1)
    ] + [block]
    gathered = grad_out.T
    for axis in reversed(BA):
        gathered = lax.all_gather(gathered, axis, axis=0, tiled=True)
    starts = jnp.sum(
        (all_seg[None, :] < jnp.arange(DOCS, dtype=jnp.int32)[:, None]).astype(jnp.int32), axis=1
    )
    first_start = jnp.sum((all_seg < segment_ids[0]).astype(jnp.int32))
    lowest = first_start // rows - own + reach
    info = jnp.concatenate((jnp.stack((lowest, own * rows)), starts))
    qseg = segment_ids[None, :]
    lse, out = attention_stats(info, qseg, query, window)
    doutt = dot(w_out, gathered).astype(BF16)
    gqt, partial = attention_grads(info, qseg, query, doutt, lse, out, window)
    total = partial[reach].astype(F32)
    for d in range(1, reach + 1):
        total = total + lax.ppermute(
            partial[reach - d], "aa", [(i + d, i) for i in range(count - d)]
        ).astype(F32)
    gkvt = total.astype(BF16).T
    result = (
        dot(w_query, gqt) + dot(w_key, gkvt[:HD]) + dot(w_value, gkvt[HD:])
    ).astype(BF16)
    for axis in BA:
        result = lax.psum_scatter(result, axis, scatter_dimension=0, tiled=True)
    return result.T


def solution(mesh):
    finer = Mesh(mesh.devices.reshape(mesh.shape["aa"], 8, 2), ("aa", "ba_0", "ba_1"))
    return jax.shard_map(
        local,
        mesh=finer,
        in_specs=(
            P("aa", BA),
            P("aa", BA),
            P("aa", BA),
            P("aa", BA),
            P("aa"),
            P(None, BA),
            P(None, BA),
            P(None, BA),
            P(BA, None),
        ),
        out_specs=P("aa", BA),
        check_vma=False,
    )
```

```python
import math

import jax
import jax.numpy as jnp
from jax import lax
from jax.experimental import pallas as pl
from jax.experimental.pallas import tpu as pltpu
from jax.sharding import Mesh
from jax.sharding import PartitionSpec as P

D = 5376
HQ = 32
HD = 128
DOCS = 6
DOC_MOST = 3456
ROWS = 384
HALF = 5
BLOCKS = 2 * HALF
SEG_ROWS = 16
PACKED = ROWS + SEG_ROWS
FEATS = 336
RING = 8
AA = ("xl", "y", "core")
BA = ("z", "xh")
NEG_FILL = -1e30
SCALE = (D / HQ) ** (-0.5)
SCALE2 = SCALE * math.log2(math.e)
F32 = jnp.float32
BF16 = jnp.bfloat16
VMEM = pl.BlockSpec(memory_space=pltpu.VMEM)
SMEM = pl.BlockSpec(memory_space=pltpu.SMEM)
ANY = pl.BlockSpec(memory_space=pl.ANY)


def dot(a, b):
    return lax.dot_general(a, b, (((1,), (0,)), ((), ())), preferred_element_type=F32)


def load_window(kv_refs, buf, sem):
    copies = [pltpu.make_async_copy(kv_refs[b], buf.at[b], sem.at[b]) for b in range(BLOCKS)]
    for c in copies:
        c.start()
    return copies


def stats_kernel(own_ref, qseg_ref, q_ref, *refs):
    kv_refs = refs[:BLOCKS]
    lse_ref, out_ref, start_ref, low_ref, buf, qt_ref, m_ref, l_ref, sem = refs[BLOCKS:]
    copies = load_window(kv_refs, buf, sem)
    own = own_ref[0]
    qt_ref[...] = q_ref[...].T
    m_ref[...] = jnp.full(m_ref.shape, NEG_FILL, F32)
    l_ref[...] = jnp.zeros(l_ref.shape, F32)
    out_ref[...] = jnp.zeros(out_ref.shape, F32)
    seg = qseg_ref[...]
    seg0 = jnp.min(seg, axis=1, keepdims=True)
    for c in copies:
        c.wait()
    count = jnp.zeros((SEG_ROWS, HD), jnp.int32)
    line = lax.broadcasted_iota(jnp.int32, (SEG_ROWS, HD), 0)
    for b in range(BLOCKS - 1):
        ids = buf[b, ROWS:, :HD].astype(F32).astype(jnp.int32)
        before = (line < ROWS // HD) & (ids < seg0) & (own + b >= BLOCKS - 1)
        count = count + before.astype(jnp.int32)
    start0 = jnp.sum(count) + jnp.maximum(own - (BLOCKS - 1), 0) * ROWS
    start = jnp.zeros((1, ROWS), jnp.int32) + start0
    for s in range(1, DOCS):
        here = own * ROWS + jnp.sum((seg < s).astype(jnp.int32), axis=1, keepdims=True)
        start = jnp.where((seg == s) & (seg > seg0), here, start)
    start_ref[...] = start
    lowest = lax.div(start0, ROWS) - own + (BLOCKS - 1)
    low_ref[0] = lowest
    pos = own * ROWS + lax.broadcasted_iota(jnp.int32, (1, ROWS), 1)
    key_at = lax.broadcasted_iota(jnp.int32, (ROWS, ROWS), 0)

    def one_block(b, carry):
        first = (own + b - (BLOCKS - 1)) * ROWS
        allowed = (key_at >= start - first) & (key_at <= pos - first)
        kb = buf[b, :ROWS, :HD]
        vt = buf[b, :ROWS, HD:].T
        for h in range(2):
            part = slice(h * HD, (h + 1) * HD)
            s = jnp.where(allowed, dot(kb, qt_ref[part, :]) * SCALE2, NEG_FILL)
            m_old = m_ref[h : h + 1, :]
            m_new = jnp.maximum(m_old, jnp.max(s, axis=0, keepdims=True))
            p = jnp.exp2(s - m_new)
            back = jnp.exp2(m_old - m_new)
            l_ref[h : h + 1, :] = l_ref[h : h + 1, :] * back + jnp.sum(p, axis=0, keepdims=True)
            m_ref[h : h + 1, :] = m_new
            high = p.astype(BF16)
            low = (p - high.astype(F32)).astype(BF16)
            out_ref[part, :] = out_ref[part, :] * back + (dot(vt, high) + dot(vt, low))
        return carry

    lax.fori_loop(lowest, BLOCKS, one_block, 0)
    lse_ref[...] = m_ref[...] + jnp.log2(l_ref[...])
    for h in range(2):
        part = slice(h * HD, (h + 1) * HD)
        out_ref[part, :] = out_ref[part, :] / l_ref[h : h + 1, :]


def grads_kernel(own_ref, low_ref, start_ref, q_ref, doutt_ref, lse_ref, out_ref, *refs):
    kv_refs = refs[:BLOCKS]
    gqt_ref, mine_ref, theirs_ref, buf, qt_ref, dout_ref, delta_ref, acc_ref, sem = refs[BLOCKS:]
    copies = load_window(kv_refs, buf, sem)
    own = own_ref[0]
    lowest = low_ref[0]
    qt_ref[...] = q_ref[...].T
    dout_ref[...] = doutt_ref[...].T
    for h in range(2):
        part = slice(h * HD, (h + 1) * HD)
        delta_ref[h : h + 1, :] = jnp.sum(
            doutt_ref[part, :].astype(F32) * out_ref[part, :], axis=0, keepdims=True
        )
    acc_ref[...] = jnp.zeros(acc_ref.shape, F32)
    start = start_ref[...]
    pos = own * ROWS + lax.broadcasted_iota(jnp.int32, (1, ROWS), 1)
    key_at = lax.broadcasted_iota(jnp.int32, (ROWS, ROWS), 0)
    for c in copies:
        c.wait()

    def one_block(b, target, d):
        @pl.when(b >= lowest)
        def _():
            first = (own + b - (BLOCKS - 1)) * ROWS
            allowed = (key_at >= start - first) & (key_at <= pos - first)
            kb = buf[b, :ROWS, :HD]
            vb = buf[b, :ROWS, HD:]
            kt = kb.T
            gk = gv = None
            for h in range(2):
                part = slice(h * HD, (h + 1) * HD)
                s = dot(kb, qt_ref[part, :]) * SCALE2
                dp = dot(vb, doutt_ref[part, :])
                p = jnp.where(allowed, jnp.exp2(s - lse_ref[h : h + 1, :]), 0.0)
                ds = (p * (dp - delta_ref[h : h + 1, :])).astype(BF16)
                add_v = dot(p.astype(BF16), dout_ref[:, part])
                add_k = dot(ds, q_ref[:, part])
                gv = add_v if h == 0 else gv + add_v
                gk = add_k if h == 0 else gk + add_k
                acc_ref[part, :] += dot(kt, ds)
            target[d, :, :HD] = (gk * SCALE).astype(BF16)
            target[d, :, HD:] = gv.astype(BF16)

        @pl.when(b < lowest)
        def _():
            target[d] = jnp.zeros((ROWS, 2 * HD), BF16)

    def two_blocks(d, carry):
        one_block(BLOCKS - 1 - 2 * d, mine_ref, d)
        one_block(BLOCKS - 2 - 2 * d, theirs_ref, d)
        return carry

    lax.fori_loop(0, HALF, two_blocks, 0)
    gqt_ref[...] = (acc_ref[...] * SCALE).astype(BF16)


def attention_stats(own, qseg, query, window):
    return pl.pallas_call(
        stats_kernel,
        name="attention_stats",
        out_shape=(
            jax.ShapeDtypeStruct((2, ROWS), F32),
            jax.ShapeDtypeStruct((2 * HD, ROWS), F32),
            jax.ShapeDtypeStruct((1, ROWS), jnp.int32),
            jax.ShapeDtypeStruct((1,), jnp.int32),
        ),
        in_specs=[SMEM, VMEM, VMEM] + [ANY] * BLOCKS,
        out_specs=(VMEM, VMEM, VMEM, SMEM),
        scratch_shapes=[
            pltpu.VMEM((BLOCKS, PACKED, 2 * HD), BF16),
            pltpu.VMEM((2 * HD, ROWS), BF16),
            pltpu.VMEM((2, ROWS), F32),
            pltpu.VMEM((2, ROWS), F32),
            pltpu.SemaphoreType.DMA((BLOCKS,)),
        ],
    )(own, qseg, query, *window)


def attention_grads(own, stats, query, doutt, window):
    lse, out, start, lowest = stats
    return pl.pallas_call(
        grads_kernel,
        name="attention_grads",
        out_shape=(
            jax.ShapeDtypeStruct((2 * HD, ROWS), BF16),
            jax.ShapeDtypeStruct((HALF, ROWS, 2 * HD), BF16),
            jax.ShapeDtypeStruct((HALF, ROWS, 2 * HD), BF16),
        ),
        in_specs=[SMEM, SMEM] + [VMEM] * 5 + [ANY] * BLOCKS,
        out_specs=(VMEM, VMEM, VMEM),
        scratch_shapes=[
            pltpu.VMEM((BLOCKS, PACKED, 2 * HD), BF16),
            pltpu.VMEM((2 * HD, ROWS), BF16),
            pltpu.VMEM((ROWS, 2 * HD), BF16),
            pltpu.VMEM((2, ROWS), F32),
            pltpu.VMEM((2 * HD, ROWS), F32),
            pltpu.SemaphoreType.DMA((BLOCKS,)),
        ],
    )(own, lowest, start, query, doutt, lse, out, *window)


def join_kernel(core_ref, mine_ref, got_ref, own_ref, *send_refs):
    core = core_ref[0]
    for d in range(HALF + 1):
        at = d - core
        inside = (at >= 0) & (at < HALF)
        other = got_ref[jnp.clip(at, 0, HALF - 1)].astype(F32)
        total = jnp.where(inside, other, 0.0)
        if d < HALF:
            total = total + mine_ref[d].astype(F32)
        if d == 0:
            own_ref[...] = total
        else:
            send_refs[d - 1][...] = total.astype(BF16)


def join_partials(core, mine, got):
    shape = (ROWS, 2 * HD)
    result = pl.pallas_call(
        join_kernel,
        name="join_partials",
        out_shape=(jax.ShapeDtypeStruct(shape, F32),) + (jax.ShapeDtypeStruct(shape, BF16),) * HALF,
        in_specs=[SMEM, VMEM, VMEM],
        out_specs=(VMEM,) * (HALF + 1),
    )(core, mine, got)
    return result[0], result[1:]


def total_kernel(own_ref, *refs):
    total = own_ref[...]
    for ref in refs[:HALF]:
        total = total + ref[...].astype(F32)
    refs[HALF][...] = total.astype(BF16).T


def total_partials(own, parts):
    return pl.pallas_call(
        total_kernel,
        name="total_partials",
        out_shape=jax.ShapeDtypeStruct((2 * HD, ROWS), BF16),
        in_specs=[VMEM] * (HALF + 1),
        out_specs=VMEM,
    )(own, *parts)


def project_kernel(deltas, at_ref, *refs):
    wq, wk, wv, pa, pb, gq, gkv, gq2, gkv2 = refs[:9]
    outs = refs[9 : 9 + len(deltas)]
    bq, bk, bv, bp, sem = refs[9 + len(deltas) :]
    z, xh, core = at_ref[0], at_ref[1], at_ref[2]
    copies = []
    for n, delta in enumerate(deltas):
        chunk = lax.rem(z + delta + RING, RING)
        rows = pl.ds(pl.multiple_of((2 * chunk + xh) * FEATS, 16), FEATS)
        mine = [
            pltpu.make_async_copy(w.at[rows, :], b.at[n], sem.at[n, i])
            for i, (w, b) in enumerate(((wq, bq), (wk, bk), (wv, bv)))
        ]
        for c in mine:
            c.start()
        half = lax.div(chunk, RING // 2)
        inner = lax.rem(chunk, RING // 2)

        @pl.when(half == core)
        def _(n=n, inner=inner):
            pltpu.make_async_copy(pa.at[inner], bp.at[n], sem.at[n, 3]).start()

        @pl.when(half != core)
        def _(n=n, inner=inner):
            pltpu.make_async_copy(pb.at[inner], bp.at[n], sem.at[n, 3]).start()

        copies.append(mine + [pltpu.make_async_copy(pa.at[0], bp.at[n], sem.at[n, 3])])
    for n in range(len(deltas)):
        for c in copies[n]:
            c.wait()
        total = dot(bq[n], gq[...]) + dot(bk[n], gkv[:HD, :]) + dot(bv[n], gkv[HD:, :])
        total = total + dot(bp[n, :, : 2 * HD], gq2[...]) + dot(bp[n, :, 2 * HD :], gkv2[...])
        outs[n][...] = total.astype(outs[n].dtype)


def project(deltas, at, weights, far, grads, kind):
    n = len(deltas)
    return pl.pallas_call(
        lambda *refs: project_kernel(deltas, *refs),
        name="project",
        out_shape=(jax.ShapeDtypeStruct((FEATS, ROWS), kind),) * n,
        in_specs=[SMEM] + [ANY] * 5 + [VMEM] * 4,
        out_specs=(VMEM,) * n,
        scratch_shapes=[
            pltpu.VMEM((n, FEATS, 2 * HD), BF16),
            pltpu.VMEM((n, FEATS, HD), BF16),
            pltpu.VMEM((n, FEATS, HD), BF16),
            pltpu.VMEM((n, FEATS, 4 * HD), BF16),
            pltpu.SemaphoreType.DMA((n, 4)),
        ],
    )(at, *weights, *far, *grads)


def swapped(x, axis):
    return lax.ppermute(x, axis, [(0, 1), (1, 0)])


def chip_pairs(d):
    return [(i, i + 2 * d) for i in range(lax.axis_size(AA) - 2 * d) if d < HALF or i % 2]


def chips_on(x, d):
    return lax.ppermute(x, AA, chip_pairs(d))


def chips_back(x, d):
    return lax.ppermute(x, AA, [(j, i) for i, j in chip_pairs(d)])


def round_z(x, step):
    return lax.ppermute(x, "z", [(i, (i + step) % RING) for i in range(RING)])


def local(query, keys, values, grad_out, segment_ids, w_query, w_key, w_value, w_out):
    core = lax.axis_index("core")
    z = lax.axis_index("z")
    xh = lax.axis_index("xh")
    own = lax.axis_index(AA)[None]
    at = jnp.stack((z, xh, core))
    ids = jnp.pad(
        segment_ids.astype(BF16).reshape(ROWS // HD, HD),
        ((0, SEG_ROWS - ROWS // HD), (0, HD)),
    )
    block = jnp.concatenate((jnp.concatenate((keys, values), axis=1), ids), axis=0)
    twins = [block] + [chips_on(block, d) for d in range(1, HALF + 1)]
    others = [
        swapped(jnp.where(core == 1, twins[d + 1], twins[d]), "core") for d in range(HALF)
    ]
    window = [None] * BLOCKS
    for d in range(HALF):
        window[BLOCKS - 1 - 2 * d] = twins[d]
        window[BLOCKS - 2 - 2 * d] = others[d]
    gathered = grad_out.T
    for axis in reversed(BA):
        gathered = lax.all_gather(gathered, axis, axis=0, tiled=True)
    wanted = [
        lax.dynamic_index_in_dim(w.reshape(2, RING // 2, 2, FEATS, -1), core, 0, keepdims=False)
        for w in (w_query, w_key, w_value)
    ]
    wanted = [lax.dynamic_index_in_dim(w, 1 - xh, 1, keepdims=False) for w in wanted]
    far_mine = swapped(jnp.concatenate(wanted, axis=2), "xh")
    far_other = swapped(far_mine, "core")

    stats = attention_stats(own, segment_ids[None, :], query, window)
    doutt = dot(w_out, gathered).astype(BF16)
    gqt, mine, theirs = attention_grads(own, stats, query, doutt, window)
    gqt_far = swapped(gqt, "xh")
    own_total, sends = join_partials(core[None], mine, swapped(theirs, "core"))
    parts = [chips_back(sends[d - 1], d) for d in range(HALF, 0, -1)]
    gkvt = total_partials(own_total, parts)
    gkvt_far = swapped(gkvt, "xh")

    weights = (w_query, w_key, w_value)
    far = (far_mine, far_other)
    grads = (gqt, gkvt, gqt_far, gkvt_far)
    ahead, behind = project((4, -3), at, weights, far, grads, BF16)
    rest = project((3, -2, 2, -1, 1, 0), at, weights, far, grads, F32)
    ahead = round_z(ahead, 1)
    behind = round_z(behind, -1)
    for add_ahead, add_behind in ((rest[0], rest[1]), (rest[2], rest[3])):
        ahead = round_z((ahead.astype(F32) + add_ahead).astype(BF16), 1)
        behind = round_z((behind.astype(F32) + add_behind).astype(BF16), -1)
    ahead = round_z((ahead.astype(F32) + rest[4]).astype(BF16), 1)
    result = (ahead.astype(F32) + behind.astype(F32) + rest[5]).astype(BF16)
    return result.T


def solution(mesh):
    finer = Mesh(mesh.devices.reshape(2, 4, 2, RING, 2), AA + BA)
    return jax.shard_map(
        local,
        mesh=finer,
        in_specs=(
            P(AA, BA),
            P(AA, BA),
            P(AA, BA),
            P(AA, BA),
            P(AA),
            P(None, BA),
            P(None, BA),
            P(None, BA),
            P(BA, None),
        ),
        out_specs=P(AA, BA),
        check_vma=False,
    )
```

```python
import math

import jax
import jax.numpy as jnp
from jax import lax
from jax.experimental import pallas as pl
from jax.experimental.pallas import tpu as pltpu
from jax.sharding import Mesh
from jax.sharding import PartitionSpec as P

D = 5376
HQ = 32
HD = 128
DOCS = 6
DOC_MOST = 3456
ROWS = 384
HALF = 5
BLOCKS = 2 * HALF
SEG_ROWS = 16
PACKED = ROWS + SEG_ROWS
FEATS = 336
CHUNK = 384
WINDOW = 512
NEAR = 6
RING = 8
AA = ("xl", "y", "core")
BA = ("z", "xh")
NEG_FILL = -1e30
SCALE = (D / HQ) ** (-0.5)
SCALE2 = SCALE * math.log2(math.e)
F32 = jnp.float32
BF16 = jnp.bfloat16
VMEM = pl.BlockSpec(memory_space=pltpu.VMEM)
SMEM = pl.BlockSpec(memory_space=pltpu.SMEM)
ANY = pl.BlockSpec(memory_space=pl.ANY)


def dot(a, b):
    return lax.dot_general(a, b, (((1,), (0,)), ((), ())), preferred_element_type=F32)


def load_window(kv_refs, buf, sem):
    copies = [
        pltpu.make_async_copy(ref, buf.at[b], sem.at[b]) for b, ref in enumerate(kv_refs)
    ]
    for c in copies:
        c.start()
    return copies


def stats_kernel(low, high, own_ref, qseg_ref, q_ref, *refs):
    near = high == BLOCKS
    count = high - low
    if near:
        kv_refs = refs[:count]
        m_ref, l_ref, out_ref, start_ref, buf, qt_ref, sem = refs[count:]
    else:
        m_in, l_in, out_in, start_in = refs[:4]
        kv_refs = refs[4 : 4 + count]
        lse_ref, out_ref, start_ref, low_ref, buf, qt_ref, m_ref, l_ref, sem = refs[4 + count :]
    copies = load_window(kv_refs, buf, sem)
    own = own_ref[0]
    qt_ref[...] = q_ref[...].T
    if near:
        m_ref[...] = jnp.full(m_ref.shape, NEG_FILL, F32)
        l_ref[...] = jnp.zeros(l_ref.shape, F32)
        out_ref[...] = jnp.zeros(out_ref.shape, F32)
    else:
        m_ref[...] = m_in[...]
        l_ref[...] = l_in[...]
        out_ref[...] = out_in[...]
    seg = qseg_ref[...]
    seg0 = jnp.min(seg, axis=1, keepdims=True)
    for c in copies:
        c.wait()
    before = jnp.zeros((SEG_ROWS, HD), jnp.int32)
    line = lax.broadcasted_iota(jnp.int32, (SEG_ROWS, HD), 0)
    for b in range(low, min(high, BLOCKS - 1)):
        ids = buf[b - low, ROWS:, :HD].astype(F32).astype(jnp.int32)
        hit = (line < ROWS // HD) & (ids < seg0) & (own + b >= BLOCKS - 1)
        before = before + hit.astype(jnp.int32)
    start0 = jnp.sum(before) + jnp.maximum(own + low - (BLOCKS - 1), 0) * ROWS
    first_next = (own + high - (BLOCKS - 1)) * ROWS
    start = jnp.zeros((1, ROWS), jnp.int32) + start0
    if near:
        for s in range(1, DOCS):
            here = own * ROWS + jnp.sum((seg < s).astype(jnp.int32), axis=1, keepdims=True)
            start = jnp.where((seg == s) & (seg > seg0), here, start)
        start_ref[...] = start
    else:
        start = jnp.where((seg == seg0) & (start0 < first_next), start, start_in[...])
        start_ref[...] = start
        start0 = jnp.min(start)
    lowest = lax.div(start0, ROWS) - own + (BLOCKS - 1)
    pos = own * ROWS + lax.broadcasted_iota(jnp.int32, (1, ROWS), 1)
    key_at = lax.broadcasted_iota(jnp.int32, (ROWS, ROWS), 0)

    def one_block(back_to, carry):
        b = high - 1 - back_to
        first = (own + b - (BLOCKS - 1)) * ROWS
        allowed = (key_at >= start - first) & (key_at <= pos - first)
        kb = buf[b - low, :ROWS, :HD]
        vt = buf[b - low, :ROWS, HD:].T
        for h in range(2):
            part = slice(h * HD, (h + 1) * HD)
            s = jnp.where(allowed, dot(kb, qt_ref[part, :]) * SCALE2, NEG_FILL)
            m_old = m_ref[h : h + 1, :]
            m_new = jnp.maximum(m_old, jnp.max(s, axis=0, keepdims=True))
            p = jnp.exp2(s - m_new)
            back = jnp.exp2(m_old - m_new)
            l_ref[h : h + 1, :] = l_ref[h : h + 1, :] * back + jnp.sum(p, axis=0, keepdims=True)
            m_ref[h : h + 1, :] = m_new
            out_ref[part, :] = out_ref[part, :] * back + dot(vt, p.astype(BF16))
        return carry

    lax.fori_loop(0, high - jnp.clip(lowest, low, high), one_block, 0)
    if not near:
        low_ref[0] = lowest
        lse_ref[...] = m_ref[...] + jnp.log2(l_ref[...])
        for h in range(2):
            part = slice(h * HD, (h + 1) * HD)
            out_ref[part, :] = out_ref[part, :] / l_ref[h : h + 1, :]


def grads_kernel(own_ref, low_ref, start_ref, q_ref, near_ref, far_ref, lse_ref, out_ref, *refs):
    kv_refs = refs[:BLOCKS]
    gqt_ref, mine_ref, theirs_ref = refs[BLOCKS : BLOCKS + 3]
    buf, qt_ref, dout_ref, doutt_ref, delta_ref, acc_ref, sem = refs[BLOCKS + 3 :]
    copies = load_window(kv_refs, buf, sem)
    own = own_ref[0]
    lowest = low_ref[0]
    qt_ref[...] = q_ref[...].T
    doutt_ref[...] = (near_ref[...] + far_ref[...].astype(F32)).astype(BF16)
    dout_ref[...] = doutt_ref[...].T
    for h in range(2):
        part = slice(h * HD, (h + 1) * HD)
        delta_ref[h : h + 1, :] = jnp.sum(
            doutt_ref[part, :].astype(F32) * out_ref[part, :], axis=0, keepdims=True
        )
    acc_ref[...] = jnp.zeros(acc_ref.shape, F32)
    start = start_ref[...]
    pos = own * ROWS + lax.broadcasted_iota(jnp.int32, (1, ROWS), 1)
    key_at = lax.broadcasted_iota(jnp.int32, (ROWS, ROWS), 0)
    for c in copies:
        c.wait()

    def one_block(b, target, d):
        @pl.when(b >= lowest)
        def _():
            first = (own + b - (BLOCKS - 1)) * ROWS
            allowed = (key_at >= start - first) & (key_at <= pos - first)
            kb = buf[b, :ROWS, :HD]
            vb = buf[b, :ROWS, HD:]
            kt = kb.T
            gk = gv = None
            for h in range(2):
                part = slice(h * HD, (h + 1) * HD)
                s = dot(kb, qt_ref[part, :]) * SCALE2
                dp = dot(vb, doutt_ref[part, :])
                p = jnp.where(allowed, jnp.exp2(s - lse_ref[h : h + 1, :]), 0.0)
                ds = (p * (dp - delta_ref[h : h + 1, :])).astype(BF16)
                add_v = dot(p.astype(BF16), dout_ref[:, part])
                add_k = dot(ds, q_ref[:, part])
                gv = add_v if h == 0 else gv + add_v
                gk = add_k if h == 0 else gk + add_k
                acc_ref[part, :] += dot(kt, ds)
            target[d, :, :HD] = (gk * SCALE).astype(BF16)
            target[d, :, HD:] = gv.astype(BF16)

        @pl.when(b < lowest)
        def _():
            target[d] = jnp.zeros((ROWS, 2 * HD), BF16)

    def two_blocks(d, carry):
        one_block(BLOCKS - 1 - 2 * d, mine_ref, d)
        one_block(BLOCKS - 2 - 2 * d, theirs_ref, d)
        return carry

    lax.fori_loop(0, HALF, two_blocks, 0)
    gqt_ref[...] = (acc_ref[...] * SCALE).astype(BF16)


def attention_stats(own, qseg, query, window, low, high, state=()):
    count = high - low
    row = jax.ShapeDtypeStruct((2, ROWS), F32)
    wide = jax.ShapeDtypeStruct((2 * HD, ROWS), F32)
    start = jax.ShapeDtypeStruct((1, ROWS), jnp.int32)
    lowest = jax.ShapeDtypeStruct((1,), jnp.int32)
    scratch = [
        pltpu.VMEM((count, PACKED, 2 * HD), BF16),
        pltpu.VMEM((2 * HD, ROWS), BF16),
    ]
    if state:
        scratch += [pltpu.VMEM((2, ROWS), F32), pltpu.VMEM((2, ROWS), F32)]
    return pl.pallas_call(
        lambda *refs: stats_kernel(low, high, *refs),
        name="stats_far" if state else "stats_near",
        out_shape=(row, wide, start, lowest) if state else (row, row, wide, start),
        in_specs=[SMEM, VMEM, VMEM] + [VMEM] * len(state) + [ANY] * count,
        out_specs=(VMEM, VMEM, VMEM, SMEM if state else VMEM),
        scratch_shapes=scratch + [pltpu.SemaphoreType.DMA((count,))],
    )(own, qseg, query, *state, *window[low:high])


def attention_grads(own, stats, query, near, far, window):
    lse, out, start, lowest = stats
    return pl.pallas_call(
        grads_kernel,
        name="attention_grads",
        out_shape=(
            jax.ShapeDtypeStruct((2 * HD, ROWS), BF16),
            jax.ShapeDtypeStruct((HALF, ROWS, 2 * HD), BF16),
            jax.ShapeDtypeStruct((HALF, ROWS, 2 * HD), BF16),
        ),
        in_specs=[SMEM, SMEM] + [VMEM] * 6 + [ANY] * BLOCKS,
        out_specs=(VMEM, VMEM, VMEM),
        scratch_shapes=[
            pltpu.VMEM((BLOCKS, PACKED, 2 * HD), BF16),
            pltpu.VMEM((2 * HD, ROWS), BF16),
            pltpu.VMEM((ROWS, 2 * HD), BF16),
            pltpu.VMEM((2 * HD, ROWS), BF16),
            pltpu.VMEM((2, ROWS), F32),
            pltpu.VMEM((2 * HD, ROWS), F32),
            pltpu.SemaphoreType.DMA((BLOCKS,)),
        ],
    )(own, lowest, start, query, near, far, lse, out, *window)


def split_kernel(at_ref, w_ref, own_ref, send_ref, buf, sem):
    z_half = at_ref[2] * (RING // 2)
    xh = at_ref[1]
    chunks = [(own_ref, i, 2 * i + xh) for i in range(RING)]
    chunks += [(send_ref, i, 2 * (z_half + i) + (1 - xh)) for i in range(RING // 2)]
    copies = []
    for n, (_, _, chunk) in enumerate(chunks):
        base = jnp.minimum(lax.div(chunk * FEATS, HD) * HD, D - WINDOW)
        copy = pltpu.make_async_copy(
            w_ref.at[:, pl.ds(pl.multiple_of(base, HD), WINDOW)], buf.at[n], sem.at[n]
        )
        copy.start()
        copies.append((copy, chunk * FEATS - base))
    lane = lax.broadcasted_iota(jnp.int32, (2 * HD, CHUNK), 1)
    for n in (*range(RING, RING + RING // 2), *range(RING)):
        copy, skip = copies[n]
        copy.wait()
        moved = pltpu.roll(buf[n].astype(F32), lax.rem(WINDOW - skip, WINDOW), 1)[:, :CHUNK]
        ref, i, _ = chunks[n]
        ref[i] = jnp.where(lane < FEATS, moved, 0.0).astype(BF16)


def split_w_out(at, w_out):
    n = RING + RING // 2
    return pl.pallas_call(
        split_kernel,
        name="split_w_out",
        out_shape=(
            jax.ShapeDtypeStruct((RING, 2 * HD, CHUNK), BF16),
            jax.ShapeDtypeStruct((RING // 2, 2 * HD, CHUNK), BF16),
        ),
        in_specs=[SMEM, ANY],
        out_specs=(VMEM, VMEM),
        scratch_shapes=[
            pltpu.VMEM((n, 2 * HD, WINDOW), BF16),
            pltpu.SemaphoreType.DMA((n,)),
        ],
    )(at, w_out)


def dout_kernel(deltas, last, at_ref, *refs):
    n = len(deltas)
    own_ref, pa, pb = refs[:3]
    shards = refs[3 : 3 + n]
    if last:
        sum_in, near_ref, send_ref, wbuf, gbuf, sem = refs[3 + n :]
        total = sum_in[...]
    else:
        sum_ref, wbuf, gbuf, sem = refs[3 + n :]
        total = None
    z, core = at_ref[0], at_ref[2]
    copies = []
    for i, delta in enumerate(deltas):
        chunk = lax.rem(z + delta + RING, RING)
        half = lax.div(chunk, RING // 2)
        inner = lax.rem(chunk, RING // 2)
        mine = [
            pltpu.make_async_copy(own_ref.at[chunk], wbuf.at[i, : 2 * HD], sem.at[i, 0]),
            pltpu.make_async_copy(shards[i], gbuf.at[i, :FEATS], sem.at[i, 1]),
        ]
        for c in mine:
            c.start()

        @pl.when(half == core)
        def _(i=i, inner=inner):
            pltpu.make_async_copy(pa.at[inner], wbuf.at[i, 2 * HD :], sem.at[i, 2]).start()

        @pl.when(half != core)
        def _(i=i, inner=inner):
            pltpu.make_async_copy(pb.at[inner], wbuf.at[i, 2 * HD :], sem.at[i, 2]).start()

        copies.append(mine + [pltpu.make_async_copy(pa.at[0], wbuf.at[i, 2 * HD :], sem.at[i, 2])])
    for i in range(n):
        gbuf[i, FEATS:] = jnp.zeros((CHUNK - FEATS, ROWS), BF16)
    for i in range(n):
        for c in copies[i]:
            c.wait()
        add = dot(wbuf[i], gbuf[i])
        total = add if total is None else total + add
    if last:
        near_ref[...] = total[: 2 * HD]
        send_ref[...] = total[2 * HD :].astype(BF16)
    else:
        sum_ref[...] = total


def dout_part(deltas, at, own_w, far_w, shards, before=None):
    n = len(deltas)
    last = before is not None
    half = (2 * HD, ROWS)
    out = jax.ShapeDtypeStruct((4 * HD, ROWS), F32)
    if last:
        out = (jax.ShapeDtypeStruct(half, F32), jax.ShapeDtypeStruct(half, BF16))
    return pl.pallas_call(
        lambda *refs: dout_kernel(deltas, last, *refs),
        name="dout_last" if last else "dout_first",
        out_shape=out,
        in_specs=[SMEM] + [ANY] * (3 + n) + [VMEM] * last,
        out_specs=(VMEM, VMEM) if last else VMEM,
        scratch_shapes=[
            pltpu.VMEM((n, 4 * HD, CHUNK), BF16),
            pltpu.VMEM((n, CHUNK, ROWS), BF16),
            pltpu.SemaphoreType.DMA((n, 3)),
        ],
    )(at, own_w, *far_w, *shards, *((before,) if last else ()))


def join_kernel(core_ref, mine_ref, got_ref, own_ref, *send_refs):
    core = core_ref[0]
    for d in range(HALF + 1):
        at = d - core
        inside = (at >= 0) & (at < HALF)
        other = got_ref[jnp.clip(at, 0, HALF - 1)].astype(F32)
        total = jnp.where(inside, other, 0.0)
        if d < HALF:
            total = total + mine_ref[d].astype(F32)
        if d == 0:
            own_ref[...] = total
        else:
            send_refs[d - 1][...] = total.astype(BF16)


def join_partials(core, mine, got):
    shape = (ROWS, 2 * HD)
    result = pl.pallas_call(
        join_kernel,
        name="join_partials",
        out_shape=(jax.ShapeDtypeStruct(shape, F32),) + (jax.ShapeDtypeStruct(shape, BF16),) * HALF,
        in_specs=[SMEM, VMEM, VMEM],
        out_specs=(VMEM,) * (HALF + 1),
    )(core, mine, got)
    return result[0], result[1:]


def total_kernel(own_ref, *refs):
    total = own_ref[...]
    for ref in refs[:HALF]:
        total = total + ref[...].astype(F32)
    refs[HALF][...] = total.astype(BF16).T


def total_partials(own, parts):
    return pl.pallas_call(
        total_kernel,
        name="total_partials",
        out_shape=jax.ShapeDtypeStruct((2 * HD, ROWS), BF16),
        in_specs=[VMEM] * (HALF + 1),
        out_specs=VMEM,
    )(own, *parts)


def project_kernel(deltas, at_ref, *refs):
    wq, wk, wv, pa, pb, gq, gkv, gq2, gkv2 = refs[:9]
    outs = refs[9 : 9 + len(deltas)]
    bq, bk, bv, bp, sem = refs[9 + len(deltas) :]
    z, xh, core = at_ref[0], at_ref[1], at_ref[2]
    copies = []
    for n, delta in enumerate(deltas):
        chunk = lax.rem(z + delta + RING, RING)
        rows = pl.ds(pl.multiple_of((2 * chunk + xh) * FEATS, 16), FEATS)
        mine = [
            pltpu.make_async_copy(w.at[rows, :], b.at[n], sem.at[n, i])
            for i, (w, b) in enumerate(((wq, bq), (wk, bk), (wv, bv)))
        ]
        for c in mine:
            c.start()
        half = lax.div(chunk, RING // 2)
        inner = lax.rem(chunk, RING // 2)

        @pl.when(half == core)
        def _(n=n, inner=inner):
            pltpu.make_async_copy(pa.at[inner], bp.at[n], sem.at[n, 3]).start()

        @pl.when(half != core)
        def _(n=n, inner=inner):
            pltpu.make_async_copy(pb.at[inner], bp.at[n], sem.at[n, 3]).start()

        copies.append(mine + [pltpu.make_async_copy(pa.at[0], bp.at[n], sem.at[n, 3])])
    for n in range(len(deltas)):
        for c in copies[n]:
            c.wait()
        total = dot(bq[n], gq[...]) + dot(bk[n], gkv[:HD, :]) + dot(bv[n], gkv[HD:, :])
        total = total + dot(bp[n, :, : 2 * HD], gq2[...]) + dot(bp[n, :, 2 * HD :], gkv2[...])
        outs[n][...] = total.astype(outs[n].dtype)


def project(deltas, at, weights, far, grads, kind):
    n = len(deltas)
    return pl.pallas_call(
        lambda *refs: project_kernel(deltas, *refs),
        name="project",
        out_shape=(jax.ShapeDtypeStruct((FEATS, ROWS), kind),) * n,
        in_specs=[SMEM] + [ANY] * 5 + [VMEM] * 4,
        out_specs=(VMEM,) * n,
        scratch_shapes=[
            pltpu.VMEM((n, FEATS, 2 * HD), BF16),
            pltpu.VMEM((n, FEATS, HD), BF16),
            pltpu.VMEM((n, FEATS, HD), BF16),
            pltpu.VMEM((n, FEATS, 4 * HD), BF16),
            pltpu.SemaphoreType.DMA((n, 4)),
        ],
    )(at, *weights, *far, *grads)


def swapped(x, axis):
    return lax.ppermute(x, axis, [(0, 1), (1, 0)])


def chip_pairs(d):
    return [(i, i + 2 * d) for i in range(lax.axis_size(AA) - 2 * d) if d < HALF or i % 2]


def chips_on(x, d):
    return lax.ppermute(x, AA, chip_pairs(d))


def chips_back(x, d):
    return lax.ppermute(x, AA, [(j, i) for i, j in chip_pairs(d)])


def round_z(x, step):
    return lax.ppermute(x, "z", [(i, (i + step) % RING) for i in range(RING)])


def local(query, keys, values, grad_out, segment_ids, w_query, w_key, w_value, w_out):
    core = lax.axis_index("core")
    z = lax.axis_index("z")
    xh = lax.axis_index("xh")
    own = lax.axis_index(AA)[None]
    at = jnp.stack((z, xh, core))
    ids = jnp.pad(
        segment_ids.astype(BF16).reshape(ROWS // HD, HD),
        ((0, SEG_ROWS - ROWS // HD), (0, HD)),
    )
    block = jnp.concatenate((jnp.concatenate((keys, values), axis=1), ids), axis=0)
    twins = [block] + [chips_on(block, d) for d in range(1, HALF + 1)]
    others = [
        swapped(jnp.where(core == 1, twins[d + 1], twins[d]), "core") for d in range(HALF)
    ]
    window = [None] * BLOCKS
    for d in range(HALF):
        window[BLOCKS - 1 - 2 * d] = twins[d]
        window[BLOCKS - 2 - 2 * d] = others[d]
    shard = grad_out.T
    shards = {0: shard}
    for k in range(1, RING // 2 + 1):
        shards[-k] = round_z(shards[1 - k], 1)
        if k < RING // 2:
            shards[k] = round_z(shards[k - 1], -1)
    own_w, send_w = split_w_out(at, w_out)
    out_mine = swapped(send_w, "xh")
    far_w = (out_mine, swapped(out_mine, "core"))
    wanted = [
        lax.dynamic_index_in_dim(w.reshape(2, RING // 2, 2, FEATS, -1), core, 0, keepdims=False)
        for w in (w_query, w_key, w_value)
    ]
    wanted = [lax.dynamic_index_in_dim(w, 1 - xh, 1, keepdims=False) for w in wanted]
    far_mine = swapped(jnp.concatenate(wanted, axis=2), "xh")
    far_other = swapped(far_mine, "core")

    qseg = segment_ids[None, :]
    state = attention_stats(own, qseg, query, window, NEAR, BLOCKS)
    stats = attention_stats(own, qseg, query, window, 0, NEAR, state)
    early = (0, -1, 1, -2, 2)
    late = (-3, 3, -4)
    part = dout_part(early, at, own_w, far_w, [shards[d] for d in early])
    near, send = dout_part(late, at, own_w, far_w, [shards[d] for d in late], part)
    gqt, mine, theirs = attention_grads(own, stats, query, near, swapped(send, "xh"), window)
    gqt_far = swapped(gqt, "xh")
    own_total, sends = join_partials(core[None], mine, swapped(theirs, "core"))
    parts = [chips_back(sends[d - 1], d) for d in range(HALF, 0, -1)]
    gkvt = total_partials(own_total, parts)
    gkvt_far = swapped(gkvt, "xh")

    weights = (w_query, w_key, w_value)
    far = (far_mine, far_other)
    grads = (gqt, gkvt, gqt_far, gkvt_far)
    ahead, behind = project((4, -3), at, weights, far, grads, BF16)
    rest = project((3, -2, 2, -1, 1, 0), at, weights, far, grads, F32)
    ahead = round_z(ahead, 1)
    behind = round_z(behind, -1)
    for add_ahead, add_behind in ((rest[0], rest[1]), (rest[2], rest[3])):
        ahead = round_z((ahead.astype(F32) + add_ahead).astype(BF16), 1)
        behind = round_z((behind.astype(F32) + add_behind).astype(BF16), -1)
    ahead = round_z((ahead.astype(F32) + rest[4]).astype(BF16), 1)
    result = (ahead.astype(F32) + behind.astype(F32) + rest[5]).astype(BF16)
    return result.T


def solution(mesh):
    finer = Mesh(mesh.devices.reshape(2, 4, 2, RING, 2), AA + BA)
    return jax.shard_map(
        local,
        mesh=finer,
        in_specs=(
            P(AA, BA),
            P(AA, BA),
            P(AA, BA),
            P(AA, BA),
            P(AA),
            P(None, BA),
            P(None, BA),
            P(None, BA),
            P(BA, None),
        ),
        out_specs=P(AA, BA),
        check_vma=False,
    )
```

```python
import math

import jax
import jax.numpy as jnp
from jax import lax
from jax.experimental import pallas as pl
from jax.experimental.pallas import tpu as pltpu
from jax.sharding import Mesh
from jax.sharding import PartitionSpec as P


D = 5376
HQ = 32
HD = 128
DOCS = 6
ROWS = 384
HALF = 5
BLOCKS = 2 * HALF
SEG_ROWS = 16
PACKED = ROWS + SEG_ROWS
FEATS = 336
CHUNK = 384
WINDOW = 512
NEAR = 6
RING = 8
AA = ("xl", "y", "core")
BA = ("z", "xh")
NEG_FILL = -1e30
SCALE = (D / HQ) ** (-0.5)
SCALE2 = SCALE * math.log2(math.e)
F32 = jnp.float32
BF16 = jnp.bfloat16
VMEM = pl.BlockSpec(memory_space=pltpu.VMEM)
SMEM = pl.BlockSpec(memory_space=pltpu.SMEM)
ANY = pl.BlockSpec(memory_space=pl.ANY)


def dot(a, b):
    return lax.dot_general(a, b, (((1,), (0,)), ((), ())), preferred_element_type=F32)


def sources(low, high):
    odd = [d for d in range(HALF) if low <= BLOCKS - 1 - 2 * d < high]
    even = [k for k in range(HALF) if low <= BLOCKS - 2 - 2 * k < high]
    return odd, even, sorted({k for e in even for k in (e, e + 1)})


def load_window(low, high, core, kv_refs, buf, sem):
    odd, even, extra = sources(low, high)
    twin = dict(zip(odd, kv_refs))
    other = dict(zip(extra, kv_refs[len(odd) :]))
    copies = []
    for d in odd:
        at = BLOCKS - 1 - 2 * d - low
        copies.append(pltpu.make_async_copy(twin[d], buf.at[at], sem.at[at]))
        copies[-1].start()
    for k in even:
        at = BLOCKS - 2 - 2 * k - low
        from_low = pltpu.make_async_copy(other[k], buf.at[at], sem.at[at])
        from_high = pltpu.make_async_copy(other[k + 1], buf.at[at], sem.at[at])

        @pl.when(core == 1)
        def _(copy=from_low):
            copy.start()

        @pl.when(core == 0)
        def _(copy=from_high):
            copy.start()

        copies.append(from_low)
    return copies


def window_refs(low, high, twins, others):
    odd, _, extra = sources(low, high)
    return [twins[d] for d in odd] + [others[k] for k in extra]


def stats_kernel(low, high, own_ref, qseg_ref, q_ref, *refs):
    near = high == BLOCKS
    odd, _, extra = sources(low, high)
    count = len(odd) + len(extra)
    if near:
        kv_refs = refs[:count]
        m_ref, l_ref, out_ref, start_ref, buf, qt_ref, sem = refs[count:]
    else:
        m_in, l_in, out_in, start_in = refs[:4]
        kv_refs = refs[4 : 4 + count]
        lse_ref, out_ref, start_ref, low_ref, buf, qt_ref, m_ref, l_ref, sem = refs[4 + count :]
    own = own_ref[0]
    copies = load_window(low, high, lax.rem(own, 2), kv_refs, buf, sem)
    qt_ref[...] = q_ref[...].T
    if near:
        m_ref[...] = jnp.full(m_ref.shape, NEG_FILL, F32)
        l_ref[...] = jnp.zeros(l_ref.shape, F32)
        out_ref[...] = jnp.zeros(out_ref.shape, F32)
    else:
        m_ref[...] = m_in[...]
        l_ref[...] = l_in[...]
        out_ref[...] = out_in[...]
    seg = qseg_ref[...]
    seg0 = jnp.min(seg, axis=1, keepdims=True)
    for c in copies:
        c.wait()
    before = jnp.zeros((SEG_ROWS, HD), jnp.int32)
    line = lax.broadcasted_iota(jnp.int32, (SEG_ROWS, HD), 0)
    for b in range(low, min(high, BLOCKS - 1)):
        ids = buf[b - low, ROWS:, :HD].astype(F32).astype(jnp.int32)
        hit = (line < ROWS // HD) & (ids < seg0) & (own + b >= BLOCKS - 1)
        before = before + hit.astype(jnp.int32)
    start0 = jnp.sum(before) + jnp.maximum(own + low - (BLOCKS - 1), 0) * ROWS
    first_next = (own + high - (BLOCKS - 1)) * ROWS
    start = jnp.zeros((1, ROWS), jnp.int32) + start0
    if near:
        for s in range(1, DOCS):
            here = own * ROWS + jnp.sum((seg < s).astype(jnp.int32), axis=1, keepdims=True)
            start = jnp.where((seg == s) & (seg > seg0), here, start)
        start_ref[...] = start
    else:
        start = jnp.where((seg == seg0) & (start0 < first_next), start, start_in[...])
        start_ref[...] = start
        start0 = jnp.min(start)
    lowest = lax.div(start0, ROWS) - own + (BLOCKS - 1)
    pos = own * ROWS + lax.broadcasted_iota(jnp.int32, (1, ROWS), 1)
    key_at = lax.broadcasted_iota(jnp.int32, (ROWS, ROWS), 0)

    def one_block(back_to, carry):
        b = high - 1 - back_to
        first = (own + b - (BLOCKS - 1)) * ROWS
        allowed = (key_at >= start - first) & (key_at <= pos - first)
        kb = buf[b - low, :ROWS, :HD]
        vt = buf[b - low, :ROWS, HD:].T
        for h in range(2):
            part = slice(h * HD, (h + 1) * HD)
            s = jnp.where(allowed, dot(kb, qt_ref[part, :]) * SCALE2, NEG_FILL)
            m_old = m_ref[h : h + 1, :]
            m_new = jnp.maximum(m_old, jnp.max(s, axis=0, keepdims=True))
            p = jnp.exp2(s - m_new)
            back = jnp.exp2(m_old - m_new)
            l_ref[h : h + 1, :] = l_ref[h : h + 1, :] * back + jnp.sum(p, axis=0, keepdims=True)
            m_ref[h : h + 1, :] = m_new
            out_ref[part, :] = out_ref[part, :] * back + dot(vt, p.astype(BF16))
        return carry

    lax.fori_loop(0, high - jnp.clip(lowest, low, high), one_block, 0)
    if not near:
        low_ref[0] = lowest
        lse_ref[...] = m_ref[...] + jnp.log2(l_ref[...])
        for h in range(2):
            part = slice(h * HD, (h + 1) * HD)
            out_ref[part, :] = out_ref[part, :] / l_ref[h : h + 1, :]


def grads_kernel(own_ref, low_ref, start_ref, q_ref, near_ref, far_ref, lse_ref, out_ref, *refs):
    kv_refs, refs = refs[: BLOCKS + 1], refs[BLOCKS + 1 :]
    gqt_ref, mine_ref, theirs_ref = refs[:3]
    buf, qt_ref, dout_ref, doutt_ref, delta_ref, acc_ref, sem = refs[3:]
    own = own_ref[0]
    copies = load_window(0, BLOCKS, lax.rem(own, 2), kv_refs, buf, sem)
    lowest = low_ref[0]
    qt_ref[...] = q_ref[...].T
    doutt_ref[...] = (near_ref[...] + far_ref[...].astype(F32)).astype(BF16)
    dout_ref[...] = doutt_ref[...].T
    for h in range(2):
        part = slice(h * HD, (h + 1) * HD)
        delta_ref[h : h + 1, :] = jnp.sum(
            doutt_ref[part, :].astype(F32) * out_ref[part, :], axis=0, keepdims=True
        )
    acc_ref[...] = jnp.zeros(acc_ref.shape, F32)
    start = start_ref[...]
    pos = own * ROWS + lax.broadcasted_iota(jnp.int32, (1, ROWS), 1)
    key_at = lax.broadcasted_iota(jnp.int32, (ROWS, ROWS), 0)
    for c in copies:
        c.wait()

    def one_block(b, target, d):
        @pl.when(b >= lowest)
        def _():
            first = (own + b - (BLOCKS - 1)) * ROWS
            allowed = (key_at >= start - first) & (key_at <= pos - first)
            kb = buf[b, :ROWS, :HD]
            vb = buf[b, :ROWS, HD:]
            kt = kb.T
            gk = gv = None
            for h in range(2):
                part = slice(h * HD, (h + 1) * HD)
                s = dot(kb, qt_ref[part, :]) * SCALE2
                dp = dot(vb, doutt_ref[part, :])
                p = jnp.where(allowed, jnp.exp2(s - lse_ref[h : h + 1, :]), 0.0)
                ds = (p * (dp - delta_ref[h : h + 1, :])).astype(BF16)
                add_v = dot(p.astype(BF16), dout_ref[:, part])
                add_k = dot(ds, q_ref[:, part])
                gv = add_v if h == 0 else gv + add_v
                gk = add_k if h == 0 else gk + add_k
                acc_ref[part, :] += dot(kt, ds)
            target[d, :, :HD] = (gk * SCALE).astype(BF16)
            target[d, :, HD:] = gv.astype(BF16)

        @pl.when(b < lowest)
        def _():
            target[d] = jnp.zeros((ROWS, 2 * HD), BF16)

    def two_blocks(d, carry):
        one_block(BLOCKS - 1 - 2 * d, mine_ref, d)
        one_block(BLOCKS - 2 - 2 * d, theirs_ref, d)
        return carry

    lax.fori_loop(0, HALF, two_blocks, 0)
    gqt_ref[...] = (acc_ref[...] * SCALE).astype(BF16)


def attention_stats(own, qseg, query, twins, others, low, high, state=()):
    count = high - low
    window = window_refs(low, high, twins, others)
    row = jax.ShapeDtypeStruct((2, ROWS), F32)
    wide = jax.ShapeDtypeStruct((2 * HD, ROWS), F32)
    start = jax.ShapeDtypeStruct((1, ROWS), jnp.int32)
    lowest = jax.ShapeDtypeStruct((1,), jnp.int32)
    scratch = [
        pltpu.VMEM((count, PACKED, 2 * HD), BF16),
        pltpu.VMEM((2 * HD, ROWS), BF16),
    ]
    if state:
        scratch += [pltpu.VMEM((2, ROWS), F32), pltpu.VMEM((2, ROWS), F32)]
    return pl.pallas_call(
        lambda *refs: stats_kernel(low, high, *refs),
        name="stats_far" if state else "stats_near",
        out_shape=(row, wide, start, lowest) if state else (row, row, wide, start),
        in_specs=[SMEM, VMEM, VMEM] + [VMEM] * len(state) + [ANY] * len(window),
        out_specs=(VMEM, VMEM, VMEM, SMEM if state else VMEM),
        scratch_shapes=scratch + [pltpu.SemaphoreType.DMA((count,))],
    )(own, qseg, query, *state, *window)


def attention_grads(own, stats, query, near, far, twins, others):
    lse, out, start, lowest = stats
    window = window_refs(0, BLOCKS, twins, others)
    return pl.pallas_call(
        grads_kernel,
        name="attention_grads",
        out_shape=(
            jax.ShapeDtypeStruct((2 * HD, ROWS), BF16),
            jax.ShapeDtypeStruct((HALF, ROWS, 2 * HD), BF16),
            jax.ShapeDtypeStruct((HALF, ROWS, 2 * HD), BF16),
        ),
        in_specs=[SMEM, SMEM] + [VMEM] * 6 + [ANY] * len(window),
        out_specs=(VMEM, VMEM, VMEM),
        scratch_shapes=[
            pltpu.VMEM((BLOCKS, PACKED, 2 * HD), BF16),
            pltpu.VMEM((2 * HD, ROWS), BF16),
            pltpu.VMEM((ROWS, 2 * HD), BF16),
            pltpu.VMEM((2 * HD, ROWS), BF16),
            pltpu.VMEM((2, ROWS), F32),
            pltpu.VMEM((2 * HD, ROWS), F32),
            pltpu.SemaphoreType.DMA((BLOCKS,)),
        ],
    )(own, lowest, start, query, near, far, lse, out, *window)


def column_window(chunk):
    base = jnp.minimum(lax.div(chunk * FEATS, HD) * HD, D - WINDOW)
    return pl.ds(pl.multiple_of(base, HD), WINDOW), chunk * FEATS - base


def split_kernel(at_ref, w_ref, send_ref, buf, sem):
    first = at_ref[2] * (RING // 2)
    other = 1 - at_ref[1]
    copies = []
    for i in range(RING // 2):
        lanes, skip = column_window(2 * (first + i) + other)
        copy = pltpu.make_async_copy(w_ref.at[:, lanes], buf.at[i], sem.at[i])
        copy.start()
        copies.append((copy, skip))
    lane = lax.broadcasted_iota(jnp.int32, (2 * HD, CHUNK), 1)
    for i, (copy, skip) in enumerate(copies):
        copy.wait()
        moved = pltpu.roll(buf[i].astype(F32), lax.rem(WINDOW - skip, WINDOW), 1)[:, :CHUNK]
        send_ref[i] = jnp.where(lane < FEATS, moved, 0.0).astype(BF16)


def split_w_out(at, w_out):
    n = RING // 2
    return pl.pallas_call(
        split_kernel,
        name="split_w_out",
        out_shape=jax.ShapeDtypeStruct((n, 2 * HD, CHUNK), BF16),
        in_specs=[SMEM, ANY],
        out_specs=VMEM,
        scratch_shapes=[
            pltpu.VMEM((n, 2 * HD, WINDOW), BF16),
            pltpu.SemaphoreType.DMA((n,)),
        ],
    )(at, w_out)


def dout_kernel(deltas, at_ref, w_ref, pa, pb, *refs):
    shards = refs[:RING]
    near_ref, send_ref, wbuf, fbuf, gbuf, hbuf, sem = refs[RING:]
    z, xh, core = at_ref[0], at_ref[1], at_ref[2]
    copies = []
    for i in range(RING):
        chunk = lax.rem(z + deltas[i] + RING, RING)
        half = lax.div(chunk, RING // 2)
        inner = lax.rem(chunk, RING // 2)
        lanes, skip = column_window(2 * chunk + xh)
        place = pl.ds(pl.multiple_of(skip, 16), FEATS)
        far = pltpu.make_async_copy(pa.at[inner], fbuf.at[i], sem.at[i, 1])
        far_too = pltpu.make_async_copy(pb.at[inner], fbuf.at[i], sem.at[i, 1])
        pltpu.make_async_copy(w_ref.at[:, lanes], wbuf.at[i], sem.at[i, 0]).start()

        @pl.when(half == core)
        def _(copy=far):
            copy.start()

        @pl.when(half != core)
        def _(copy=far_too):
            copy.start()

        gbuf[i] = jnp.zeros((WINDOW, ROWS), BF16)
        hbuf[i, FEATS:] = jnp.zeros((CHUNK - FEATS, ROWS), BF16)
        to_far = pltpu.make_async_copy(shards[i], hbuf.at[i, :FEATS], sem.at[i, 2])
        to_far.start()
        to_own = pltpu.make_async_copy(shards[i], gbuf.at[i, place], sem.at[i, 3])
        to_own.start()
        copies.append(
            (pltpu.make_async_copy(w_ref.at[:, lanes], wbuf.at[i], sem.at[i, 0]), far, to_far, to_own)
        )
    near = far = None
    for i in range(RING):
        for c in copies[i]:
            c.wait()
        add_far = dot(fbuf[i], hbuf[i])
        add_near = dot(wbuf[i], gbuf[i])
        far = add_far if i == 0 else far + add_far
        near = add_near if i == 0 else near + add_near
    near_ref[...] = near
    send_ref[...] = far.astype(BF16)


def dout_parts(at, w_out, far_w, shards):
    deltas = tuple(shards)
    half = (2 * HD, ROWS)
    return pl.pallas_call(
        lambda *refs: dout_kernel(deltas, *refs),
        name="dout_parts",
        out_shape=(jax.ShapeDtypeStruct(half, F32), jax.ShapeDtypeStruct(half, BF16)),
        in_specs=[SMEM] + [ANY] * (3 + RING),
        out_specs=(VMEM, VMEM),
        scratch_shapes=[
            pltpu.VMEM((RING, 2 * HD, WINDOW), BF16),
            pltpu.VMEM((RING, 2 * HD, CHUNK), BF16),
            pltpu.VMEM((RING, WINDOW, ROWS), BF16),
            pltpu.VMEM((RING, CHUNK, ROWS), BF16),
            pltpu.SemaphoreType.DMA((RING, 4)),
        ],
    )(at, w_out, *far_w, *shards.values())


def join_kernel(core_ref, mine_ref, got_ref, own_ref, *send_refs):
    core = core_ref[0]
    for d in range(HALF + 1):
        at = d - core
        inside = (at >= 0) & (at < HALF)
        other = got_ref[jnp.clip(at, 0, HALF - 1)].astype(F32)
        total = jnp.where(inside, other, 0.0)
        if d < HALF:
            total = total + mine_ref[d].astype(F32)
        if d == 0:
            own_ref[...] = total
        else:
            send_refs[d - 1][...] = total.astype(BF16)


def join_partials(core, mine, got):
    shape = (ROWS, 2 * HD)
    result = pl.pallas_call(
        join_kernel,
        name="join_partials",
        out_shape=(jax.ShapeDtypeStruct(shape, F32),) + (jax.ShapeDtypeStruct(shape, BF16),) * HALF,
        in_specs=[SMEM, VMEM, VMEM],
        out_specs=(VMEM,) * (HALF + 1),
    )(core, mine, got)
    return result[0], result[1:]


def total_kernel(own_ref, *refs):
    total = own_ref[...]
    for ref in refs[:HALF]:
        total = total + ref[...].astype(F32)
    refs[HALF][...] = total.astype(BF16).T


def total_partials(own, parts):
    return pl.pallas_call(
        total_kernel,
        name="total_partials",
        out_shape=jax.ShapeDtypeStruct((2 * HD, ROWS), BF16),
        in_specs=[VMEM] * (HALF + 1),
        out_specs=VMEM,
    )(own, *parts)


def project_kernel(deltas, at_ref, *refs):
    wq, wk, wv, pa, pb, gq, gkv, gq2, gkv2 = refs[:9]
    outs = refs[9 : 9 + len(deltas)]
    bq, bk, bv, bp, sem = refs[9 + len(deltas) :]
    z, xh, core = at_ref[0], at_ref[1], at_ref[2]
    copies = []
    for n, delta in enumerate(deltas):
        chunk = lax.rem(z + delta + RING, RING)
        rows = pl.ds(pl.multiple_of((2 * chunk + xh) * FEATS, 16), FEATS)
        mine = [
            pltpu.make_async_copy(w.at[rows, :], b.at[n], sem.at[n, i])
            for i, (w, b) in enumerate(((wq, bq), (wk, bk), (wv, bv)))
        ]
        for c in mine:
            c.start()
        half = lax.div(chunk, RING // 2)
        inner = lax.rem(chunk, RING // 2)

        @pl.when(half == core)
        def _(n=n, inner=inner):
            pltpu.make_async_copy(pa.at[inner], bp.at[n], sem.at[n, 3]).start()

        @pl.when(half != core)
        def _(n=n, inner=inner):
            pltpu.make_async_copy(pb.at[inner], bp.at[n], sem.at[n, 3]).start()

        copies.append(mine + [pltpu.make_async_copy(pa.at[0], bp.at[n], sem.at[n, 3])])
    for n in range(len(deltas)):
        for c in copies[n]:
            c.wait()
        total = dot(bq[n], gq[...]) + dot(bk[n], gkv[:HD, :]) + dot(bv[n], gkv[HD:, :])
        total = total + dot(bp[n, :, : 2 * HD], gq2[...]) + dot(bp[n, :, 2 * HD :], gkv2[...])
        outs[n][...] = total.astype(outs[n].dtype)


def project(deltas, at, weights, far, grads, kind):
    n = len(deltas)
    return pl.pallas_call(
        lambda *refs: project_kernel(deltas, *refs),
        name="project",
        out_shape=(jax.ShapeDtypeStruct((FEATS, ROWS), kind),) * n,
        in_specs=[SMEM] + [ANY] * 5 + [VMEM] * 4,
        out_specs=(VMEM,) * n,
        scratch_shapes=[
            pltpu.VMEM((n, FEATS, 2 * HD), BF16),
            pltpu.VMEM((n, FEATS, HD), BF16),
            pltpu.VMEM((n, FEATS, HD), BF16),
            pltpu.VMEM((n, FEATS, 4 * HD), BF16),
            pltpu.SemaphoreType.DMA((n, 4)),
        ],
    )(at, *weights, *far, *grads)


def swapped(x, axis):
    return lax.ppermute(x, axis, [(0, 1), (1, 0)])


def chip_pairs(d):
    return [(i, i + 2 * d) for i in range(lax.axis_size(AA) - 2 * d) if d < HALF or i % 2]


def chips_on(x, d):
    return lax.ppermute(x, AA, chip_pairs(d))


def chips_back(x, d):
    return lax.ppermute(x, AA, [(j, i) for i, j in chip_pairs(d)])


def round_z(x, step):
    return lax.ppermute(x, "z", [(i, (i + step) % RING) for i in range(RING)])


def body(query, keys, values, grad_out, segment_ids, w_query, w_key, w_value, w_out):
    core = lax.axis_index("core")
    z = lax.axis_index("z")
    xh = lax.axis_index("xh")
    own = lax.axis_index(AA)[None]
    at = jnp.stack((z, xh, core))
    shards = {0: grad_out.T}
    for k in range(1, RING // 2 + 1):
        shards[-k] = round_z(shards[1 - k], 1)
        if k < RING // 2:
            shards[k] = round_z(shards[k - 1], -1)
    send_w = split_w_out(at, w_out)
    far_w = swapped(send_w, "xh")
    far_w = (far_w, swapped(far_w, "core"))
    ids = jnp.pad(
        segment_ids.astype(BF16).reshape(ROWS // HD, HD),
        ((0, SEG_ROWS - ROWS // HD), (0, HD)),
    )
    block = jnp.concatenate((jnp.concatenate((keys, values), axis=1), ids), axis=0)
    twins = [block] + [chips_on(block, d) for d in range(1, HALF + 1)]
    others = [swapped(twins[d], "core") for d in range(HALF + 1)]
    wanted = [
        lax.dynamic_index_in_dim(w.reshape(2, RING // 2, 2, FEATS, -1), core, 0, keepdims=False)
        for w in (w_query, w_key, w_value)
    ]
    wanted = [lax.dynamic_index_in_dim(w, 1 - xh, 1, keepdims=False) for w in wanted]
    far_mine = swapped(jnp.concatenate(wanted, axis=2), "xh")
    far_other = swapped(far_mine, "core")

    qseg = segment_ids[None, :]
    state = attention_stats(own, qseg, query, twins, others, NEAR, BLOCKS)
    near, send = dout_parts(at, w_out, far_w, shards)
    far = swapped(send, "xh")
    stats = attention_stats(own, qseg, query, twins, others, 0, NEAR, state)
    gqt, mine, theirs = attention_grads(own, stats, query, near, far, twins, others)
    got = swapped(theirs, "core")
    gqt_far = swapped(gqt, "xh")
    own_total, sends = join_partials(core[None], mine, got)
    parts = [chips_back(sends[d - 1], d) for d in range(HALF, 0, -1)]
    gkvt = total_partials(own_total, parts)
    gkvt_far = swapped(gkvt, "xh")

    weights = (w_query, w_key, w_value)
    far_rows = (far_mine, far_other)
    grads = (gqt, gkvt, gqt_far, gkvt_far)
    ahead, behind = project((4, -3), at, weights, far_rows, grads, BF16)
    rest = project((3, -2, 2, -1, 1, 0), at, weights, far_rows, grads, F32)
    ahead = round_z(ahead, 1)
    behind = round_z(behind, -1)
    for k in (2, 3):
        add_ahead, add_behind = rest[2 * k - 4], rest[2 * k - 3]
        ahead = round_z((ahead.astype(F32) + add_ahead).astype(BF16), 1)
        behind = round_z((behind.astype(F32) + add_behind).astype(BF16), -1)
    ahead = round_z((ahead.astype(F32) + rest[4]).astype(BF16), 1)
    result = (ahead.astype(F32) + behind.astype(F32) + rest[5]).astype(BF16)
    return result.T


def solution(mesh):
    finer = Mesh(mesh.devices.reshape(2, 4, 2, RING, 2), AA + BA)
    return jax.shard_map(
        body,
        mesh=finer,
        in_specs=(
            P(AA, BA),
            P(AA, BA),
            P(AA, BA),
            P(AA, BA),
            P(AA),
            P(None, BA),
            P(None, BA),
            P(None, BA),
            P(BA, None),
        ),
        out_specs=P(AA, BA),
        check_vma=False,
    )
```

```python
import math

import jax
import jax.numpy as jnp
from jax import lax
from jax.experimental import pallas as pl
from jax.experimental.pallas import tpu as pltpu
from jax.sharding import Mesh
from jax.sharding import PartitionSpec as P


D = 5376
HQ = 32
HD = 128
DOCS = 6
ROWS = 384
HALF = 5
BLOCKS = 2 * HALF
SEG_ROWS = 16
PACKED = ROWS + SEG_ROWS
FEATS = 336
CHUNK = 384
WINDOW = 512
BOTH = 2 * ROWS
TILE = 256
STATS_TILE = 128
NEAR = 6
RING = 8
AA = ("xl", "y", "core")
BA = ("z", "xh")
NEG_FILL = -1e30
SCALE = (D / HQ) ** (-0.5)
SCALE2 = SCALE * math.log2(math.e)
F32 = jnp.float32
BF16 = jnp.bfloat16
VMEM = pl.BlockSpec(memory_space=pltpu.VMEM)
SMEM = pl.BlockSpec(memory_space=pltpu.SMEM)
ANY = pl.BlockSpec(memory_space=pl.ANY)


def dot(a, b):
    return lax.dot_general(a, b, (((1,), (0,)), ((), ())), preferred_element_type=F32)


def sources(low, high):
    odd = [d for d in range(HALF) if low <= BLOCKS - 1 - 2 * d < high]
    even = [k for k in range(HALF) if low <= BLOCKS - 2 - 2 * k < high]
    return odd, even, sorted({k for e in even for k in (e, e + 1)})


def load_window(low, high, core, kv_refs, buf, sem):
    odd, even, extra = sources(low, high)
    twin = dict(zip(odd, kv_refs))
    other = dict(zip(extra, kv_refs[len(odd) :]))
    copies = []
    for d in odd:
        at = BLOCKS - 1 - 2 * d - low
        copies.append(pltpu.make_async_copy(twin[d], buf.at[at], sem.at[at]))
        copies[-1].start()
    for k in even:
        at = BLOCKS - 2 - 2 * k - low
        from_low = pltpu.make_async_copy(other[k], buf.at[at], sem.at[at])
        from_high = pltpu.make_async_copy(other[k + 1], buf.at[at], sem.at[at])

        @pl.when(core == 1)
        def _(copy=from_low):
            copy.start()

        @pl.when(core == 0)
        def _(copy=from_high):
            copy.start()

        copies.append(from_low)
    return copies


def window_refs(low, high, twins, others):
    odd, _, extra = sources(low, high)
    return [twins[d] for d in odd] + [others[k] for k in extra]


def side_by_side(x):
    return jnp.concatenate((x[:HD, :], x[HD:, :]), axis=1)


def one_above_other(x):
    return jnp.concatenate((x[:, :HD], x[:, HD:]), axis=0)


def tiles(width):
    return [slice(t, t + width) for t in range(0, BOTH, width)]


def stats_kernel(low, high, own_ref, qseg_ref, q_ref, *refs):
    near = high == BLOCKS
    odd, _, extra = sources(low, high)
    count = len(odd) + len(extra)
    if near:
        kv_refs = refs[:count]
        m_ref, l_ref, out_ref, start_ref, buf, qt_ref, sem = refs[count:]
    else:
        m_in, l_in, out_in, start_in = refs[:4]
        kv_refs = refs[4 : 4 + count]
        lse_ref, out_ref, start_ref, low_ref, buf, qt_ref, m_ref, l_ref, sem = refs[4 + count :]
    own = own_ref[0]
    copies = load_window(low, high, lax.rem(own, 2), kv_refs, buf, sem)
    qt_ref[...] = one_above_other(q_ref[...]).T
    if near:
        m_ref[...] = jnp.full(m_ref.shape, NEG_FILL, F32)
        l_ref[...] = jnp.zeros(l_ref.shape, F32)
        out_ref[...] = jnp.zeros(out_ref.shape, F32)
    else:
        m_ref[...] = m_in[...]
        l_ref[...] = l_in[...]
        out_ref[...] = out_in[...]
    seg = qseg_ref[...]
    seg0 = jnp.min(seg, axis=1, keepdims=True)
    for c in copies:
        c.wait()
    before = jnp.zeros((SEG_ROWS, HD), jnp.int32)
    line = lax.broadcasted_iota(jnp.int32, (SEG_ROWS, HD), 0)
    for b in range(low, min(high, BLOCKS - 1)):
        ids = buf[b - low, ROWS:, :HD].astype(F32).astype(jnp.int32)
        hit = (line < ROWS // HD) & (ids < seg0) & (own + b >= BLOCKS - 1)
        before = before + hit.astype(jnp.int32)
    start0 = jnp.sum(before) + jnp.maximum(own + low - (BLOCKS - 1), 0) * ROWS
    first_next = (own + high - (BLOCKS - 1)) * ROWS
    start = jnp.zeros((1, ROWS), jnp.int32) + start0
    if near:
        for s in range(1, DOCS):
            here = own * ROWS + jnp.sum((seg < s).astype(jnp.int32), axis=1, keepdims=True)
            start = jnp.where((seg == s) & (seg > seg0), here, start)
        start_ref[...] = start
    else:
        start = jnp.where((seg == seg0) & (start0 < first_next), start, start_in[...])
        start_ref[...] = start
        start0 = jnp.min(start)
    lowest = lax.div(start0, ROWS) - own + (BLOCKS - 1)
    latest = jnp.max(start)
    pos = own * ROWS + lax.broadcasted_iota(jnp.int32, (1, ROWS), 1)
    start = jnp.concatenate((start, start), axis=1)
    pos = jnp.concatenate((pos, pos), axis=1)
    key_at = lax.broadcasted_iota(jnp.int32, (ROWS, STATS_TILE), 0)

    def add_block(b, first, whole):
        kb = buf[b - low, :ROWS, :HD]
        vt = buf[b - low, :ROWS, HD:].T
        for t in tiles(STATS_TILE):
            s = dot(kb, qt_ref[:, t]) * SCALE2
            if not whole:
                allowed = (key_at >= start[:, t] - first) & (key_at <= pos[:, t] - first)
                s = jnp.where(allowed, s, NEG_FILL)
            m_old = m_ref[:, t]
            m_new = jnp.maximum(m_old, jnp.max(s, axis=0, keepdims=True))
            p = jnp.exp2(s - m_new)
            back = jnp.exp2(m_old - m_new)
            l_ref[:, t] = l_ref[:, t] * back + jnp.sum(p, axis=0, keepdims=True)
            m_ref[:, t] = m_new
            out_ref[:, t] = out_ref[:, t] * back + dot(vt, p.astype(BF16))

    def one_block(back_to, carry):
        b = high - 1 - back_to
        first = (own + b - (BLOCKS - 1)) * ROWS
        whole = (first >= latest) & (b < BLOCKS - 1)

        @pl.when(whole)
        def _():
            add_block(b, first, True)

        @pl.when(jnp.logical_not(whole))
        def _():
            add_block(b, first, False)

        return carry

    lax.fori_loop(0, high - jnp.clip(lowest, low, high), one_block, 0)
    if not near:
        low_ref[0] = lowest
        lse_ref[...] = m_ref[...] + jnp.log2(l_ref[...])
        out_ref[...] = out_ref[...] / l_ref[...]


def grads_kernel(own_ref, low_ref, *refs):
    given, refs = refs[:6], refs[6:]
    kv_refs, refs = refs[: BLOCKS + 1], refs[BLOCKS + 1 :]
    gqt_ref, mine_ref, theirs_ref = refs[:3]
    start_ref, q_ref, near_ref, far_ref, lse_ref, out_ref = held = refs[3:9]
    buf, qt_ref, qn_ref, dout_ref, doutt_ref, delta_ref, acc_ref, made, sem, in_sem, out_sem = refs[9:]
    own = own_ref[0]
    arrivals = [pltpu.make_async_copy(x, y, in_sem.at[i]) for i, (x, y) in enumerate(zip(given, held))]
    for c in arrivals:
        c.start()
    load_window(0, BLOCKS, lax.rem(own, 2), kv_refs, buf, sem)
    lowest = low_ref[0]
    acc_ref[...] = jnp.zeros(acc_ref.shape, F32)
    key_at = lax.broadcasted_iota(jnp.int32, (ROWS, TILE), 0)
    for c in arrivals:
        c.wait()
    qn_ref[...] = one_above_other(q_ref[...])
    qt_ref[...] = qn_ref[...].T
    doutt_ref[...] = side_by_side((near_ref[...] + far_ref[...].astype(F32)).astype(BF16))
    dout_ref[...] = doutt_ref[...].T
    delta_ref[...] = jnp.sum(doutt_ref[...].astype(F32) * out_ref[...], axis=0, keepdims=True)
    start = start_ref[...]
    latest = jnp.max(start)
    pos = own * ROWS + lax.broadcasted_iota(jnp.int32, (1, ROWS), 1)
    start = jnp.concatenate((start, start), axis=1)
    pos = jnp.concatenate((pos, pos), axis=1)

    def add_block(b, first, whole):
        kb = buf[b, :ROWS, :HD]
        vb = buf[b, :ROWS, HD:]
        kt = kb.T
        gk = gv = None
        for t in tiles(TILE):
            s = dot(kb, qt_ref[:, t]) * SCALE2
            dp = dot(vb, doutt_ref[:, t])
            p = jnp.exp2(s - lse_ref[:, t])
            if not whole:
                allowed = (key_at >= start[:, t] - first) & (key_at <= pos[:, t] - first)
                p = jnp.where(allowed, p, 0.0)
            ds = (p * (dp - delta_ref[:, t])).astype(BF16)
            add_v = dot(p.astype(BF16), dout_ref[t, :])
            add_k = dot(ds, qn_ref[t, :])
            gv = add_v if gv is None else gv + add_v
            gk = add_k if gk is None else gk + add_k
            acc_ref[:, t] += dot(kt, ds)
        made[b, :, :HD] = (gk * SCALE).astype(BF16)
        made[b, :, HD:] = gv.astype(BF16)

    def departure(b, target):
        d = (BLOCKS - 1 - b) // 2 if isinstance(b, int) else lax.div(BLOCKS - 1 - b, 2)
        return pltpu.make_async_copy(made.at[b], target.at[d], out_sem.at[b])

    def one_block(b, carry):
        pltpu.make_async_copy(kv_refs[0], buf.at[b], sem.at[b]).wait()
        first = (own + b - (BLOCKS - 1)) * ROWS
        whole = (first >= latest) & (b < BLOCKS - 1)

        @pl.when((b >= lowest) & whole)
        def _():
            add_block(b, first, True)

        @pl.when((b >= lowest) & jnp.logical_not(whole))
        def _():
            add_block(b, first, False)

        @pl.when(b < lowest)
        def _():
            made[b] = jnp.zeros((ROWS, 2 * HD), BF16)

        odd = lax.rem(b, 2) == 1

        @pl.when(odd)
        def _():
            departure(b, mine_ref).start()

        @pl.when(jnp.logical_not(odd))
        def _():
            departure(b, theirs_ref).start()

        return carry

    lax.fori_loop(0, BLOCKS, one_block, 0)
    gqt_ref[:HD, :] = (acc_ref[:, :ROWS] * SCALE).astype(BF16)
    gqt_ref[HD:, :] = (acc_ref[:, ROWS:] * SCALE).astype(BF16)
    for b in range(BLOCKS):
        departure(b, mine_ref if b % 2 else theirs_ref).wait()


def attention_stats(own, qseg, query, twins, others, low, high, state=()):
    count = high - low
    window = window_refs(low, high, twins, others)
    row = jax.ShapeDtypeStruct((1, BOTH), F32)
    wide = jax.ShapeDtypeStruct((HD, BOTH), F32)
    start = jax.ShapeDtypeStruct((1, ROWS), jnp.int32)
    lowest = jax.ShapeDtypeStruct((1,), jnp.int32)
    scratch = [
        pltpu.VMEM((count, PACKED, 2 * HD), BF16),
        pltpu.VMEM((HD, BOTH), BF16),
    ]
    if state:
        scratch += [pltpu.VMEM((1, BOTH), F32), pltpu.VMEM((1, BOTH), F32)]
    return pl.pallas_call(
        lambda *refs: stats_kernel(low, high, *refs),
        name="stats_far" if state else "stats_near",
        out_shape=(row, wide, start, lowest) if state else (row, row, wide, start),
        in_specs=[SMEM, VMEM, VMEM] + [VMEM] * len(state) + [ANY] * len(window),
        out_specs=(VMEM, VMEM, VMEM, SMEM if state else VMEM),
        scratch_shapes=scratch + [pltpu.SemaphoreType.DMA((count,))],
    )(own, qseg, query, *state, *window)


def attention_grads(own, stats, query, near, far, twins, others):
    lse, out, start, lowest = stats
    window = window_refs(0, BLOCKS, twins, others)
    given = (start, query, near, far, lse, out)
    return pl.pallas_call(
        grads_kernel,
        name="attention_grads",
        out_shape=(
            jax.ShapeDtypeStruct((2 * HD, ROWS), BF16),
            jax.ShapeDtypeStruct((HALF, ROWS, 2 * HD), BF16),
            jax.ShapeDtypeStruct((HALF, ROWS, 2 * HD), BF16),
        ),
        in_specs=[SMEM, SMEM] + [ANY] * (len(given) + len(window)),
        out_specs=(VMEM, ANY, ANY),
        scratch_shapes=[pltpu.VMEM(x.shape, x.dtype) for x in given]
        + [
            pltpu.VMEM((BLOCKS, PACKED, 2 * HD), BF16),
            pltpu.VMEM((HD, BOTH), BF16),
            pltpu.VMEM((BOTH, HD), BF16),
            pltpu.VMEM((BOTH, HD), BF16),
            pltpu.VMEM((HD, BOTH), BF16),
            pltpu.VMEM((1, BOTH), F32),
            pltpu.VMEM((HD, BOTH), F32),
            pltpu.VMEM((BLOCKS, ROWS, 2 * HD), BF16),
            pltpu.SemaphoreType.DMA((BLOCKS,)),
            pltpu.SemaphoreType.DMA((len(given),)),
            pltpu.SemaphoreType.DMA((BLOCKS,)),
        ],
    )(own, lowest, *given, *window)


def column_window(chunk):
    base = jnp.minimum(lax.div(chunk * FEATS, HD) * HD, D - WINDOW)
    return pl.ds(pl.multiple_of(base, HD), WINDOW), chunk * FEATS - base


def split_kernel(at_ref, w_ref, send_ref, buf, sem):
    first = at_ref[2] * (RING // 2)
    other = 1 - at_ref[1]
    copies = []
    for i in range(RING // 2):
        lanes, skip = column_window(2 * (first + i) + other)
        copy = pltpu.make_async_copy(w_ref.at[:, lanes], buf.at[i], sem.at[i])
        copy.start()
        copies.append((copy, skip))
    lane = lax.broadcasted_iota(jnp.int32, (2 * HD, CHUNK), 1)
    for i, (copy, skip) in enumerate(copies):
        copy.wait()
        moved = pltpu.roll(buf[i].astype(F32), lax.rem(WINDOW - skip, WINDOW), 1)[:, :CHUNK]
        send_ref[i] = jnp.where(lane < FEATS, moved, 0.0).astype(BF16)


def split_w_out(at, w_out):
    n = RING // 2
    return pl.pallas_call(
        split_kernel,
        name="split_w_out",
        out_shape=jax.ShapeDtypeStruct((n, 2 * HD, CHUNK), BF16),
        in_specs=[SMEM, ANY],
        out_specs=VMEM,
        scratch_shapes=[
            pltpu.VMEM((n, 2 * HD, WINDOW), BF16),
            pltpu.SemaphoreType.DMA((n,)),
        ],
    )(at, w_out)


def dout_kernel(deltas, at_ref, w_ref, pa, pb, *refs):
    shards = refs[:RING]
    near_ref, send_ref, wbuf, fbuf, gbuf, hbuf, sem = refs[RING:]
    z, xh, core = at_ref[0], at_ref[1], at_ref[2]
    copies = []
    for i in range(RING):
        chunk = lax.rem(z + deltas[i] + RING, RING)
        half = lax.div(chunk, RING // 2)
        inner = lax.rem(chunk, RING // 2)
        lanes, skip = column_window(2 * chunk + xh)
        place = pl.ds(pl.multiple_of(skip, 16), FEATS)
        far = pltpu.make_async_copy(pa.at[inner], fbuf.at[i], sem.at[i, 1])
        far_too = pltpu.make_async_copy(pb.at[inner], fbuf.at[i], sem.at[i, 1])
        pltpu.make_async_copy(w_ref.at[:, lanes], wbuf.at[i], sem.at[i, 0]).start()

        @pl.when(half == core)
        def _(copy=far):
            copy.start()

        @pl.when(half != core)
        def _(copy=far_too):
            copy.start()

        gbuf[i] = jnp.zeros((WINDOW, ROWS), BF16)
        hbuf[i, FEATS:] = jnp.zeros((CHUNK - FEATS, ROWS), BF16)
        to_far = pltpu.make_async_copy(shards[i], hbuf.at[i, :FEATS], sem.at[i, 2])
        to_far.start()
        own_rows = pltpu.make_async_copy(w_ref.at[:, lanes], wbuf.at[i], sem.at[i, 0])
        copies.append((own_rows, far, to_far, place))
    near = far = None
    for i in range(RING):
        for c in copies[i][:3]:
            c.wait()
        gbuf[i, copies[i][3], :] = hbuf[i, :FEATS]
        add_far = dot(fbuf[i], hbuf[i])
        add_near = dot(wbuf[i], gbuf[i])
        far = add_far if i == 0 else far + add_far
        near = add_near if i == 0 else near + add_near
    near_ref[...] = near
    send_ref[...] = far.astype(BF16)


def dout_parts(at, w_out, far_w, shards):
    deltas = tuple(shards)
    half = (2 * HD, ROWS)
    return pl.pallas_call(
        lambda *refs: dout_kernel(deltas, *refs),
        name="dout_parts",
        out_shape=(jax.ShapeDtypeStruct(half, F32), jax.ShapeDtypeStruct(half, BF16)),
        in_specs=[SMEM] + [ANY] * (3 + RING),
        out_specs=(VMEM, VMEM),
        scratch_shapes=[
            pltpu.VMEM((RING, 2 * HD, WINDOW), BF16),
            pltpu.VMEM((RING, 2 * HD, CHUNK), BF16),
            pltpu.VMEM((RING, WINDOW, ROWS), BF16),
            pltpu.VMEM((RING, CHUNK, ROWS), BF16),
            pltpu.SemaphoreType.DMA((RING, 3)),
        ],
    )(at, w_out, *far_w, *shards.values())


def join_kernel(core_ref, mine_ref, got_ref, own_ref, *send_refs):
    core = core_ref[0]
    for d in range(HALF + 1):
        at = d - core
        inside = (at >= 0) & (at < HALF)
        other = got_ref[jnp.clip(at, 0, HALF - 1)].astype(F32)
        total = jnp.where(inside, other, 0.0)
        if d < HALF:
            total = total + mine_ref[d].astype(F32)
        if d == 0:
            own_ref[...] = total
        else:
            send_refs[d - 1][...] = total.astype(BF16)


def join_partials(core, mine, got):
    shape = (ROWS, 2 * HD)
    result = pl.pallas_call(
        join_kernel,
        name="join_partials",
        out_shape=(jax.ShapeDtypeStruct(shape, F32),) + (jax.ShapeDtypeStruct(shape, BF16),) * HALF,
        in_specs=[SMEM, VMEM, VMEM],
        out_specs=(VMEM,) * (HALF + 1),
    )(core, mine, got)
    return result[0], result[1:]


def total_kernel(own_ref, *refs):
    total = own_ref[...]
    for ref in refs[:HALF]:
        total = total + ref[...].astype(F32)
    refs[HALF][...] = total.astype(BF16).T


def total_partials(own, parts):
    return pl.pallas_call(
        total_kernel,
        name="total_partials",
        out_shape=jax.ShapeDtypeStruct((2 * HD, ROWS), BF16),
        in_specs=[VMEM] * (HALF + 1),
        out_specs=VMEM,
    )(own, *parts)


def own_project_kernel(deltas, at_ref, *refs):
    n = len(deltas)
    wq, wk, wv, pa, pb, gq, gkv, gq2 = refs[:8]
    outs = refs[8 : 8 + n]
    wbuf, gbuf, obuf, sem, g_sem, out_sem = refs[8 + n :]
    z, xh, core = at_ref[0], at_ref[1], at_ref[2]
    g_copies = [
        pltpu.make_async_copy(g, gbuf.at[2 * HD * i : 2 * HD * (i + 1)], g_sem.at[i])
        for i, g in enumerate((gq, gkv, gq2))
    ]
    for c in g_copies:
        c.start()
    copies = []
    for i, delta in enumerate(deltas):
        chunk = lax.rem(z + delta + RING, RING)
        rows = pl.ds(pl.multiple_of((2 * chunk + xh) * FEATS, 16), FEATS)
        place = ((wq, 0, 2 * HD), (wk, 2 * HD, HD), (wv, 3 * HD, HD))
        mine = [
            pltpu.make_async_copy(w.at[rows, :], wbuf.at[i, :, lane : lane + size], sem.at[i, j])
            for j, (w, lane, size) in enumerate(place)
        ]
        for c in mine:
            c.start()
        inner = lax.rem(chunk, RING // 2)
        near, far = [
            pltpu.make_async_copy(
                p.at[inner, :, : 2 * HD], wbuf.at[i, :, 4 * HD :], sem.at[i, 3]
            )
            for p in (pa, pb)
        ]
        same = lax.div(chunk, RING // 2) == core

        @pl.when(same)
        def _(copy=near):
            copy.start()

        @pl.when(jnp.logical_not(same))
        def _(copy=far):
            copy.start()

        copies.append(mine + [near])
    for c in g_copies:
        c.wait()
    results = []
    for i in range(n):
        for c in copies[i]:
            c.wait()
        obuf[i] = dot(wbuf[i], gbuf[...])
        results.append(pltpu.make_async_copy(obuf.at[i], outs[i], out_sem.at[i]))
        results[-1].start()
    for c in results:
        c.wait()


def own_project(deltas, at, weights, far, grads):
    n = len(deltas)
    return pl.pallas_call(
        lambda *refs: own_project_kernel(deltas, *refs),
        name="own_project",
        out_shape=(jax.ShapeDtypeStruct((FEATS, ROWS), F32),) * n,
        in_specs=[SMEM] + [ANY] * 8,
        out_specs=(ANY,) * n,
        scratch_shapes=[
            pltpu.VMEM((n, FEATS, 6 * HD), BF16),
            pltpu.VMEM((6 * HD, ROWS), BF16),
            pltpu.VMEM((n, FEATS, ROWS), F32),
            pltpu.SemaphoreType.DMA((n, 4)),
            pltpu.SemaphoreType.DMA((3,)),
            pltpu.SemaphoreType.DMA((n,)),
        ],
    )(at, *weights, *far, *grads)


def far_project_kernel(deltas, at_ref, *refs):
    n = len(deltas)
    pa, pb, gkv2 = refs[:3]
    sums = refs[3 : 3 + n]
    outs = refs[3 + n : 3 + 2 * n]
    wbuf, gbuf, abuf, obuf, sem, g_sem, out_sem = refs[3 + 2 * n :]
    z, core = at_ref[0], at_ref[2]
    g_copy = pltpu.make_async_copy(gkv2, gbuf, g_sem.at[0])
    g_copy.start()
    copies = []
    for i, delta in enumerate(deltas):
        chunk = lax.rem(z + delta + RING, RING)
        inner = lax.rem(chunk, RING // 2)
        near, far = [
            pltpu.make_async_copy(p.at[inner, :, 2 * HD :], wbuf.at[i], sem.at[i, 0])
            for p in (pa, pb)
        ]
        same = lax.div(chunk, RING // 2) == core

        @pl.when(same)
        def _(copy=near):
            copy.start()

        @pl.when(jnp.logical_not(same))
        def _(copy=far):
            copy.start()

        before = pltpu.make_async_copy(sums[i], abuf.at[i], sem.at[i, 1])
        before.start()
        copies.append((near, before))
    g_copy.wait()
    results = []
    for i in range(n):
        for c in copies[i]:
            c.wait()
        obuf[i] = (abuf[i] + dot(wbuf[i], gbuf[...])).astype(obuf.dtype)
        results.append(pltpu.make_async_copy(obuf.at[i], outs[i], out_sem.at[i]))
        results[-1].start()
    for c in results:
        c.wait()


def far_project(deltas, at, far, gkvt_far, sums, kind):
    n = len(deltas)
    return pl.pallas_call(
        lambda *refs: far_project_kernel(deltas, *refs),
        name="far_project",
        out_shape=(jax.ShapeDtypeStruct((FEATS, ROWS), kind),) * n,
        in_specs=[SMEM] + [ANY] * (3 + n),
        out_specs=(ANY,) * n,
        scratch_shapes=[
            pltpu.VMEM((n, FEATS, 2 * HD), BF16),
            pltpu.VMEM((2 * HD, ROWS), BF16),
            pltpu.VMEM((n, FEATS, ROWS), F32),
            pltpu.VMEM((n, FEATS, ROWS), kind),
            pltpu.SemaphoreType.DMA((n, 2)),
            pltpu.SemaphoreType.DMA((1,)),
            pltpu.SemaphoreType.DMA((n,)),
        ],
    )(at, *far, gkvt_far, *sums)


def swapped(x, axis):
    return lax.ppermute(x, axis, [(0, 1), (1, 0)])


def chip_pairs(d):
    return [(i, i + 2 * d) for i in range(lax.axis_size(AA) - 2 * d) if d < HALF or i % 2]


def chips_on(x, d):
    return lax.ppermute(x, AA, chip_pairs(d))


def chips_back(x, d):
    return lax.ppermute(x, AA, [(j, i) for i, j in chip_pairs(d)])


def round_z(x, step):
    return lax.ppermute(x, "z", [(i, (i + step) % RING) for i in range(RING)])


def body(query, keys, values, grad_out, segment_ids, w_query, w_key, w_value, w_out):
    core = lax.axis_index("core")
    z = lax.axis_index("z")
    xh = lax.axis_index("xh")
    own = lax.axis_index(AA)[None]
    at = jnp.stack((z, xh, core))
    shards = {0: grad_out.T}
    for k in range(1, RING // 2 + 1):
        shards[-k] = round_z(shards[1 - k], 1)
        if k < RING // 2:
            shards[k] = round_z(shards[k - 1], -1)
    send_w = split_w_out(at, w_out)
    far_w = swapped(send_w, "xh")
    far_w = (far_w, swapped(far_w, "core"))
    ids = jnp.pad(
        segment_ids.astype(BF16).reshape(ROWS // HD, HD),
        ((0, SEG_ROWS - ROWS // HD), (0, HD)),
    )
    block = jnp.concatenate((jnp.concatenate((keys, values), axis=1), ids), axis=0)
    twins = [block] + [chips_on(block, d) for d in range(1, HALF + 1)]
    others = [swapped(twins[d], "core") for d in range(HALF + 1)]
    wanted = [
        lax.dynamic_index_in_dim(
            w.reshape(2, RING // 2, 2, FEATS, -1), core, 0, keepdims=False
        )
        for w in (w_query, w_key, w_value)
    ]
    wanted = [lax.dynamic_index_in_dim(w, 1 - xh, 1, keepdims=False) for w in wanted]
    wanted = jnp.concatenate(wanted, axis=2)
    far_mine = swapped(wanted, "xh")
    far_other = swapped(far_mine, "core")

    qseg = segment_ids[None, :]
    state = attention_stats(own, qseg, query, twins, others, NEAR, BLOCKS)
    near, send = dout_parts(at, w_out, far_w, shards)
    far = swapped(send, "xh")
    stats = attention_stats(own, qseg, query, twins, others, 0, NEAR, state)
    gqt, mine, theirs = attention_grads(own, stats, query, near, far, twins, others)
    got = swapped(theirs, "core")
    gqt_far = swapped(gqt, "xh")
    own_total, sends = join_partials(core[None], mine, got)
    parts = [chips_back(sends[d - 1], d) for d in range(HALF, 0, -1)]
    gkvt = total_partials(own_total, parts)
    gkvt_far = swapped(gkvt, "xh")

    weights = (w_query, w_key, w_value)
    far_rows = (far_mine, far_other)
    deltas = (4, -3, 3, -2, 2, -1, 1, 0)
    sums = own_project(deltas, at, weights, far_rows, (gqt, gkvt, gqt_far))
    ahead, behind = far_project(deltas[:2], at, far_rows, gkvt_far, sums[:2], BF16)
    rest = far_project(deltas[2:], at, far_rows, gkvt_far, sums[2:], F32)
    ahead = round_z(ahead, 1)
    behind = round_z(behind, -1)
    for k in (2, 3):
        add_ahead, add_behind = rest[2 * k - 4], rest[2 * k - 3]
        ahead = round_z((ahead.astype(F32) + add_ahead).astype(BF16), 1)
        behind = round_z((behind.astype(F32) + add_behind).astype(BF16), -1)
    ahead = round_z((ahead.astype(F32) + rest[4]).astype(BF16), 1)
    result = (ahead.astype(F32) + behind.astype(F32) + rest[5]).astype(BF16)
    return result.T


def solution(mesh):
    finer = Mesh(mesh.devices.reshape(2, 4, 2, RING, 2), AA + BA)
    return jax.shard_map(
        body,
        mesh=finer,
        in_specs=(
            P(AA, BA),
            P(AA, BA),
            P(AA, BA),
            P(AA, BA),
            P(AA),
            P(None, BA),
            P(None, BA),
            P(None, BA),
            P(BA, None),
        ),
        out_specs=P(AA, BA),
        check_vma=False,
    )
```

```python
import math

import jax
import jax.numpy as jnp
from jax import lax
from jax.experimental import pallas as pl
from jax.experimental.pallas import tpu as pltpu
from jax.sharding import Mesh
from jax.sharding import PartitionSpec as P


D = 5376
HQ = 32
HD = 128
DOCS = 6
ROWS = 384
HALF = 5
BLOCKS = 2 * HALF
SEG_ROWS = 16
PACKED = ROWS + SEG_ROWS
FEATS = 336
UP_ROWS = 176
CHUNK = 384
WINDOW = 512
BOTH = 2 * ROWS
TILE = 256
STATS_TILE = 128
NEAR = 6
RING = 8
AA = ("xl", "y", "core")
BA = ("z", "xh")
NEG_FILL = -1e30
SCALE = (D / HQ) ** (-0.5)
SCALE2 = SCALE * math.log2(math.e)
F32 = jnp.float32
BF16 = jnp.bfloat16
VMEM = pl.BlockSpec(memory_space=pltpu.VMEM)
SMEM = pl.BlockSpec(memory_space=pltpu.SMEM)
ANY = pl.BlockSpec(memory_space=pl.ANY)


def dot(a, b):
    return lax.dot_general(a, b, (((1,), (0,)), ((), ())), preferred_element_type=F32)


def sources(low, high):
    odd = [d for d in range(HALF) if low <= BLOCKS - 1 - 2 * d < high]
    even = [k for k in range(HALF) if low <= BLOCKS - 2 - 2 * k < high]
    return odd, even, sorted({k for e in even for k in (e, e + 1)})


def load_window(low, high, core, kv_refs, buf, sem):
    odd, even, extra = sources(low, high)
    twin = dict(zip(odd, kv_refs))
    other = dict(zip(extra, kv_refs[len(odd) :]))
    copies = []
    for d in odd:
        at = BLOCKS - 1 - 2 * d - low
        copies.append(pltpu.make_async_copy(twin[d], buf.at[at], sem.at[at]))
        copies[-1].start()
    for k in even:
        at = BLOCKS - 2 - 2 * k - low
        from_low = pltpu.make_async_copy(other[k], buf.at[at], sem.at[at])
        from_high = pltpu.make_async_copy(other[k + 1], buf.at[at], sem.at[at])

        @pl.when(core == 1)
        def _(copy=from_low):
            copy.start()

        @pl.when(core == 0)
        def _(copy=from_high):
            copy.start()

        copies.append(from_low)
    return copies


def window_refs(low, high, twins, others):
    odd, _, extra = sources(low, high)
    return [twins[d] for d in odd] + [others[k] for k in extra]


def side_by_side(x):
    return jnp.concatenate((x[:HD, :], x[HD:, :]), axis=1)


def one_above_other(x):
    return jnp.concatenate((x[:, :HD], x[:, HD:]), axis=0)


def tiles(width):
    return [slice(t, t + width) for t in range(0, BOTH, width)]


def stats_kernel(low, high, own_ref, qseg_ref, q_ref, *refs):
    near = high == BLOCKS
    odd, _, extra = sources(low, high)
    count = len(odd) + len(extra)
    if near:
        kv_refs = refs[:count]
        m_ref, l_ref, out_ref, start_ref, buf, qt_ref, sem = refs[count:]
    else:
        m_in, l_in, out_in, start_in = refs[:4]
        kv_refs = refs[4 : 4 + count]
        lse_ref, out_ref, start_ref, low_ref, buf, qt_ref, m_ref, l_ref, sem = refs[4 + count :]
    own = own_ref[0]
    copies = load_window(low, high, lax.rem(own, 2), kv_refs, buf, sem)
    qt_ref[...] = one_above_other(q_ref[...]).T
    if near:
        m_ref[...] = jnp.full(m_ref.shape, NEG_FILL, F32)
        l_ref[...] = jnp.zeros(l_ref.shape, F32)
        out_ref[...] = jnp.zeros(out_ref.shape, F32)
    else:
        m_ref[...] = m_in[...]
        l_ref[...] = l_in[...]
        out_ref[...] = out_in[...]
    seg = qseg_ref[...]
    seg0 = jnp.min(seg, axis=1, keepdims=True)
    for c in copies:
        c.wait()
    before = jnp.zeros((SEG_ROWS, HD), jnp.int32)
    line = lax.broadcasted_iota(jnp.int32, (SEG_ROWS, HD), 0)
    for b in range(low, min(high, BLOCKS - 1)):
        ids = buf[b - low, ROWS:, :HD].astype(F32).astype(jnp.int32)
        hit = (line < ROWS // HD) & (ids < seg0) & (own + b >= BLOCKS - 1)
        before = before + hit.astype(jnp.int32)
    start0 = jnp.sum(before) + jnp.maximum(own + low - (BLOCKS - 1), 0) * ROWS
    first_next = (own + high - (BLOCKS - 1)) * ROWS
    start = jnp.zeros((1, ROWS), jnp.int32) + start0
    if near:
        for s in range(1, DOCS):
            here = own * ROWS + jnp.sum((seg < s).astype(jnp.int32), axis=1, keepdims=True)
            start = jnp.where((seg == s) & (seg > seg0), here, start)
        start_ref[...] = start
    else:
        start = jnp.where((seg == seg0) & (start0 < first_next), start, start_in[...])
        start_ref[...] = start
        start0 = jnp.min(start)
    lowest = lax.div(start0, ROWS) - own + (BLOCKS - 1)
    latest = jnp.max(start)
    pos = own * ROWS + lax.broadcasted_iota(jnp.int32, (1, ROWS), 1)
    start = jnp.concatenate((start, start), axis=1)
    pos = jnp.concatenate((pos, pos), axis=1)
    key_at = lax.broadcasted_iota(jnp.int32, (ROWS, STATS_TILE), 0)

    def add_block(b, first, whole):
        kb = buf[b - low, :ROWS, :HD]
        vt = buf[b - low, :ROWS, HD:].T
        for t in tiles(STATS_TILE):
            s = dot(kb, qt_ref[:, t]) * SCALE2
            if not whole:
                allowed = (key_at >= start[:, t] - first) & (key_at <= pos[:, t] - first)
                s = jnp.where(allowed, s, NEG_FILL)
            m_old = m_ref[:, t]
            m_new = jnp.maximum(m_old, jnp.max(s, axis=0, keepdims=True))
            p = jnp.exp2(s - m_new)
            back = jnp.exp2(m_old - m_new)
            l_ref[:, t] = l_ref[:, t] * back + jnp.sum(p, axis=0, keepdims=True)
            m_ref[:, t] = m_new
            out_ref[:, t] = out_ref[:, t] * back + dot(vt, p.astype(BF16))

    def one_block(back_to, carry):
        b = high - 1 - back_to
        first = (own + b - (BLOCKS - 1)) * ROWS
        whole = (first >= latest) & (b < BLOCKS - 1)

        @pl.when(whole)
        def _():
            add_block(b, first, True)

        @pl.when(jnp.logical_not(whole))
        def _():
            add_block(b, first, False)

        return carry

    lax.fori_loop(0, high - jnp.clip(lowest, low, high), one_block, 0)
    if not near:
        low_ref[0] = lowest
        lse_ref[...] = m_ref[...] + jnp.log2(l_ref[...])
        out_ref[...] = out_ref[...] / l_ref[...]


def grads_kernel(own_ref, low_ref, *refs):
    given, refs = refs[:6], refs[6:]
    kv_refs, refs = refs[: BLOCKS + 1], refs[BLOCKS + 1 :]
    gqt_ref, mine_ref, theirs_ref = refs[:3]
    start_ref, q_ref, near_ref, far_ref, lse_ref, out_ref = held = refs[3:9]
    buf, qt_ref, qn_ref, dout_ref, doutt_ref, delta_ref, acc_ref, made, sem, in_sem, out_sem = refs[9:]
    own = own_ref[0]
    arrivals = [pltpu.make_async_copy(x, y, in_sem.at[i]) for i, (x, y) in enumerate(zip(given, held))]
    for c in arrivals:
        c.start()
    load_window(0, BLOCKS, lax.rem(own, 2), kv_refs, buf, sem)
    lowest = low_ref[0]
    acc_ref[...] = jnp.zeros(acc_ref.shape, F32)
    key_at = lax.broadcasted_iota(jnp.int32, (ROWS, TILE), 0)
    for c in arrivals:
        c.wait()
    qn_ref[...] = one_above_other(q_ref[...])
    qt_ref[...] = qn_ref[...].T
    doutt_ref[...] = side_by_side((near_ref[...] + far_ref[...].astype(F32)).astype(BF16))
    dout_ref[...] = doutt_ref[...].T
    delta_ref[...] = jnp.sum(doutt_ref[...].astype(F32) * out_ref[...], axis=0, keepdims=True)
    start = start_ref[...]
    latest = jnp.max(start)
    pos = own * ROWS + lax.broadcasted_iota(jnp.int32, (1, ROWS), 1)
    start = jnp.concatenate((start, start), axis=1)
    pos = jnp.concatenate((pos, pos), axis=1)

    def add_block(b, first, whole):
        kb = buf[b, :ROWS, :HD]
        vb = buf[b, :ROWS, HD:]
        kt = kb.T
        gk = gv = None
        for t in tiles(TILE):
            s = dot(kb, qt_ref[:, t]) * SCALE2
            dp = dot(vb, doutt_ref[:, t])
            p = jnp.exp2(s - lse_ref[:, t])
            if not whole:
                allowed = (key_at >= start[:, t] - first) & (key_at <= pos[:, t] - first)
                p = jnp.where(allowed, p, 0.0)
            ds = (p * (dp - delta_ref[:, t])).astype(BF16)
            add_v = dot(p.astype(BF16), dout_ref[t, :])
            add_k = dot(ds, qn_ref[t, :])
            gv = add_v if gv is None else gv + add_v
            gk = add_k if gk is None else gk + add_k
            acc_ref[:, t] += dot(kt, ds)
        made[b, :, :HD] = (gk * SCALE).astype(BF16)
        made[b, :, HD:] = gv.astype(BF16)

    def departure(b, target):
        d = (BLOCKS - 1 - b) // 2 if isinstance(b, int) else lax.div(BLOCKS - 1 - b, 2)
        return pltpu.make_async_copy(made.at[b], target.at[d], out_sem.at[b])

    def one_block(b, carry):
        pltpu.make_async_copy(kv_refs[0], buf.at[b], sem.at[b]).wait()
        first = (own + b - (BLOCKS - 1)) * ROWS
        whole = (first >= latest) & (b < BLOCKS - 1)

        @pl.when((b >= lowest) & whole)
        def _():
            add_block(b, first, True)

        @pl.when((b >= lowest) & jnp.logical_not(whole))
        def _():
            add_block(b, first, False)

        @pl.when(b < lowest)
        def _():
            made[b] = jnp.zeros((ROWS, 2 * HD), BF16)

        odd = lax.rem(b, 2) == 1

        @pl.when(odd)
        def _():
            departure(b, mine_ref).start()

        @pl.when(jnp.logical_not(odd))
        def _():
            departure(b, theirs_ref).start()

        return carry

    lax.fori_loop(0, BLOCKS, one_block, 0)
    gqt_ref[:HD, :] = (acc_ref[:, :ROWS] * SCALE).astype(BF16)
    gqt_ref[HD:, :] = (acc_ref[:, ROWS:] * SCALE).astype(BF16)
    for b in range(BLOCKS):
        departure(b, mine_ref if b % 2 else theirs_ref).wait()


def attention_stats(own, qseg, query, twins, others, low, high, state=()):
    count = high - low
    window = window_refs(low, high, twins, others)
    row = jax.ShapeDtypeStruct((1, BOTH), F32)
    wide = jax.ShapeDtypeStruct((HD, BOTH), F32)
    start = jax.ShapeDtypeStruct((1, ROWS), jnp.int32)
    lowest = jax.ShapeDtypeStruct((1,), jnp.int32)
    scratch = [
        pltpu.VMEM((count, PACKED, 2 * HD), BF16),
        pltpu.VMEM((HD, BOTH), BF16),
    ]
    if state:
        scratch += [pltpu.VMEM((1, BOTH), F32), pltpu.VMEM((1, BOTH), F32)]
    return pl.pallas_call(
        lambda *refs: stats_kernel(low, high, *refs),
        name="stats_far" if state else "stats_near",
        out_shape=(row, wide, start, lowest) if state else (row, row, wide, start),
        in_specs=[SMEM, VMEM, VMEM] + [VMEM] * len(state) + [ANY] * len(window),
        out_specs=(VMEM, VMEM, VMEM, SMEM if state else VMEM),
        scratch_shapes=scratch + [pltpu.SemaphoreType.DMA((count,))],
    )(own, qseg, query, *state, *window)


def attention_grads(own, stats, query, near, far, twins, others):
    lse, out, start, lowest = stats
    window = window_refs(0, BLOCKS, twins, others)
    given = (start, query, near, far, lse, out)
    return pl.pallas_call(
        grads_kernel,
        name="attention_grads",
        out_shape=(
            jax.ShapeDtypeStruct((2 * HD, ROWS), BF16),
            jax.ShapeDtypeStruct((HALF, ROWS, 2 * HD), BF16),
            jax.ShapeDtypeStruct((HALF, ROWS, 2 * HD), BF16),
        ),
        in_specs=[SMEM, SMEM] + [ANY] * (len(given) + len(window)),
        out_specs=(VMEM, ANY, ANY),
        scratch_shapes=[pltpu.VMEM(x.shape, x.dtype) for x in given]
        + [
            pltpu.VMEM((BLOCKS, PACKED, 2 * HD), BF16),
            pltpu.VMEM((HD, BOTH), BF16),
            pltpu.VMEM((BOTH, HD), BF16),
            pltpu.VMEM((BOTH, HD), BF16),
            pltpu.VMEM((HD, BOTH), BF16),
            pltpu.VMEM((1, BOTH), F32),
            pltpu.VMEM((HD, BOTH), F32),
            pltpu.VMEM((BLOCKS, ROWS, 2 * HD), BF16),
            pltpu.SemaphoreType.DMA((BLOCKS,)),
            pltpu.SemaphoreType.DMA((len(given),)),
            pltpu.SemaphoreType.DMA((BLOCKS,)),
        ],
    )(own, lowest, *given, *window)


def column_window(chunk):
    base = jnp.minimum(lax.div(chunk * FEATS, HD) * HD, D - WINDOW)
    return pl.ds(pl.multiple_of(base, HD), WINDOW), chunk * FEATS - base


def split_kernel(at_ref, w_ref, send_ref, buf, sem):
    first = at_ref[2] * (RING // 2)
    other = 1 - at_ref[1]
    copies = []
    for i in range(RING // 2):
        lanes, skip = column_window(2 * (first + i) + other)
        copy = pltpu.make_async_copy(w_ref.at[:, lanes], buf.at[i], sem.at[i])
        copy.start()
        copies.append((copy, skip))
    lane = lax.broadcasted_iota(jnp.int32, (2 * HD, CHUNK), 1)
    for i, (copy, skip) in enumerate(copies):
        copy.wait()
        moved = pltpu.roll(buf[i].astype(F32), lax.rem(WINDOW - skip, WINDOW), 1)[:, :CHUNK]
        send_ref[i] = jnp.where(lane < FEATS, moved, 0.0).astype(BF16)


def split_w_out(at, w_out):
    n = RING // 2
    return pl.pallas_call(
        split_kernel,
        name="split_w_out",
        out_shape=jax.ShapeDtypeStruct((n, 2 * HD, CHUNK), BF16),
        in_specs=[SMEM, ANY],
        out_specs=VMEM,
        scratch_shapes=[
            pltpu.VMEM((n, 2 * HD, WINDOW), BF16),
            pltpu.SemaphoreType.DMA((n,)),
        ],
    )(at, w_out)


def dout_kernel(deltas, at_ref, w_ref, pa, pb, *refs):
    shards = refs[:RING]
    near_ref, send_ref, wbuf, fbuf, gbuf, hbuf, sem = refs[RING:]
    z, xh, core = at_ref[0], at_ref[1], at_ref[2]
    copies = []
    for i in range(RING):
        chunk = lax.rem(z + deltas[i] + RING, RING)
        half = lax.div(chunk, RING // 2)
        inner = lax.rem(chunk, RING // 2)
        lanes, skip = column_window(2 * chunk + xh)
        place = pl.ds(pl.multiple_of(skip, 16), FEATS)
        far = pltpu.make_async_copy(pa.at[inner], fbuf.at[i], sem.at[i, 1])
        far_too = pltpu.make_async_copy(pb.at[inner], fbuf.at[i], sem.at[i, 1])
        pltpu.make_async_copy(w_ref.at[:, lanes], wbuf.at[i], sem.at[i, 0]).start()

        @pl.when(half == core)
        def _(copy=far):
            copy.start()

        @pl.when(half != core)
        def _(copy=far_too):
            copy.start()

        gbuf[i] = jnp.zeros((WINDOW, ROWS), BF16)
        hbuf[i, FEATS:] = jnp.zeros((CHUNK - FEATS, ROWS), BF16)
        to_far = pltpu.make_async_copy(shards[i], hbuf.at[i, :FEATS], sem.at[i, 2])
        to_far.start()
        own_rows = pltpu.make_async_copy(w_ref.at[:, lanes], wbuf.at[i], sem.at[i, 0])
        copies.append((own_rows, far, to_far, place))
    near = far = None
    for i in range(RING):
        for c in copies[i][:3]:
            c.wait()
        gbuf[i, copies[i][3], :] = hbuf[i, :FEATS]
        add_far = dot(fbuf[i], hbuf[i])
        add_near = dot(wbuf[i], gbuf[i])
        far = add_far if i == 0 else far + add_far
        near = add_near if i == 0 else near + add_near
    near_ref[...] = near
    send_ref[...] = far.astype(BF16)


def dout_parts(at, w_out, far_w, shards):
    deltas = tuple(shards)
    half = (2 * HD, ROWS)
    return pl.pallas_call(
        lambda *refs: dout_kernel(deltas, *refs),
        name="dout_parts",
        out_shape=(jax.ShapeDtypeStruct(half, F32), jax.ShapeDtypeStruct(half, BF16)),
        in_specs=[SMEM] + [ANY] * (3 + RING),
        out_specs=(VMEM, VMEM),
        scratch_shapes=[
            pltpu.VMEM((RING, 2 * HD, WINDOW), BF16),
            pltpu.VMEM((RING, 2 * HD, CHUNK), BF16),
            pltpu.VMEM((RING, WINDOW, ROWS), BF16),
            pltpu.VMEM((RING, CHUNK, ROWS), BF16),
            pltpu.SemaphoreType.DMA((RING, 3)),
        ],
    )(at, w_out, *far_w, *shards.values())


def join_kernel(core_ref, mine_ref, got_ref, own_ref, *refs):
    send_refs = refs[:HALF]
    mine, got, own, made, in_sem, out_sem = refs[HALF:]
    core = core_ref[0]
    arrivals = []
    for d in reversed(range(HALF)):
        pair = [
            pltpu.make_async_copy(x.at[d], y.at[d], in_sem.at[i, d])
            for i, (x, y) in enumerate(((got_ref, got), (mine_ref, mine)))
        ]
        for c in pair:
            c.start()
        arrivals.append(pair)
    arrivals.reverse()
    departures = []
    for d in reversed(range(HALF + 1)):
        if d > 0:
            for c in arrivals[d - 1]:
                c.wait()
        at = d - core
        inside = (at >= 0) & (at < HALF)
        total = jnp.where(inside, got[jnp.clip(at, 0, HALF - 1)].astype(F32), 0.0)
        if d < HALF:
            total = total + mine[d].astype(F32)
        if d == 0:
            own[...] = total
            departures.append(pltpu.make_async_copy(own, own_ref, out_sem.at[d]))
        else:
            made[d - 1] = total.astype(BF16)
            departures.append(
                pltpu.make_async_copy(made.at[d - 1], send_refs[d - 1], out_sem.at[d])
            )
        departures[-1].start()
    for c in departures:
        c.wait()


def join_partials(core, mine, got):
    shape = (ROWS, 2 * HD)
    result = pl.pallas_call(
        join_kernel,
        name="join_partials",
        out_shape=(jax.ShapeDtypeStruct(shape, F32),) + (jax.ShapeDtypeStruct(shape, BF16),) * HALF,
        in_specs=[SMEM, ANY, ANY],
        out_specs=(ANY,) * (HALF + 1),
        scratch_shapes=[
            pltpu.VMEM((HALF, *shape), BF16),
            pltpu.VMEM((HALF, *shape), BF16),
            pltpu.VMEM(shape, F32),
            pltpu.VMEM((HALF, *shape), BF16),
            pltpu.SemaphoreType.DMA((2, HALF)),
            pltpu.SemaphoreType.DMA((HALF + 1,)),
        ],
    )(core, mine, got)
    return result[0], result[1:]


def total_kernel(own_ref, *refs):
    part_refs, (out_ref, own, parts, sem) = refs[:HALF], refs[HALF:]
    copies = [pltpu.make_async_copy(own_ref, own, sem.at[HALF])]
    copies += [pltpu.make_async_copy(x, parts.at[i], sem.at[i]) for i, x in enumerate(part_refs)]
    for c in copies:
        c.start()
    for c in copies:
        c.wait()
    total = own[...]
    for i in range(HALF):
        total = total + parts[i].astype(F32)
    out_ref[...] = total.astype(BF16).T


def total_partials(own, parts):
    shape = (ROWS, 2 * HD)
    return pl.pallas_call(
        total_kernel,
        name="total_partials",
        out_shape=jax.ShapeDtypeStruct((2 * HD, ROWS), BF16),
        in_specs=[ANY] * (HALF + 1),
        out_specs=VMEM,
        scratch_shapes=[
            pltpu.VMEM(shape, F32),
            pltpu.VMEM((HALF, *shape), BF16),
            pltpu.SemaphoreType.DMA((HALF + 1,)),
        ],
    )(own, *parts)


def project_kernel(deltas, own_lanes, far_lane, more, at_ref, *refs):
    n, k = len(deltas), len(own_lanes)
    weights = refs[:k]
    pa, pb, g_own, g_far = refs[k : k + 4]
    refs = refs[k + 4 :]
    sums, refs = (refs[:n], refs[n:]) if more else ((), refs)
    outs, refs = refs[:n], refs[n:]
    wbuf, gbuf, obuf, sem, g_sem, out_sem, *held = refs
    z, xh, core = at_ref[0], at_ref[1], at_ref[2]
    width = 2 * HD
    g_copies = [
        pltpu.make_async_copy(g, gbuf.at[width * i : width * (i + 1)], g_sem.at[i])
        for i, g in enumerate((g_own, g_far))
    ]
    for c in g_copies:
        c.start()
    copies = []
    for i, delta in enumerate(deltas):
        chunk = lax.rem(z + delta + RING, RING)
        rows = pl.ds(pl.multiple_of((2 * chunk + xh) * FEATS, 16), FEATS)
        mine = [
            pltpu.make_async_copy(w.at[rows, :], wbuf.at[i, :, lane : lane + size], sem.at[i, j])
            for j, (w, (lane, size)) in enumerate(zip(weights, own_lanes))
        ]
        if more:
            mine.append(pltpu.make_async_copy(sums[i], held[0].at[i], sem.at[i, k + 1]))
        for c in mine:
            c.start()
        inner = lax.rem(chunk, RING // 2)
        near, far = [
            pltpu.make_async_copy(
                p.at[inner, :, far_lane : far_lane + width], wbuf.at[i, :, width:], sem.at[i, k]
            )
            for p in (pa, pb)
        ]
        same = lax.div(chunk, RING // 2) == core

        @pl.when(same)
        def _(copy=near):
            copy.start()

        @pl.when(jnp.logical_not(same))
        def _(copy=far):
            copy.start()

        copies.append(mine + [near])
    for c in g_copies:
        c.wait()
    results = []
    for i in range(n):
        for c in copies[i]:
            c.wait()
        total = dot(wbuf[i], gbuf[...])
        if more:
            total = total + held[0][i]
        obuf[i] = total.astype(obuf.dtype)
        results.append(pltpu.make_async_copy(obuf.at[i], outs[i], out_sem.at[i]))
        results[-1].start()
    for c in results:
        c.wait()


def project(deltas, at, weights, own_lanes, far, far_lane, g_own, g_far, sums, kind):
    n, k = len(deltas), len(weights)
    more = len(sums) > 0
    return pl.pallas_call(
        lambda *refs: project_kernel(deltas, own_lanes, far_lane, more, *refs),
        name="project",
        out_shape=(jax.ShapeDtypeStruct((FEATS, ROWS), kind),) * n,
        in_specs=[SMEM] + [ANY] * (k + 4 + len(sums)),
        out_specs=(ANY,) * n,
        scratch_shapes=[
            pltpu.VMEM((n, FEATS, 4 * HD), BF16),
            pltpu.VMEM((4 * HD, ROWS), BF16),
            pltpu.VMEM((n, FEATS, ROWS), kind),
            pltpu.SemaphoreType.DMA((n, k + 2)),
            pltpu.SemaphoreType.DMA((2,)),
            pltpu.SemaphoreType.DMA((n,)),
        ]
        + [pltpu.VMEM((n, FEATS, ROWS), F32)] * more,
    )(at, *weights, *far, g_own, g_far, *sums)


def arrive(x):
    return pltpu.with_memory_space_constraint(x, pltpu.VMEM)


def swapped(x, axis):
    return lax.ppermute(x, axis, [(0, 1), (1, 0)])


def chip_pairs(d):
    return [(i, i + 2 * d) for i in range(lax.axis_size(AA) - 2 * d) if d < HALF or i % 2]


def chips_on(x, d):
    return lax.ppermute(x, AA, chip_pairs(d))


def chips_back(x, d):
    return arrive(lax.ppermute(x, AA, [(j, i) for i, j in chip_pairs(d)]))


def round_z(x, step):
    return lax.ppermute(x, "z", [(i, (i + step) % RING) for i in range(RING)])


def body(query, keys, values, grad_out, segment_ids, w_query, w_key, w_value, w_out):
    core = lax.axis_index("core")
    z = lax.axis_index("z")
    xh = lax.axis_index("xh")
    own = lax.axis_index(AA)[None]
    at = jnp.stack((z, xh, core))
    shards = {0: grad_out.T}
    for k in range(1, RING // 2 + 1):
        shards[-k] = round_z(shards[1 - k], 1)
        if k < RING // 2:
            shards[k] = round_z(shards[k - 1], -1)
    send_w = split_w_out(at, w_out)
    far_w = swapped(send_w, "xh")
    far_w = (far_w, swapped(far_w, "core"))
    ids = jnp.pad(
        segment_ids.astype(BF16).reshape(ROWS // HD, HD),
        ((0, SEG_ROWS - ROWS // HD), (0, HD)),
    )
    block = jnp.concatenate((jnp.concatenate((keys, values), axis=1), ids), axis=0)
    twins = [block] + [chips_on(block, d) for d in range(1, HALF + 1)]
    others = [swapped(twins[d], "core") for d in range(HALF + 1)]
    wanted = [
        lax.dynamic_index_in_dim(
            w.reshape(2, RING // 2, 2, FEATS, -1), core, 0, keepdims=False
        )
        for w in (w_query, w_key, w_value)
    ]
    wanted = [lax.dynamic_index_in_dim(w, 1 - xh, 1, keepdims=False) for w in wanted]
    wanted = jnp.concatenate(wanted, axis=2)
    far_mine = swapped(wanted, "xh")
    far_other = swapped(far_mine, "core")

    qseg = segment_ids[None, :]
    state = attention_stats(own, qseg, query, twins, others, NEAR, BLOCKS)
    near, send = dout_parts(at, w_out, far_w, shards)
    far = arrive(swapped(send, "xh"))
    stats = attention_stats(own, qseg, query, twins, others, 0, NEAR, state)
    gqt, mine, theirs = attention_grads(own, stats, query, near, far, twins, others)
    got = swapped(theirs, "core")
    gqt_far = arrive(swapped(gqt, "xh"))
    own_total, sends = join_partials(core[None], mine, got)
    parts = [chips_back(sends[d - 1], d) for d in range(HALF, 0, -1)]
    gkvt = total_partials(own_total, parts)
    gkvt_far = arrive(swapped(gkvt, "xh"))

    deltas = (4, 3, -3, 2, -2, 1, -1, 0)
    far_rows = (far_mine, far_other)
    q_lanes = ((0, 2 * HD),)
    sums = project(deltas, at, (w_query,), q_lanes, far_rows, 0, gqt, gqt_far, (), F32)
    kv = (w_key, w_value)
    kv_lanes = ((0, HD), (HD, HD))
    args = (at, kv, kv_lanes, far_rows, 2 * HD, gkvt, gkvt_far)
    (across,) = project(deltas[:1], *args, sums[:1], BF16)
    rest = project(deltas[1:], *args, sums[1:], F32)
    ahead = round_z(across[:UP_ROWS], 1).astype(F32)
    behind = round_z(across[UP_ROWS:], -1).astype(F32)
    ahead = rest[0] + jnp.pad(ahead, ((0, FEATS - UP_ROWS), (0, 0)))
    behind = rest[1] + jnp.pad(behind, ((UP_ROWS, 0), (0, 0)))
    for k in (2, 3, 4):
        ahead = round_z(ahead.astype(BF16), 1).astype(F32)
        behind = round_z(behind.astype(BF16), -1).astype(F32)
        if k < 4:
            ahead, behind = ahead + rest[2 * k - 2], behind + rest[2 * k - 1]
    result = (ahead + behind + rest[6]).astype(BF16)
    return result.T


def solution(mesh):
    finer = Mesh(mesh.devices.reshape(2, 4, 2, RING, 2), AA + BA)
    return jax.shard_map(
        body,
        mesh=finer,
        in_specs=(
            P(AA, BA),
            P(AA, BA),
            P(AA, BA),
            P(AA, BA),
            P(AA),
            P(None, BA),
            P(None, BA),
            P(None, BA),
            P(BA, None),
        ),
        out_specs=P(AA, BA),
        check_vma=False,
    )
```

```python
import math

import jax
import jax.numpy as jnp
from jax import lax
from jax.experimental import pallas as pl
from jax.experimental.pallas import tpu as pltpu
from jax.sharding import Mesh
from jax.sharding import PartitionSpec as P


D = 5376
HQ = 32
HD = 128
DOCS = 6
ROWS = 384
HALF = 5
BLOCKS = 2 * HALF
SEG_ROWS = 16
PACKED = ROWS + SEG_ROWS
FEATS = 336
CHUNK = 384
WINDOW = 512
BOTH = 2 * ROWS
TILE = 256
STATS_TILE = 128
NEAR = 6
RING = 8
AA = ("xl", "y", "core")
BA = ("z", "xh")
NEG_FILL = -1e30
SCALE = (D / HQ) ** (-0.5)
SCALE2 = SCALE * math.log2(math.e)
F32 = jnp.float32
BF16 = jnp.bfloat16
VMEM = pl.BlockSpec(memory_space=pltpu.VMEM)
SMEM = pl.BlockSpec(memory_space=pltpu.SMEM)
ANY = pl.BlockSpec(memory_space=pl.ANY)


def dot(a, b):
    return lax.dot_general(a, b, (((1,), (0,)), ((), ())), preferred_element_type=F32)


def sources(low, high):
    odd = [d for d in range(HALF) if low <= BLOCKS - 1 - 2 * d < high]
    even = [k for k in range(HALF) if low <= BLOCKS - 2 - 2 * k < high]
    return odd, even, sorted({k for e in even for k in (e, e + 1)})


def load_window(low, high, core, kv_refs, buf, sem):
    odd, even, extra = sources(low, high)
    twin = dict(zip(odd, kv_refs))
    other = dict(zip(extra, kv_refs[len(odd) :]))
    copies = []
    for d in odd:
        at = BLOCKS - 1 - 2 * d - low
        copies.append(pltpu.make_async_copy(twin[d], buf.at[at], sem.at[at]))
        copies[-1].start()
    for k in even:
        at = BLOCKS - 2 - 2 * k - low
        from_low = pltpu.make_async_copy(other[k], buf.at[at], sem.at[at])
        from_high = pltpu.make_async_copy(other[k + 1], buf.at[at], sem.at[at])

        @pl.when(core == 1)
        def _(copy=from_low):
            copy.start()

        @pl.when(core == 0)
        def _(copy=from_high):
            copy.start()

        copies.append(from_low)
    return copies


def window_refs(low, high, twins, others):
    odd, _, extra = sources(low, high)
    return [twins[d] for d in odd] + [others[k] for k in extra]


def side_by_side(x):
    return jnp.concatenate((x[:HD, :], x[HD:, :]), axis=1)


def one_above_other(x):
    return jnp.concatenate((x[:, :HD], x[:, HD:]), axis=0)


def tiles(width):
    return [slice(t, t + width) for t in range(0, BOTH, width)]


def stats_kernel(low, high, own_ref, qseg_ref, q_ref, *refs):
    near = high == BLOCKS
    odd, _, extra = sources(low, high)
    count = len(odd) + len(extra)
    if near:
        kv_refs = refs[:count]
        m_ref, l_ref, out_ref, start_ref, buf, qt_ref, sem = refs[count:]
    else:
        m_in, l_in, out_in, start_in = refs[:4]
        kv_refs = refs[4 : 4 + count]
        lse_ref, out_ref, start_ref, low_ref, buf, qt_ref, m_ref, l_ref, sem = refs[4 + count :]
    own = own_ref[0]
    copies = load_window(low, high, lax.rem(own, 2), kv_refs, buf, sem)
    qt_ref[...] = one_above_other(q_ref[...]).T
    if near:
        m_ref[...] = jnp.full(m_ref.shape, NEG_FILL, F32)
        l_ref[...] = jnp.zeros(l_ref.shape, F32)
        out_ref[...] = jnp.zeros(out_ref.shape, F32)
    else:
        m_ref[...] = m_in[...]
        l_ref[...] = l_in[...]
        out_ref[...] = out_in[...]
    seg = qseg_ref[...]
    seg0 = jnp.min(seg, axis=1, keepdims=True)
    for c in copies:
        c.wait()
    before = jnp.zeros((SEG_ROWS, HD), jnp.int32)
    line = lax.broadcasted_iota(jnp.int32, (SEG_ROWS, HD), 0)
    for b in range(low, min(high, BLOCKS - 1)):
        ids = buf[b - low, ROWS:, :HD].astype(F32).astype(jnp.int32)
        hit = (line < ROWS // HD) & (ids < seg0) & (own + b >= BLOCKS - 1)
        before = before + hit.astype(jnp.int32)
    start0 = jnp.sum(before) + jnp.maximum(own + low - (BLOCKS - 1), 0) * ROWS
    first_next = (own + high - (BLOCKS - 1)) * ROWS
    start = jnp.zeros((1, ROWS), jnp.int32) + start0
    if near:
        for s in range(1, DOCS):
            here = own * ROWS + jnp.sum((seg < s).astype(jnp.int32), axis=1, keepdims=True)
            start = jnp.where((seg == s) & (seg > seg0), here, start)
        start_ref[...] = start
    else:
        start = jnp.where((seg == seg0) & (start0 < first_next), start, start_in[...])
        start_ref[...] = start
        start0 = jnp.min(start)
    lowest = lax.div(start0, ROWS) - own + (BLOCKS - 1)
    latest = jnp.max(start)
    pos = own * ROWS + lax.broadcasted_iota(jnp.int32, (1, ROWS), 1)
    start = jnp.concatenate((start, start), axis=1)
    pos = jnp.concatenate((pos, pos), axis=1)
    key_at = lax.broadcasted_iota(jnp.int32, (ROWS, STATS_TILE), 0)

    def add_block(b, first, whole):
        kb = buf[b - low, :ROWS, :HD]
        vt = buf[b - low, :ROWS, HD:].T
        for t in tiles(STATS_TILE):
            s = dot(kb, qt_ref[:, t]) * SCALE2
            if not whole:
                allowed = (key_at >= start[:, t] - first) & (key_at <= pos[:, t] - first)
                s = jnp.where(allowed, s, NEG_FILL)
            m_old = m_ref[:, t]
            m_new = jnp.maximum(m_old, jnp.max(s, axis=0, keepdims=True))
            p = jnp.exp2(s - m_new)
            back = jnp.exp2(m_old - m_new)
            l_ref[:, t] = l_ref[:, t] * back + jnp.sum(p, axis=0, keepdims=True)
            m_ref[:, t] = m_new
            out_ref[:, t] = out_ref[:, t] * back + dot(vt, p.astype(BF16))

    def one_block(back_to, carry):
        b = high - 1 - back_to
        first = (own + b - (BLOCKS - 1)) * ROWS
        whole = (first >= latest) & (b < BLOCKS - 1)

        @pl.when(whole)
        def _():
            add_block(b, first, True)

        @pl.when(jnp.logical_not(whole))
        def _():
            add_block(b, first, False)

        return carry

    lax.fori_loop(0, high - jnp.clip(lowest, low, high), one_block, 0)
    if not near:
        low_ref[0] = lowest
        lse_ref[...] = m_ref[...] + jnp.log2(l_ref[...])
        out_ref[...] = out_ref[...] / l_ref[...]


def grads_kernel(own_ref, low_ref, *refs):
    given, refs = refs[:6], refs[6:]
    kv_refs, refs = refs[: BLOCKS + 1], refs[BLOCKS + 1 :]
    gqt_ref, mine_ref, theirs_ref = refs[:3]
    start_ref, q_ref, near_ref, far_ref, lse_ref, out_ref = held = refs[3:9]
    buf, qt_ref, qn_ref, dout_ref, doutt_ref, delta_ref, acc_ref, made, sem, in_sem, out_sem = refs[9:]
    own = own_ref[0]
    arrivals = [pltpu.make_async_copy(x, y, in_sem.at[i]) for i, (x, y) in enumerate(zip(given, held))]
    for c in arrivals:
        c.start()
    load_window(0, BLOCKS, lax.rem(own, 2), kv_refs, buf, sem)
    lowest = low_ref[0]
    acc_ref[...] = jnp.zeros(acc_ref.shape, F32)
    key_at = lax.broadcasted_iota(jnp.int32, (ROWS, TILE), 0)
    for c in arrivals:
        c.wait()
    qn_ref[...] = one_above_other(q_ref[...])
    qt_ref[...] = qn_ref[...].T
    doutt_ref[...] = side_by_side((near_ref[...] + far_ref[...].astype(F32)).astype(BF16))
    dout_ref[...] = doutt_ref[...].T
    delta_ref[...] = jnp.sum(doutt_ref[...].astype(F32) * out_ref[...], axis=0, keepdims=True)
    start = start_ref[...]
    latest = jnp.max(start)
    pos = own * ROWS + lax.broadcasted_iota(jnp.int32, (1, ROWS), 1)
    start = jnp.concatenate((start, start), axis=1)
    pos = jnp.concatenate((pos, pos), axis=1)

    def add_block(b, first, whole):
        kb = buf[b, :ROWS, :HD]
        vb = buf[b, :ROWS, HD:]
        kt = kb.T
        gk = gv = None
        for t in tiles(TILE):
            s = dot(kb, qt_ref[:, t]) * SCALE2
            dp = dot(vb, doutt_ref[:, t])
            p = jnp.exp2(s - lse_ref[:, t])
            if not whole:
                allowed = (key_at >= start[:, t] - first) & (key_at <= pos[:, t] - first)
                p = jnp.where(allowed, p, 0.0)
            ds = (p * (dp - delta_ref[:, t])).astype(BF16)
            add_v = dot(p.astype(BF16), dout_ref[t, :])
            add_k = dot(ds, qn_ref[t, :])
            gv = add_v if gv is None else gv + add_v
            gk = add_k if gk is None else gk + add_k
            acc_ref[:, t] += dot(kt, ds)
        made[b, :, :HD] = (gk * SCALE).astype(BF16)
        made[b, :, HD:] = gv.astype(BF16)

    def departure(b, target):
        d = (BLOCKS - 1 - b) // 2 if isinstance(b, int) else lax.div(BLOCKS - 1 - b, 2)
        return pltpu.make_async_copy(made.at[b], target.at[d], out_sem.at[b])

    def one_block(b, carry):
        pltpu.make_async_copy(kv_refs[0], buf.at[b], sem.at[b]).wait()
        first = (own + b - (BLOCKS - 1)) * ROWS
        whole = (first >= latest) & (b < BLOCKS - 1)

        @pl.when((b >= lowest) & whole)
        def _():
            add_block(b, first, True)

        @pl.when((b >= lowest) & jnp.logical_not(whole))
        def _():
            add_block(b, first, False)

        @pl.when(b < lowest)
        def _():
            made[b] = jnp.zeros((ROWS, 2 * HD), BF16)

        odd = lax.rem(b, 2) == 1

        @pl.when(odd)
        def _():
            departure(b, mine_ref).start()

        @pl.when(jnp.logical_not(odd))
        def _():
            departure(b, theirs_ref).start()

        return carry

    lax.fori_loop(0, BLOCKS, one_block, 0)
    gqt_ref[:HD, :] = (acc_ref[:, :ROWS] * SCALE).astype(BF16)
    gqt_ref[HD:, :] = (acc_ref[:, ROWS:] * SCALE).astype(BF16)
    for b in range(BLOCKS):
        departure(b, mine_ref if b % 2 else theirs_ref).wait()


def attention_stats(own, qseg, query, twins, others, low, high, state=()):
    count = high - low
    window = window_refs(low, high, twins, others)
    row = jax.ShapeDtypeStruct((1, BOTH), F32)
    wide = jax.ShapeDtypeStruct((HD, BOTH), F32)
    start = jax.ShapeDtypeStruct((1, ROWS), jnp.int32)
    lowest = jax.ShapeDtypeStruct((1,), jnp.int32)
    scratch = [
        pltpu.VMEM((count, PACKED, 2 * HD), BF16),
        pltpu.VMEM((HD, BOTH), BF16),
    ]
    if state:
        scratch += [pltpu.VMEM((1, BOTH), F32), pltpu.VMEM((1, BOTH), F32)]
    return pl.pallas_call(
        lambda *refs: stats_kernel(low, high, *refs),
        name="stats_far" if state else "stats_near",
        out_shape=(row, wide, start, lowest) if state else (row, row, wide, start),
        in_specs=[SMEM, VMEM, VMEM] + [VMEM] * len(state) + [ANY] * len(window),
        out_specs=(VMEM, VMEM, VMEM, SMEM if state else VMEM),
        scratch_shapes=scratch + [pltpu.SemaphoreType.DMA((count,))],
    )(own, qseg, query, *state, *window)


def attention_grads(own, stats, query, near, far, twins, others):
    lse, out, start, lowest = stats
    window = window_refs(0, BLOCKS, twins, others)
    given = (start, query, near, far, lse, out)
    return pl.pallas_call(
        grads_kernel,
        name="attention_grads",
        out_shape=(
            jax.ShapeDtypeStruct((2 * HD, ROWS), BF16),
            jax.ShapeDtypeStruct((HALF, ROWS, 2 * HD), BF16),
            jax.ShapeDtypeStruct((HALF, ROWS, 2 * HD), BF16),
        ),
        in_specs=[SMEM, SMEM] + [ANY] * (len(given) + len(window)),
        out_specs=(VMEM, ANY, ANY),
        scratch_shapes=[pltpu.VMEM(x.shape, x.dtype) for x in given]
        + [
            pltpu.VMEM((BLOCKS, PACKED, 2 * HD), BF16),
            pltpu.VMEM((HD, BOTH), BF16),
            pltpu.VMEM((BOTH, HD), BF16),
            pltpu.VMEM((BOTH, HD), BF16),
            pltpu.VMEM((HD, BOTH), BF16),
            pltpu.VMEM((1, BOTH), F32),
            pltpu.VMEM((HD, BOTH), F32),
            pltpu.VMEM((BLOCKS, ROWS, 2 * HD), BF16),
            pltpu.SemaphoreType.DMA((BLOCKS,)),
            pltpu.SemaphoreType.DMA((len(given),)),
            pltpu.SemaphoreType.DMA((BLOCKS,)),
        ],
    )(own, lowest, *given, *window)


def column_window(chunk):
    base = jnp.minimum(lax.div(chunk * FEATS, HD) * HD, D - WINDOW)
    return pl.ds(pl.multiple_of(base, HD), WINDOW), chunk * FEATS - base


def split_kernel(at_ref, w_ref, send_ref, buf, sem):
    first = at_ref[2] * (RING // 2)
    other = 1 - at_ref[1]
    copies = []
    for i in range(RING // 2):
        lanes, skip = column_window(2 * (first + i) + other)
        copy = pltpu.make_async_copy(w_ref.at[:, lanes], buf.at[i], sem.at[i])
        copy.start()
        copies.append((copy, skip))
    lane = lax.broadcasted_iota(jnp.int32, (2 * HD, CHUNK), 1)
    for i, (copy, skip) in enumerate(copies):
        copy.wait()
        moved = pltpu.roll(buf[i].astype(F32), lax.rem(WINDOW - skip, WINDOW), 1)[:, :CHUNK]
        send_ref[i] = jnp.where(lane < FEATS, moved, 0.0).astype(BF16)


def split_w_out(at, w_out):
    n = RING // 2
    return pl.pallas_call(
        split_kernel,
        name="split_w_out",
        out_shape=jax.ShapeDtypeStruct((n, 2 * HD, CHUNK), BF16),
        in_specs=[SMEM, ANY],
        out_specs=VMEM,
        scratch_shapes=[
            pltpu.VMEM((n, 2 * HD, WINDOW), BF16),
            pltpu.SemaphoreType.DMA((n,)),
        ],
    )(at, w_out)


def dout_kernel(deltas, at_ref, w_ref, pa, pb, *refs):
    shards = refs[:RING]
    near_ref, send_ref, wbuf, fbuf, gbuf, hbuf, sem = refs[RING:]
    z, xh, core = at_ref[0], at_ref[1], at_ref[2]
    copies = []
    for i in range(RING):
        chunk = lax.rem(z + deltas[i] + RING, RING)
        half = lax.div(chunk, RING // 2)
        inner = lax.rem(chunk, RING // 2)
        lanes, skip = column_window(2 * chunk + xh)
        place = pl.ds(pl.multiple_of(skip, 16), FEATS)
        far = pltpu.make_async_copy(pa.at[inner], fbuf.at[i], sem.at[i, 1])
        far_too = pltpu.make_async_copy(pb.at[inner], fbuf.at[i], sem.at[i, 1])
        pltpu.make_async_copy(w_ref.at[:, lanes], wbuf.at[i], sem.at[i, 0]).start()

        @pl.when(half == core)
        def _(copy=far):
            copy.start()

        @pl.when(half != core)
        def _(copy=far_too):
            copy.start()

        gbuf[i] = jnp.zeros((WINDOW, ROWS), BF16)
        hbuf[i, FEATS:] = jnp.zeros((CHUNK - FEATS, ROWS), BF16)
        to_far = pltpu.make_async_copy(shards[i], hbuf.at[i, :FEATS], sem.at[i, 2])
        to_far.start()
        own_rows = pltpu.make_async_copy(w_ref.at[:, lanes], wbuf.at[i], sem.at[i, 0])
        copies.append((own_rows, far, to_far, place))
    near = far = None
    for i in range(RING):
        for c in copies[i][:3]:
            c.wait()
        gbuf[i, copies[i][3], :] = hbuf[i, :FEATS]
        add_far = dot(fbuf[i], hbuf[i])
        add_near = dot(wbuf[i], gbuf[i])
        far = add_far if i == 0 else far + add_far
        near = add_near if i == 0 else near + add_near
    near_ref[...] = near
    send_ref[...] = far.astype(BF16)


def dout_parts(at, w_out, far_w, shards):
    deltas = tuple(shards)
    half = (2 * HD, ROWS)
    return pl.pallas_call(
        lambda *refs: dout_kernel(deltas, *refs),
        name="dout_parts",
        out_shape=(jax.ShapeDtypeStruct(half, F32), jax.ShapeDtypeStruct(half, BF16)),
        in_specs=[SMEM] + [ANY] * (3 + RING),
        out_specs=(VMEM, VMEM),
        scratch_shapes=[
            pltpu.VMEM((RING, 2 * HD, WINDOW), BF16),
            pltpu.VMEM((RING, 2 * HD, CHUNK), BF16),
            pltpu.VMEM((RING, WINDOW, ROWS), BF16),
            pltpu.VMEM((RING, CHUNK, ROWS), BF16),
            pltpu.SemaphoreType.DMA((RING, 3)),
        ],
    )(at, w_out, *far_w, *shards.values())


def join_kernel(core_ref, mine_ref, got_ref, own_ref, *refs):
    send_refs = refs[:HALF]
    mine, got, own, made, in_sem, out_sem = refs[HALF:]
    core = core_ref[0]
    arrivals = []
    for d in reversed(range(HALF)):
        pair = [
            pltpu.make_async_copy(x.at[d], y.at[d], in_sem.at[i, d])
            for i, (x, y) in enumerate(((got_ref, got), (mine_ref, mine)))
        ]
        for c in pair:
            c.start()
        arrivals.append(pair)
    arrivals.reverse()
    departures = []
    for d in reversed(range(HALF + 1)):
        if d > 0:
            for c in arrivals[d - 1]:
                c.wait()
        at = d - core
        inside = (at >= 0) & (at < HALF)
        total = jnp.where(inside, got[jnp.clip(at, 0, HALF - 1)].astype(F32), 0.0)
        if d < HALF:
            total = total + mine[d].astype(F32)
        if d == 0:
            own[...] = total
            departures.append(pltpu.make_async_copy(own, own_ref, out_sem.at[d]))
        else:
            made[d - 1] = total.astype(BF16)
            departures.append(
                pltpu.make_async_copy(made.at[d - 1], send_refs[d - 1], out_sem.at[d])
            )
        departures[-1].start()
    for c in departures:
        c.wait()


def join_partials(core, mine, got):
    shape = (ROWS, 2 * HD)
    result = pl.pallas_call(
        join_kernel,
        name="join_partials",
        out_shape=(jax.ShapeDtypeStruct(shape, F32),) + (jax.ShapeDtypeStruct(shape, BF16),) * HALF,
        in_specs=[SMEM, ANY, ANY],
        out_specs=(ANY,) * (HALF + 1),
        scratch_shapes=[
            pltpu.VMEM((HALF, *shape), BF16),
            pltpu.VMEM((HALF, *shape), BF16),
            pltpu.VMEM(shape, F32),
            pltpu.VMEM((HALF, *shape), BF16),
            pltpu.SemaphoreType.DMA((2, HALF)),
            pltpu.SemaphoreType.DMA((HALF + 1,)),
        ],
    )(core, mine, got)
    return result[0], result[1:]


def total_kernel(own_ref, *refs):
    part_refs, (out_ref, own, parts, sem) = refs[:HALF], refs[HALF:]
    copies = [pltpu.make_async_copy(own_ref, own, sem.at[HALF])]
    copies += [pltpu.make_async_copy(x, parts.at[i], sem.at[i]) for i, x in enumerate(part_refs)]
    for c in copies:
        c.start()
    for c in copies:
        c.wait()
    total = own[...]
    for i in range(HALF):
        total = total + parts[i].astype(F32)
    out_ref[...] = total.astype(BF16).T


def total_partials(own, parts):
    shape = (ROWS, 2 * HD)
    return pl.pallas_call(
        total_kernel,
        name="total_partials",
        out_shape=jax.ShapeDtypeStruct((2 * HD, ROWS), BF16),
        in_specs=[ANY] * (HALF + 1),
        out_specs=VMEM,
        scratch_shapes=[
            pltpu.VMEM(shape, F32),
            pltpu.VMEM((HALF, *shape), BF16),
            pltpu.SemaphoreType.DMA((HALF + 1,)),
        ],
    )(own, *parts)


def project_kernel(deltas, own_lanes, far, more, at_ref, *refs):
    n, k = len(deltas), len(own_lanes)
    weights, refs = refs[:k], refs[k:]
    pa, pb, *grads = refs[: 2 + 1 + 2 * far]
    refs = refs[3 + 2 * far :]
    sums, refs = (refs[:n], refs[n:]) if more else ((), refs)
    outs, refs = refs[:n], refs[n:]
    wbuf, gbuf, obuf, sem, g_sem, out_sem, *held = refs
    z, xh, core = at_ref[0], at_ref[1], at_ref[2]
    width = 2 * HD
    g_copies = [
        pltpu.make_async_copy(g, gbuf.at[width * i : width * (i + 1)], g_sem.at[i])
        for i, g in enumerate(grads)
    ]
    for c in g_copies:
        c.start()
    copies = []
    for i, delta in enumerate(deltas):
        chunk = lax.rem(z + delta + RING, RING)
        rows = pl.ds(pl.multiple_of((2 * chunk + xh) * FEATS, 16), FEATS)
        mine = [
            pltpu.make_async_copy(w.at[rows, :], wbuf.at[i, :, lane : lane + size], sem.at[i, j])
            for j, (w, (lane, size)) in enumerate(zip(weights, own_lanes))
        ]
        if more:
            mine.append(pltpu.make_async_copy(sums[i], held[0].at[i], sem.at[i, k + 1]))
        for c in mine:
            c.start()
        if far:
            inner = lax.rem(chunk, RING // 2)
            near_rows, far_rows = [
                pltpu.make_async_copy(p.at[inner], wbuf.at[i, :, width:], sem.at[i, k])
                for p in (pa, pb)
            ]
            same = lax.div(chunk, RING // 2) == core

            @pl.when(same)
            def _(copy=near_rows):
                copy.start()

            @pl.when(jnp.logical_not(same))
            def _(copy=far_rows):
                copy.start()

            mine.append(near_rows)
        copies.append(mine)
    for c in g_copies:
        c.wait()
    results = []
    for i in range(n):
        for c in copies[i]:
            c.wait()
        total = dot(wbuf[i], gbuf[...])
        if more:
            total = total + held[0][i]
        obuf[i] = total.astype(obuf.dtype)
        results.append(pltpu.make_async_copy(obuf.at[i], outs[i], out_sem.at[i]))
        results[-1].start()
    for c in results:
        c.wait()


def project(deltas, at, weights, own_lanes, far_rows, grads, sums, kind):
    n, k = len(deltas), len(weights)
    far = len(grads) > 1
    more = len(sums) > 0
    depth = 2 * HD * len(grads)
    return pl.pallas_call(
        lambda *refs: project_kernel(deltas, own_lanes, far, more, *refs),
        name="project",
        out_shape=(jax.ShapeDtypeStruct((FEATS, ROWS), kind),) * n,
        in_specs=[SMEM] + [ANY] * (k + 2 + len(grads) + len(sums)),
        out_specs=(ANY,) * n,
        scratch_shapes=[
            pltpu.VMEM((n, FEATS, depth), BF16),
            pltpu.VMEM((depth, ROWS), BF16),
            pltpu.VMEM((n, FEATS, ROWS), kind),
            pltpu.SemaphoreType.DMA((n, k + 2)),
            pltpu.SemaphoreType.DMA((len(grads),)),
            pltpu.SemaphoreType.DMA((n,)),
        ]
        + [pltpu.VMEM((n, FEATS, ROWS), F32)] * more,
    )(at, *weights, *far_rows, *grads, *sums)


def arrive(x):
    return pltpu.with_memory_space_constraint(x, pltpu.VMEM)


def swapped(x, axis):
    return lax.ppermute(x, axis, [(0, 1), (1, 0)])


def chip_pairs(d):
    return [(i, i + 2 * d) for i in range(lax.axis_size(AA) - 2 * d) if d < HALF or i % 2]


def chips_on(x, d):
    return lax.ppermute(x, AA, chip_pairs(d))


def chips_back(x, d):
    return arrive(lax.ppermute(x, AA, [(j, i) for i, j in chip_pairs(d)]))


def round_z(x, step):
    return lax.ppermute(x, "z", [(i, (i + step) % RING) for i in range(RING)])


def body(query, keys, values, grad_out, segment_ids, w_query, w_key, w_value, w_out):
    core = lax.axis_index("core")
    z = lax.axis_index("z")
    xh = lax.axis_index("xh")
    own = lax.axis_index(AA)[None]
    at = jnp.stack((z, xh, core))
    shards = {0: grad_out.T}
    for k in range(1, RING // 2 + 1):
        shards[-k] = round_z(shards[1 - k], 1)
        if k < RING // 2:
            shards[k] = round_z(shards[k - 1], -1)
    send_w = split_w_out(at, w_out)
    far_w = swapped(send_w, "xh")
    far_w = (far_w, swapped(far_w, "core"))
    ids = jnp.pad(
        segment_ids.astype(BF16).reshape(ROWS // HD, HD),
        ((0, SEG_ROWS - ROWS // HD), (0, HD)),
    )
    block = jnp.concatenate((jnp.concatenate((keys, values), axis=1), ids), axis=0)
    twins = [block] + [chips_on(block, d) for d in range(1, HALF + 1)]
    others = [swapped(twins[d], "core") for d in range(HALF + 1)]
    wanted = [
        lax.dynamic_index_in_dim(
            w.reshape(2, RING // 2, 2, FEATS, -1), core, 0, keepdims=False
        )
        for w in (w_query, w_key, w_value)
    ]
    wanted = [lax.dynamic_index_in_dim(w, 1 - xh, 1, keepdims=False) for w in wanted]
    wanted = jnp.concatenate(wanted, axis=2)
    far_mine = swapped(wanted, "xh")
    far_other = swapped(far_mine, "core")

    qseg = segment_ids[None, :]
    state = attention_stats(own, qseg, query, twins, others, NEAR, BLOCKS)
    near, send = dout_parts(at, w_out, far_w, shards)
    far = arrive(swapped(send, "xh"))
    stats = attention_stats(own, qseg, query, twins, others, 0, NEAR, state)
    gqt, mine, theirs = attention_grads(own, stats, query, near, far, twins, others)
    got = arrive(swapped(theirs, "core"))
    gqt_far = arrive(swapped(gqt, "xh"))
    own_total, sends = join_partials(core[None], mine, got)
    parts = [chips_back(sends[d - 1], d) for d in range(HALF, 0, -1)]
    gkvt = total_partials(own_total, parts)
    gkvt_far = arrive(swapped(gkvt, "xh"))

    deltas = (4, -3, 3, -2, 2, -1, 1, 0)
    q_lanes = ((0, 2 * HD),)
    unread = (w_query, w_query)
    sums = project(deltas, at, (w_query,), q_lanes, unread, (gqt,), (), F32)
    kv = (w_key, w_value)
    kv_lanes = ((0, HD), (HD, HD))
    args = (at, kv, kv_lanes, (far_mine, far_other), (gkvt, gqt_far, gkvt_far))
    ahead, behind = project(deltas[:2], *args, sums[:2], BF16)
    rest = project(deltas[2:4], *args, sums[2:4], F32)
    rest += project(deltas[4:], *args, sums[4:], F32)
    ahead = round_z(ahead, 1)
    behind = round_z(behind, -1)
    for k in (2, 3):
        add_ahead, add_behind = rest[2 * k - 4], rest[2 * k - 3]
        ahead = round_z((ahead.astype(F32) + add_ahead).astype(BF16), 1)
        behind = round_z((behind.astype(F32) + add_behind).astype(BF16), -1)
    ahead = round_z((ahead.astype(F32) + rest[4]).astype(BF16), 1)
    result = (ahead.astype(F32) + behind.astype(F32) + rest[5]).astype(BF16)
    return result.T


def solution(mesh):
    finer = Mesh(mesh.devices.reshape(2, 4, 2, RING, 2), AA + BA)
    return jax.shard_map(
        body,
        mesh=finer,
        in_specs=(
            P(AA, BA),
            P(AA, BA),
            P(AA, BA),
            P(AA, BA),
            P(AA),
            P(None, BA),
            P(None, BA),
            P(None, BA),
            P(BA, None),
        ),
        out_specs=P(AA, BA),
        check_vma=False,
    )
```

```python
import math

import jax
import jax.numpy as jnp
from jax import lax
from jax.experimental import pallas as pl
from jax.experimental.pallas import tpu as pltpu
from jax.sharding import Mesh
from jax.sharding import PartitionSpec as P


D = 5376
HQ = 32
HD = 128
DOCS = 6
ROWS = 384
HALF = 5
BLOCKS = 2 * HALF
SEG_ROWS = 16
PACKED = ROWS + SEG_ROWS
FEATS = 336
CHUNK = 384
WINDOW = 512
BOTH = 2 * ROWS
TILE = 256
STATS_TILE = 128
NEAR = 6
RING = 8
AA = ("xl", "y", "core")
BA = ("z", "xh")
NEG_FILL = -1e30
SCALE = (D / HQ) ** (-0.5)
SCALE2 = SCALE * math.log2(math.e)
F32 = jnp.float32
BF16 = jnp.bfloat16
VMEM = pl.BlockSpec(memory_space=pltpu.VMEM)
SMEM = pl.BlockSpec(memory_space=pltpu.SMEM)
ANY = pl.BlockSpec(memory_space=pl.ANY)


def dot(a, b):
    return lax.dot_general(a, b, (((1,), (0,)), ((), ())), preferred_element_type=F32)


def sources(low, high):
    odd = [d for d in range(HALF) if low <= BLOCKS - 1 - 2 * d < high]
    even = [k for k in range(HALF) if low <= BLOCKS - 2 - 2 * k < high]
    return odd, even, sorted({k for e in even for k in (e, e + 1)})


def load_window(low, high, core, kv_refs, buf, sem):
    odd, even, extra = sources(low, high)
    twin = dict(zip(odd, kv_refs))
    other = dict(zip(extra, kv_refs[len(odd) :]))
    copies = []
    for d in odd:
        at = BLOCKS - 1 - 2 * d - low
        copies.append(pltpu.make_async_copy(twin[d], buf.at[at], sem.at[at]))
        copies[-1].start()
    for k in even:
        at = BLOCKS - 2 - 2 * k - low
        from_low = pltpu.make_async_copy(other[k], buf.at[at], sem.at[at])
        from_high = pltpu.make_async_copy(other[k + 1], buf.at[at], sem.at[at])

        @pl.when(core == 1)
        def _(copy=from_low):
            copy.start()

        @pl.when(core == 0)
        def _(copy=from_high):
            copy.start()

        copies.append(from_low)
    return copies


def window_refs(low, high, twins, others):
    odd, _, extra = sources(low, high)
    return [twins[d] for d in odd] + [others[k] for k in extra]


def side_by_side(x):
    return jnp.concatenate((x[:HD, :], x[HD:, :]), axis=1)


def one_above_other(x):
    return jnp.concatenate((x[:, :HD], x[:, HD:]), axis=0)


def tiles(width):
    return [slice(t, t + width) for t in range(0, BOTH, width)]


def stats_kernel(low, high, own_ref, qseg_ref, q_ref, *refs):
    near = high == BLOCKS
    odd, _, extra = sources(low, high)
    count = len(odd) + len(extra)
    if near:
        kv_refs = refs[:count]
        m_ref, l_ref, out_ref, start_ref, buf, qt_ref, sem = refs[count:]
    else:
        m_in, l_in, out_in, start_in = refs[:4]
        kv_refs = refs[4 : 4 + count]
        lse_ref, out_ref, start_ref, low_ref, buf, qt_ref, m_ref, l_ref, sem = refs[4 + count :]
    own = own_ref[0]
    copies = load_window(low, high, lax.rem(own, 2), kv_refs, buf, sem)
    qt_ref[...] = one_above_other(q_ref[...]).T
    if near:
        m_ref[...] = jnp.full(m_ref.shape, NEG_FILL, F32)
        l_ref[...] = jnp.zeros(l_ref.shape, F32)
        out_ref[...] = jnp.zeros(out_ref.shape, F32)
    else:
        m_ref[...] = m_in[...]
        l_ref[...] = l_in[...]
        out_ref[...] = out_in[...]
    seg = qseg_ref[...]
    seg0 = jnp.min(seg, axis=1, keepdims=True)
    for c in copies:
        c.wait()
    before = jnp.zeros((SEG_ROWS, HD), jnp.int32)
    line = lax.broadcasted_iota(jnp.int32, (SEG_ROWS, HD), 0)
    for b in range(low, min(high, BLOCKS - 1)):
        ids = buf[b - low, ROWS:, :HD].astype(F32).astype(jnp.int32)
        hit = (line < ROWS // HD) & (ids < seg0) & (own + b >= BLOCKS - 1)
        before = before + hit.astype(jnp.int32)
    start0 = jnp.sum(before) + jnp.maximum(own + low - (BLOCKS - 1), 0) * ROWS
    first_next = (own + high - (BLOCKS - 1)) * ROWS
    start = jnp.zeros((1, ROWS), jnp.int32) + start0
    if near:
        for s in range(1, DOCS):
            here = own * ROWS + jnp.sum((seg < s).astype(jnp.int32), axis=1, keepdims=True)
            start = jnp.where((seg == s) & (seg > seg0), here, start)
        start_ref[...] = start
    else:
        start = jnp.where((seg == seg0) & (start0 < first_next), start, start_in[...])
        start_ref[...] = start
        start0 = jnp.min(start)
    lowest = lax.div(start0, ROWS) - own + (BLOCKS - 1)
    latest = jnp.max(start)
    pos = own * ROWS + lax.broadcasted_iota(jnp.int32, (1, ROWS), 1)
    start = jnp.concatenate((start, start), axis=1)
    pos = jnp.concatenate((pos, pos), axis=1)
    key_at = lax.broadcasted_iota(jnp.int32, (ROWS, STATS_TILE), 0)

    def add_block(b, first, whole):
        kb = buf[b - low, :ROWS, :HD]
        vt = buf[b - low, :ROWS, HD:].T
        for t in tiles(STATS_TILE):
            s = dot(kb, qt_ref[:, t]) * SCALE2
            if not whole:
                allowed = (key_at >= start[:, t] - first) & (key_at <= pos[:, t] - first)
                s = jnp.where(allowed, s, NEG_FILL)
            m_old = m_ref[:, t]
            m_new = jnp.maximum(m_old, jnp.max(s, axis=0, keepdims=True))
            p = jnp.exp2(s - m_new)
            back = jnp.exp2(m_old - m_new)
            l_ref[:, t] = l_ref[:, t] * back + jnp.sum(p, axis=0, keepdims=True)
            m_ref[:, t] = m_new
            out_ref[:, t] = out_ref[:, t] * back + dot(vt, p.astype(BF16))

    def one_block(back_to, carry):
        b = high - 1 - back_to
        first = (own + b - (BLOCKS - 1)) * ROWS
        whole = (first >= latest) & (b < BLOCKS - 1)

        @pl.when(whole)
        def _():
            add_block(b, first, True)

        @pl.when(jnp.logical_not(whole))
        def _():
            add_block(b, first, False)

        return carry

    lax.fori_loop(0, high - jnp.clip(lowest, low, high), one_block, 0)
    if not near:
        low_ref[0] = lowest
        lse_ref[...] = m_ref[...] + jnp.log2(l_ref[...])
        out_ref[...] = out_ref[...] / l_ref[...]


def grads_kernel(own_ref, low_ref, *refs):
    given, refs = refs[:6], refs[6:]
    kv_refs, refs = refs[: BLOCKS + 1], refs[BLOCKS + 1 :]
    gqt_ref, mine_ref, theirs_ref = refs[:3]
    start_ref, q_ref, near_ref, far_ref, lse_ref, out_ref = held = refs[3:9]
    buf, qt_ref, qn_ref, dout_ref, doutt_ref, delta_ref, acc_ref, made, sem, in_sem, out_sem = refs[9:]
    own = own_ref[0]
    arrivals = [pltpu.make_async_copy(x, y, in_sem.at[i]) for i, (x, y) in enumerate(zip(given, held))]
    for c in arrivals:
        c.start()
    load_window(0, BLOCKS, lax.rem(own, 2), kv_refs, buf, sem)
    lowest = low_ref[0]
    acc_ref[...] = jnp.zeros(acc_ref.shape, F32)
    key_at = lax.broadcasted_iota(jnp.int32, (ROWS, TILE), 0)
    for c in arrivals:
        c.wait()
    qn_ref[...] = one_above_other(q_ref[...])
    qt_ref[...] = qn_ref[...].T
    doutt_ref[...] = side_by_side((near_ref[...] + far_ref[...].astype(F32)).astype(BF16))
    dout_ref[...] = doutt_ref[...].T
    delta_ref[...] = jnp.sum(doutt_ref[...].astype(F32) * out_ref[...], axis=0, keepdims=True)
    start = start_ref[...]
    latest = jnp.max(start)
    pos = own * ROWS + lax.broadcasted_iota(jnp.int32, (1, ROWS), 1)
    start = jnp.concatenate((start, start), axis=1)
    pos = jnp.concatenate((pos, pos), axis=1)

    def add_block(b, first, whole):
        kb = buf[b, :ROWS, :HD]
        vb = buf[b, :ROWS, HD:]
        kt = kb.T
        gk = gv = None
        for t in tiles(TILE):
            s = dot(kb, qt_ref[:, t]) * SCALE2
            dp = dot(vb, doutt_ref[:, t])
            p = jnp.exp2(s - lse_ref[:, t])
            if not whole:
                allowed = (key_at >= start[:, t] - first) & (key_at <= pos[:, t] - first)
                p = jnp.where(allowed, p, 0.0)
            ds = (p * (dp - delta_ref[:, t])).astype(BF16)
            add_v = dot(p.astype(BF16), dout_ref[t, :])
            add_k = dot(ds, qn_ref[t, :])
            gv = add_v if gv is None else gv + add_v
            gk = add_k if gk is None else gk + add_k
            acc_ref[:, t] += dot(kt, ds)
        made[b, :, :HD] = (gk * SCALE).astype(BF16)
        made[b, :, HD:] = gv.astype(BF16)

    def departure(b, target):
        d = (BLOCKS - 1 - b) // 2 if isinstance(b, int) else lax.div(BLOCKS - 1 - b, 2)
        return pltpu.make_async_copy(made.at[b], target.at[d], out_sem.at[b])

    def one_block(b, carry):
        pltpu.make_async_copy(kv_refs[0], buf.at[b], sem.at[b]).wait()
        first = (own + b - (BLOCKS - 1)) * ROWS
        whole = (first >= latest) & (b < BLOCKS - 1)

        @pl.when((b >= lowest) & whole)
        def _():
            add_block(b, first, True)

        @pl.when((b >= lowest) & jnp.logical_not(whole))
        def _():
            add_block(b, first, False)

        @pl.when(b < lowest)
        def _():
            made[b] = jnp.zeros((ROWS, 2 * HD), BF16)

        odd = lax.rem(b, 2) == 1

        @pl.when(odd)
        def _():
            departure(b, mine_ref).start()

        @pl.when(jnp.logical_not(odd))
        def _():
            departure(b, theirs_ref).start()

        return carry

    lax.fori_loop(0, BLOCKS, one_block, 0)
    gqt_ref[:HD, :] = (acc_ref[:, :ROWS] * SCALE).astype(BF16)
    gqt_ref[HD:, :] = (acc_ref[:, ROWS:] * SCALE).astype(BF16)
    for b in range(BLOCKS):
        departure(b, mine_ref if b % 2 else theirs_ref).wait()


def attention_stats(own, qseg, query, twins, others, low, high, state=()):
    count = high - low
    window = window_refs(low, high, twins, others)
    row = jax.ShapeDtypeStruct((1, BOTH), F32)
    wide = jax.ShapeDtypeStruct((HD, BOTH), F32)
    start = jax.ShapeDtypeStruct((1, ROWS), jnp.int32)
    lowest = jax.ShapeDtypeStruct((1,), jnp.int32)
    scratch = [
        pltpu.VMEM((count, PACKED, 2 * HD), BF16),
        pltpu.VMEM((HD, BOTH), BF16),
    ]
    if state:
        scratch += [pltpu.VMEM((1, BOTH), F32), pltpu.VMEM((1, BOTH), F32)]
    return pl.pallas_call(
        lambda *refs: stats_kernel(low, high, *refs),
        name="stats_far" if state else "stats_near",
        out_shape=(row, wide, start, lowest) if state else (row, row, wide, start),
        in_specs=[SMEM, VMEM, VMEM] + [VMEM] * len(state) + [ANY] * len(window),
        out_specs=(VMEM, VMEM, VMEM, SMEM if state else VMEM),
        scratch_shapes=scratch + [pltpu.SemaphoreType.DMA((count,))],
    )(own, qseg, query, *state, *window)


def attention_grads(own, stats, query, near, far, twins, others):
    lse, out, start, lowest = stats
    window = window_refs(0, BLOCKS, twins, others)
    given = (start, query, near, far, lse, out)
    return pl.pallas_call(
        grads_kernel,
        name="attention_grads",
        out_shape=(
            jax.ShapeDtypeStruct((2 * HD, ROWS), BF16),
            jax.ShapeDtypeStruct((HALF, ROWS, 2 * HD), BF16),
            jax.ShapeDtypeStruct((HALF, ROWS, 2 * HD), BF16),
        ),
        in_specs=[SMEM, SMEM] + [ANY] * (len(given) + len(window)),
        out_specs=(VMEM, ANY, ANY),
        scratch_shapes=[pltpu.VMEM(x.shape, x.dtype) for x in given]
        + [
            pltpu.VMEM((BLOCKS, PACKED, 2 * HD), BF16),
            pltpu.VMEM((HD, BOTH), BF16),
            pltpu.VMEM((BOTH, HD), BF16),
            pltpu.VMEM((BOTH, HD), BF16),
            pltpu.VMEM((HD, BOTH), BF16),
            pltpu.VMEM((1, BOTH), F32),
            pltpu.VMEM((HD, BOTH), F32),
            pltpu.VMEM((BLOCKS, ROWS, 2 * HD), BF16),
            pltpu.SemaphoreType.DMA((BLOCKS,)),
            pltpu.SemaphoreType.DMA((len(given),)),
            pltpu.SemaphoreType.DMA((BLOCKS,)),
        ],
    )(own, lowest, *given, *window)


def column_window(chunk):
    base = jnp.minimum(lax.div(chunk * FEATS, HD) * HD, D - WINDOW)
    return pl.ds(pl.multiple_of(base, HD), WINDOW), chunk * FEATS - base


def split_kernel(at_ref, w_ref, send_ref, buf, sem):
    first = at_ref[2] * (RING // 2)
    other = 1 - at_ref[1]
    copies = []
    for i in range(RING // 2):
        lanes, skip = column_window(2 * (first + i) + other)
        copy = pltpu.make_async_copy(w_ref.at[:, lanes], buf.at[i], sem.at[i])
        copy.start()
        copies.append((copy, skip))
    lane = lax.broadcasted_iota(jnp.int32, (2 * HD, CHUNK), 1)
    for i, (copy, skip) in enumerate(copies):
        copy.wait()
        moved = pltpu.roll(buf[i].astype(F32), lax.rem(WINDOW - skip, WINDOW), 1)[:, :CHUNK]
        send_ref[i] = jnp.where(lane < FEATS, moved, 0.0).astype(BF16)


def split_w_out(at, w_out):
    n = RING // 2
    return pl.pallas_call(
        split_kernel,
        name="split_w_out",
        out_shape=jax.ShapeDtypeStruct((n, 2 * HD, CHUNK), BF16),
        in_specs=[SMEM, ANY],
        out_specs=VMEM,
        scratch_shapes=[
            pltpu.VMEM((n, 2 * HD, WINDOW), BF16),
            pltpu.SemaphoreType.DMA((n,)),
        ],
    )(at, w_out)


def dout_kernel(deltas, at_ref, w_ref, pa, pb, *refs):
    shards = refs[:RING]
    near_ref, send_ref, wbuf, fbuf, gbuf, hbuf, far_acc, sem = refs[RING:]
    z, xh, core = at_ref[0], at_ref[1], at_ref[2]
    for i in range(RING):
        chunk = lax.rem(z + deltas[i] + RING, RING)
        half = lax.div(chunk, RING // 2)
        inner = lax.rem(chunk, RING // 2)
        lanes, _ = column_window(2 * chunk + xh)
        far = pltpu.make_async_copy(pa.at[inner], fbuf.at[i], sem.at[i, 1])
        far_too = pltpu.make_async_copy(pb.at[inner], fbuf.at[i], sem.at[i, 1])
        pltpu.make_async_copy(w_ref.at[:, lanes], wbuf.at[i], sem.at[i, 0]).start()

        @pl.when(half == core)
        def _(copy=far):
            copy.start()

        @pl.when(half != core)
        def _(copy=far_too):
            copy.start()

        pltpu.make_async_copy(shards[i], hbuf.at[i, :FEATS], sem.at[i, 2]).start()
        hbuf[i, FEATS:] = jnp.zeros((CHUNK - FEATS, ROWS), BF16)
    near_ref[...] = jnp.zeros(near_ref.shape, F32)
    far_acc[...] = jnp.zeros(far_acc.shape, F32)

    def one_chunk(i, carry):
        pltpu.make_async_copy(w_ref.at[:, :WINDOW], wbuf.at[i], sem.at[i, 0]).wait()
        pltpu.make_async_copy(pa.at[0], fbuf.at[i], sem.at[i, 1]).wait()
        pltpu.make_async_copy(shards[0], hbuf.at[i, :FEATS], sem.at[i, 2]).wait()
        delta = jnp.where(lax.rem(i, 2) == 1, -lax.div(i + 1, 2), lax.div(i, 2))
        chunk = lax.rem(z + delta + RING, RING)
        _, skip = column_window(2 * chunk + xh)
        gbuf[...] = jnp.zeros((WINDOW, ROWS), BF16)
        gbuf[pl.ds(pl.multiple_of(skip, 16), FEATS), :] = hbuf[i, :FEATS]
        far_acc[...] += dot(fbuf[i], hbuf[i])
        near_ref[...] += dot(wbuf[i], gbuf[...])
        return carry

    lax.fori_loop(0, RING, one_chunk, 0)
    send_ref[...] = far_acc[...].astype(BF16)


def dout_parts(at, w_out, far_w, shards):
    deltas = tuple(shards)
    assert deltas == (0, -1, 1, -2, 2, -3, 3, -4)
    half = (2 * HD, ROWS)
    return pl.pallas_call(
        lambda *refs: dout_kernel(deltas, *refs),
        name="dout_parts",
        out_shape=(jax.ShapeDtypeStruct(half, F32), jax.ShapeDtypeStruct(half, BF16)),
        in_specs=[SMEM] + [ANY] * (3 + RING),
        out_specs=(VMEM, VMEM),
        scratch_shapes=[
            pltpu.VMEM((RING, 2 * HD, WINDOW), BF16),
            pltpu.VMEM((RING, 2 * HD, CHUNK), BF16),
            pltpu.VMEM((WINDOW, ROWS), BF16),
            pltpu.VMEM((RING, CHUNK, ROWS), BF16),
            pltpu.VMEM(half, F32),
            pltpu.SemaphoreType.DMA((RING, 3)),
        ],
    )(at, w_out, *far_w, *shards.values())


def join_kernel(core_ref, mine_ref, got_ref, own_ref, *send_refs):
    core = core_ref[0]
    for d in range(HALF + 1):
        at = d - core
        inside = (at >= 0) & (at < HALF)
        other = got_ref[jnp.clip(at, 0, HALF - 1)].astype(F32)
        total = jnp.where(inside, other, 0.0)
        if d < HALF:
            total = total + mine_ref[d].astype(F32)
        if d == 0:
            own_ref[...] = total
        else:
            send_refs[d - 1][...] = total.astype(BF16)


def join_partials(core, mine, got):
    shape = (ROWS, 2 * HD)
    result = pl.pallas_call(
        join_kernel,
        name="join_partials",
        out_shape=(jax.ShapeDtypeStruct(shape, F32),) + (jax.ShapeDtypeStruct(shape, BF16),) * HALF,
        in_specs=[SMEM, VMEM, VMEM],
        out_specs=(VMEM,) * (HALF + 1),
    )(core, mine, got)
    return result[0], result[1:]


def total_kernel(own_ref, *refs):
    total = own_ref[...]
    for ref in refs[:HALF]:
        total = total + ref[...].astype(F32)
    refs[HALF][...] = total.astype(BF16).T


def total_partials(own, parts):
    return pl.pallas_call(
        total_kernel,
        name="total_partials",
        out_shape=jax.ShapeDtypeStruct((2 * HD, ROWS), BF16),
        in_specs=[VMEM] * (HALF + 1),
        out_specs=VMEM,
    )(own, *parts)


def project_kernel(deltas, own_lanes, far, grad_count, more, at_ref, *refs):
    n, k = len(deltas), len(own_lanes)
    weights, refs = refs[:k], refs[k:]
    grads, refs = refs[:grad_count], refs[grad_count:]
    far_refs, refs = (refs[:4], refs[4:]) if far else ((), refs)
    sums, refs = (refs[:n], refs[n:]) if more else ((), refs)
    outs, refs = refs[:n], refs[n:]
    wbuf, gbuf, obuf, sem, g_sem, out_sem, *held = refs
    z, xh, core = at_ref[0], at_ref[1], at_ref[2]
    width = 2 * HD
    g_copies = [
        pltpu.make_async_copy(g, gbuf.at[width * i : width * (i + 1)], g_sem.at[i])
        for i, g in enumerate(grads)
    ]
    for c in g_copies:
        c.start()
    copies = []
    for i, delta in enumerate(deltas):
        chunk = lax.rem(z + delta + RING, RING)
        rows = pl.ds(pl.multiple_of((2 * chunk + xh) * FEATS, 16), FEATS)
        mine = [
            pltpu.make_async_copy(w.at[rows, :], wbuf.at[i, :, lane : lane + size], sem.at[i, j])
            for j, (w, (lane, size)) in enumerate(zip(weights, own_lanes))
        ]
        if more:
            mine.append(pltpu.make_async_copy(sums[i], held[0].at[i], sem.at[i, k + 1]))
        for c in mine:
            c.start()
        if far:
            first, size, lane = far
            part = lax.div(lax.rem(chunk, RING // 2), 2)
            other = lax.div(chunk, RING // 2) != core
            source = 2 * other.astype(jnp.int32) + part
            for j, ref in enumerate(far_refs):
                copy = pltpu.make_async_copy(
                    ref.at[lax.rem(chunk, 2), :, first : first + size],
                    wbuf.at[i, :, lane : lane + size],
                    sem.at[i, k],
                )

                @pl.when(source == j)
                def _(copy=copy):
                    copy.start()

            mine.append(copy)
        copies.append(mine)
    for c in g_copies:
        c.wait()
    results = []
    for i in range(n):
        for c in copies[i]:
            c.wait()
        total = dot(wbuf[i], gbuf[...])
        if more:
            total = total + held[0][i]
        obuf[i] = total.astype(obuf.dtype)
        results.append(pltpu.make_async_copy(obuf.at[i], outs[i], out_sem.at[i]))
        results[-1].start()
    for c in results:
        c.wait()


def project(deltas, at, weights, own_lanes, far, far_rows, grads, sums, kind):
    n, k = len(deltas), len(weights)
    more = len(sums) > 0
    depth = 2 * HD * len(grads)
    return pl.pallas_call(
        lambda *refs: project_kernel(deltas, own_lanes, far, len(grads), more, *refs),
        name="project",
        out_shape=(jax.ShapeDtypeStruct((FEATS, ROWS), kind),) * n,
        in_specs=[SMEM] + [ANY] * (k + len(grads) + len(far_rows) + len(sums)),
        out_specs=(ANY,) * n,
        scratch_shapes=[
            pltpu.VMEM((n, FEATS, depth), BF16),
            pltpu.VMEM((depth, ROWS), BF16),
            pltpu.VMEM((n, FEATS, ROWS), kind),
            pltpu.SemaphoreType.DMA((n, k + 2)),
            pltpu.SemaphoreType.DMA((len(grads),)),
            pltpu.SemaphoreType.DMA((n,)),
        ]
        + [pltpu.VMEM((n, FEATS, ROWS), F32)] * more,
    )(at, *weights, *grads, *far_rows, *sums)


def arrive(x):
    return pltpu.with_memory_space_constraint(x, pltpu.VMEM)


def swapped(x, axis):
    return lax.ppermute(x, axis, [(0, 1), (1, 0)])


def chip_pairs(d):
    return [(i, i + 2 * d) for i in range(lax.axis_size(AA) - 2 * d) if d < HALF or i % 2]


def chips_on(x, d):
    return lax.ppermute(x, AA, chip_pairs(d))


def chips_back(x, d):
    return lax.ppermute(x, AA, [(j, i) for i, j in chip_pairs(d)])


def round_z(x, step):
    return lax.ppermute(x, "z", [(i, (i + step) % RING) for i in range(RING)])


def body(query, keys, values, grad_out, segment_ids, w_query, w_key, w_value, w_out):
    core = lax.axis_index("core")
    z = lax.axis_index("z")
    xh = lax.axis_index("xh")
    own = lax.axis_index(AA)[None]
    at = jnp.stack((z, xh, core))
    shards = {0: grad_out.T}
    for k in range(1, RING // 2 + 1):
        shards[-k] = round_z(shards[1 - k], 1)
        if k < RING // 2:
            shards[k] = round_z(shards[k - 1], -1)
    send_w = split_w_out(at, w_out)
    far_w = swapped(send_w, "xh")
    far_w = (far_w, swapped(far_w, "core"))
    ids = jnp.pad(
        segment_ids.astype(BF16).reshape(ROWS // HD, HD),
        ((0, SEG_ROWS - ROWS // HD), (0, HD)),
    )
    block = jnp.concatenate((jnp.concatenate((keys, values), axis=1), ids), axis=0)
    twins = [block] + [chips_on(block, d) for d in range(1, HALF + 1)]
    others = [swapped(twins[d], "core") for d in range(HALF + 1)]
    arrivals = []
    for half in range(2):
        wanted = [
            lax.dynamic_index_in_dim(w.reshape(2, 2, 2, 2, FEATS, -1), core, 0, keepdims=False)
            for w in (w_query, w_key, w_value)
        ]
        wanted = [
            lax.dynamic_index_in_dim(w[half], 1 - xh, 1, keepdims=False) for w in wanted
        ]
        wanted = jnp.concatenate(wanted, axis=2)
        arrivals.append(swapped(wanted, "xh"))
    far_rows = (*arrivals, *(swapped(arrivals[h], "core") for h in range(2)))

    qseg = segment_ids[None, :]
    state = attention_stats(own, qseg, query, twins, others, NEAR, BLOCKS)
    near, send = dout_parts(at, w_out, far_w, shards)
    far = arrive(swapped(send, "xh"))
    stats = attention_stats(own, qseg, query, twins, others, 0, NEAR, state)
    gqt, mine, theirs = attention_grads(own, stats, query, near, far, twins, others)
    got = arrive(swapped(theirs, "core"))
    gqt_far = arrive(swapped(gqt, "xh"))
    own_total, sends = join_partials(core[None], mine, got)
    parts = [chips_back(sends[d - 1], d) for d in range(HALF, 0, -1)]
    gkvt = total_partials(own_total, parts)
    gkvt_far = arrive(swapped(gkvt, "xh"))

    deltas = (4, -3, 3, -2, 2, -1, 1, 0)
    wide = 2 * HD
    q_lanes = ((0, wide),)
    kv_lanes = ((0, HD), (HD, HD))
    kv = (w_key, w_value)
    sums = project(deltas, at, (w_query,), q_lanes, (), (), (gqt,), (), F32)
    first = project(
        deltas[:2], at, kv, kv_lanes, (0, wide, wide), far_rows,
        (gkvt, gqt_far), sums[:2], F32,
    )
    ahead, behind = project(
        deltas[:2], at, (), (), (wide, wide, 0), far_rows,
        (gkvt_far,), first, BF16,
    )
    rest = project(
        deltas[2:], at, kv, kv_lanes, (0, 2 * wide, wide), far_rows,
        (gkvt, gqt_far, gkvt_far), sums[2:], F32,
    )
    ahead = round_z(ahead, 1)
    behind = round_z(behind, -1)
    for k in (2, 3):
        add_ahead, add_behind = rest[2 * k - 4], rest[2 * k - 3]
        ahead = round_z((ahead.astype(F32) + add_ahead).astype(BF16), 1)
        behind = round_z((behind.astype(F32) + add_behind).astype(BF16), -1)
    ahead = round_z((ahead.astype(F32) + rest[4]).astype(BF16), 1)
    result = (ahead.astype(F32) + behind.astype(F32) + rest[5]).astype(BF16)
    return result.T


def solution(mesh):
    finer = Mesh(mesh.devices.reshape(2, 4, 2, RING, 2), AA + BA)
    return jax.shard_map(
        body,
        mesh=finer,
        in_specs=(
            P(AA, BA),
            P(AA, BA),
            P(AA, BA),
            P(AA, BA),
            P(AA),
            P(None, BA),
            P(None, BA),
            P(None, BA),
            P(BA, None),
        ),
        out_specs=P(AA, BA),
        check_vma=False,
    )
```

```python
import math

import jax
import jax.numpy as jnp
from jax import lax
from jax.experimental import pallas as pl
from jax.experimental.pallas import tpu as pltpu
from jax.sharding import Mesh
from jax.sharding import PartitionSpec as P


D = 5376
HQ = 32
HD = 128
DOCS = 6
ROWS = 384
HALF = 5
BLOCKS = 2 * HALF
SEG_ROWS = 16
PACKED = ROWS + SEG_ROWS
FEATS = 336
CHUNK = 384
WINDOW = 512
BOTH = 2 * ROWS
TILE = 256
STATS_TILE = 128
NEAR = 6
RING = 8
AA = ("xl", "y", "core")
BA = ("z", "xh")
NEG_FILL = -1e30
SCALE = (D / HQ) ** (-0.5)
SCALE2 = SCALE * math.log2(math.e)
F32 = jnp.float32
BF16 = jnp.bfloat16
VMEM = pl.BlockSpec(memory_space=pltpu.VMEM)
SMEM = pl.BlockSpec(memory_space=pltpu.SMEM)
ANY = pl.BlockSpec(memory_space=pl.ANY)


def dot(a, b):
    return lax.dot_general(a, b, (((1,), (0,)), ((), ())), preferred_element_type=F32)


def sources(low, high):
    odd = [d for d in range(HALF) if low <= BLOCKS - 1 - 2 * d < high]
    even = [k for k in range(HALF) if low <= BLOCKS - 2 - 2 * k < high]
    return odd, even, sorted({k for e in even for k in (e, e + 1)})


def load_window(low, high, core, kv_refs, buf, sem):
    odd, even, extra = sources(low, high)
    twin = dict(zip(odd, kv_refs))
    other = dict(zip(extra, kv_refs[len(odd) :]))
    copies = []
    for d in odd:
        at = BLOCKS - 1 - 2 * d - low
        copies.append(pltpu.make_async_copy(twin[d], buf.at[at], sem.at[at]))
        copies[-1].start()
    for k in even:
        at = BLOCKS - 2 - 2 * k - low
        from_low = pltpu.make_async_copy(other[k], buf.at[at], sem.at[at])
        from_high = pltpu.make_async_copy(other[k + 1], buf.at[at], sem.at[at])

        @pl.when(core == 1)
        def _(copy=from_low):
            copy.start()

        @pl.when(core == 0)
        def _(copy=from_high):
            copy.start()

        copies.append(from_low)
    return copies


def window_refs(low, high, twins, others):
    odd, _, extra = sources(low, high)
    return [twins[d] for d in odd] + [others[k] for k in extra]


def side_by_side(x):
    return jnp.concatenate((x[:HD, :], x[HD:, :]), axis=1)


def one_above_other(x):
    return jnp.concatenate((x[:, :HD], x[:, HD:]), axis=0)


def tiles(width):
    return [slice(t, t + width) for t in range(0, BOTH, width)]


def stats_kernel(low, high, own_ref, qseg_ref, q_ref, *refs):
    near = high == BLOCKS
    odd, _, extra = sources(low, high)
    count = len(odd) + len(extra)
    if near:
        kv_refs = refs[:count]
        m_ref, l_ref, out_ref, start_ref, buf, qt_ref, sem = refs[count:]
    else:
        m_in, l_in, out_in, start_in = refs[:4]
        kv_refs = refs[4 : 4 + count]
        lse_ref, out_ref, start_ref, low_ref, buf, qt_ref, m_ref, l_ref, sem = refs[4 + count :]
    own = own_ref[0]
    copies = load_window(low, high, lax.rem(own, 2), kv_refs, buf, sem)
    qt_ref[...] = one_above_other(q_ref[...]).T
    if near:
        m_ref[...] = jnp.full(m_ref.shape, NEG_FILL, F32)
        l_ref[...] = jnp.zeros(l_ref.shape, F32)
        out_ref[...] = jnp.zeros(out_ref.shape, F32)
    else:
        m_ref[...] = m_in[...]
        l_ref[...] = l_in[...]
        out_ref[...] = out_in[...]
    seg = qseg_ref[...]
    seg0 = jnp.min(seg, axis=1, keepdims=True)
    for c in copies:
        c.wait()
    before = jnp.zeros((SEG_ROWS, HD), jnp.int32)
    line = lax.broadcasted_iota(jnp.int32, (SEG_ROWS, HD), 0)
    for b in range(low, min(high, BLOCKS - 1)):
        ids = buf[b - low, ROWS:, :HD].astype(F32).astype(jnp.int32)
        hit = (line < ROWS // HD) & (ids < seg0) & (own + b >= BLOCKS - 1)
        before = before + hit.astype(jnp.int32)
    start0 = jnp.sum(before) + jnp.maximum(own + low - (BLOCKS - 1), 0) * ROWS
    first_next = (own + high - (BLOCKS - 1)) * ROWS
    start = jnp.zeros((1, ROWS), jnp.int32) + start0
    if near:
        for s in range(1, DOCS):
            here = own * ROWS + jnp.sum((seg < s).astype(jnp.int32), axis=1, keepdims=True)
            start = jnp.where((seg == s) & (seg > seg0), here, start)
        start_ref[...] = start
    else:
        start = jnp.where((seg == seg0) & (start0 < first_next), start, start_in[...])
        start_ref[...] = start
        start0 = jnp.min(start)
    lowest = lax.div(start0, ROWS) - own + (BLOCKS - 1)
    latest = jnp.max(start)
    pos = own * ROWS + lax.broadcasted_iota(jnp.int32, (1, ROWS), 1)
    start = jnp.concatenate((start, start), axis=1)
    pos = jnp.concatenate((pos, pos), axis=1)
    key_at = lax.broadcasted_iota(jnp.int32, (ROWS, STATS_TILE), 0)

    def add_block(b, first, whole):
        kb = buf[b - low, :ROWS, :HD]
        vt = buf[b - low, :ROWS, HD:].T
        for t in tiles(STATS_TILE):
            s = dot(kb, qt_ref[:, t]) * SCALE2
            if not whole:
                allowed = (key_at >= start[:, t] - first) & (key_at <= pos[:, t] - first)
                s = jnp.where(allowed, s, NEG_FILL)
            m_old = m_ref[:, t]
            m_new = jnp.maximum(m_old, jnp.max(s, axis=0, keepdims=True))
            p = jnp.exp2(s - m_new)
            back = jnp.exp2(m_old - m_new)
            l_ref[:, t] = l_ref[:, t] * back + jnp.sum(p, axis=0, keepdims=True)
            m_ref[:, t] = m_new
            out_ref[:, t] = out_ref[:, t] * back + dot(vt, p.astype(BF16))

    def one_block(back_to, carry):
        b = high - 1 - back_to
        first = (own + b - (BLOCKS - 1)) * ROWS
        whole = (first >= latest) & (b < BLOCKS - 1)

        @pl.when(whole)
        def _():
            add_block(b, first, True)

        @pl.when(jnp.logical_not(whole))
        def _():
            add_block(b, first, False)

        return carry

    lax.fori_loop(0, high - jnp.clip(lowest, low, high), one_block, 0)
    if not near:
        low_ref[0] = lowest
        lse_ref[...] = m_ref[...] + jnp.log2(l_ref[...])
        out_ref[...] = out_ref[...] / l_ref[...]


def grads_kernel(own_ref, low_ref, *refs):
    given, refs = refs[:6], refs[6:]
    kv_refs, refs = refs[: BLOCKS + 1], refs[BLOCKS + 1 :]
    gqt_ref, mine_ref, theirs_ref = refs[:3]
    start_ref, q_ref, near_ref, far_ref, lse_ref, out_ref = held = refs[3:9]
    buf, qt_ref, qn_ref, dout_ref, doutt_ref, delta_ref, acc_ref, made, sem, in_sem, out_sem = refs[9:]
    own = own_ref[0]
    arrivals = [pltpu.make_async_copy(x, y, in_sem.at[i]) for i, (x, y) in enumerate(zip(given, held))]
    for c in arrivals:
        c.start()
    load_window(0, BLOCKS, lax.rem(own, 2), kv_refs, buf, sem)
    lowest = low_ref[0]
    acc_ref[...] = jnp.zeros(acc_ref.shape, F32)
    key_at = lax.broadcasted_iota(jnp.int32, (ROWS, TILE), 0)
    for c in arrivals:
        c.wait()
    qn_ref[...] = one_above_other(q_ref[...])
    qt_ref[...] = qn_ref[...].T
    doutt_ref[...] = side_by_side((near_ref[...] + far_ref[...].astype(F32)).astype(BF16))
    dout_ref[...] = doutt_ref[...].T
    delta_ref[...] = jnp.sum(doutt_ref[...].astype(F32) * out_ref[...], axis=0, keepdims=True)
    start = start_ref[...]
    latest = jnp.max(start)
    pos = own * ROWS + lax.broadcasted_iota(jnp.int32, (1, ROWS), 1)
    start = jnp.concatenate((start, start), axis=1)
    pos = jnp.concatenate((pos, pos), axis=1)

    def add_block(b, first, whole):
        kb = buf[b, :ROWS, :HD]
        vb = buf[b, :ROWS, HD:]
        kt = kb.T
        gk = gv = None
        for t in tiles(TILE):
            s = dot(kb, qt_ref[:, t]) * SCALE2
            dp = dot(vb, doutt_ref[:, t])
            p = jnp.exp2(s - lse_ref[:, t])
            if not whole:
                allowed = (key_at >= start[:, t] - first) & (key_at <= pos[:, t] - first)
                p = jnp.where(allowed, p, 0.0)
            ds = (p * (dp - delta_ref[:, t])).astype(BF16)
            add_v = dot(p.astype(BF16), dout_ref[t, :])
            add_k = dot(ds, qn_ref[t, :])
            gv = add_v if gv is None else gv + add_v
            gk = add_k if gk is None else gk + add_k
            acc_ref[:, t] += dot(kt, ds)
        made[b, :, :HD] = (gk * SCALE).astype(BF16)
        made[b, :, HD:] = gv.astype(BF16)

    def departure(b, target):
        d = (BLOCKS - 1 - b) // 2 if isinstance(b, int) else lax.div(BLOCKS - 1 - b, 2)
        return pltpu.make_async_copy(made.at[b], target.at[d], out_sem.at[b])

    def one_block(b, carry):
        pltpu.make_async_copy(kv_refs[0], buf.at[b], sem.at[b]).wait()
        first = (own + b - (BLOCKS - 1)) * ROWS
        whole = (first >= latest) & (b < BLOCKS - 1)

        @pl.when((b >= lowest) & whole)
        def _():
            add_block(b, first, True)

        @pl.when((b >= lowest) & jnp.logical_not(whole))
        def _():
            add_block(b, first, False)

        @pl.when(b < lowest)
        def _():
            made[b] = jnp.zeros((ROWS, 2 * HD), BF16)

        odd = lax.rem(b, 2) == 1

        @pl.when(odd)
        def _():
            departure(b, mine_ref).start()

        @pl.when(jnp.logical_not(odd))
        def _():
            departure(b, theirs_ref).start()

        return carry

    lax.fori_loop(0, BLOCKS, one_block, 0)
    gqt_ref[:HD, :] = (acc_ref[:, :ROWS] * SCALE).astype(BF16)
    gqt_ref[HD:, :] = (acc_ref[:, ROWS:] * SCALE).astype(BF16)
    for b in range(BLOCKS):
        departure(b, mine_ref if b % 2 else theirs_ref).wait()


def attention_stats(own, qseg, query, twins, others, low, high, state=()):
    count = high - low
    window = window_refs(low, high, twins, others)
    row = jax.ShapeDtypeStruct((1, BOTH), F32)
    wide = jax.ShapeDtypeStruct((HD, BOTH), F32)
    start = jax.ShapeDtypeStruct((1, ROWS), jnp.int32)
    lowest = jax.ShapeDtypeStruct((1,), jnp.int32)
    scratch = [
        pltpu.VMEM((count, PACKED, 2 * HD), BF16),
        pltpu.VMEM((HD, BOTH), BF16),
    ]
    if state:
        scratch += [pltpu.VMEM((1, BOTH), F32), pltpu.VMEM((1, BOTH), F32)]
    return pl.pallas_call(
        lambda *refs: stats_kernel(low, high, *refs),
        name="stats_far" if state else "stats_near",
        out_shape=(row, wide, start, lowest) if state else (row, row, wide, start),
        in_specs=[SMEM, VMEM, VMEM] + [VMEM] * len(state) + [ANY] * len(window),
        out_specs=(VMEM, VMEM, VMEM, SMEM if state else VMEM),
        scratch_shapes=scratch + [pltpu.SemaphoreType.DMA((count,))],
    )(own, qseg, query, *state, *window)


def attention_grads(own, stats, query, near, far, twins, others):
    lse, out, start, lowest = stats
    window = window_refs(0, BLOCKS, twins, others)
    given = (start, query, near, far, lse, out)
    return pl.pallas_call(
        grads_kernel,
        name="attention_grads",
        out_shape=(
            jax.ShapeDtypeStruct((2 * HD, ROWS), BF16),
            jax.ShapeDtypeStruct((HALF, ROWS, 2 * HD), BF16),
            jax.ShapeDtypeStruct((HALF, ROWS, 2 * HD), BF16),
        ),
        in_specs=[SMEM, SMEM] + [ANY] * (len(given) + len(window)),
        out_specs=(VMEM, ANY, ANY),
        scratch_shapes=[pltpu.VMEM(x.shape, x.dtype) for x in given]
        + [
            pltpu.VMEM((BLOCKS, PACKED, 2 * HD), BF16),
            pltpu.VMEM((HD, BOTH), BF16),
            pltpu.VMEM((BOTH, HD), BF16),
            pltpu.VMEM((BOTH, HD), BF16),
            pltpu.VMEM((HD, BOTH), BF16),
            pltpu.VMEM((1, BOTH), F32),
            pltpu.VMEM((HD, BOTH), F32),
            pltpu.VMEM((BLOCKS, ROWS, 2 * HD), BF16),
            pltpu.SemaphoreType.DMA((BLOCKS,)),
            pltpu.SemaphoreType.DMA((len(given),)),
            pltpu.SemaphoreType.DMA((BLOCKS,)),
        ],
    )(own, lowest, *given, *window)


def column_window(chunk):
    base = jnp.minimum(lax.div(chunk * FEATS, HD) * HD, D - WINDOW)
    return pl.ds(pl.multiple_of(base, HD), WINDOW), chunk * FEATS - base


def split_kernel(at_ref, w_ref, send_ref, buf, sem):
    first = at_ref[2] * (RING // 2)
    other = 1 - at_ref[1]
    copies = []
    for i in range(RING // 2):
        lanes, skip = column_window(2 * (first + i) + other)
        copy = pltpu.make_async_copy(w_ref.at[:, lanes], buf.at[i], sem.at[i])
        copy.start()
        copies.append((copy, skip))
    lane = lax.broadcasted_iota(jnp.int32, (2 * HD, CHUNK), 1)
    for i, (copy, skip) in enumerate(copies):
        copy.wait()
        moved = pltpu.roll(buf[i].astype(F32), lax.rem(WINDOW - skip, WINDOW), 1)[:, :CHUNK]
        send_ref[i] = jnp.where(lane < FEATS, moved, 0.0).astype(BF16)


def split_w_out(at, w_out):
    n = RING // 2
    return pl.pallas_call(
        split_kernel,
        name="split_w_out",
        out_shape=jax.ShapeDtypeStruct((n, 2 * HD, CHUNK), BF16),
        in_specs=[SMEM, ANY],
        out_specs=VMEM,
        scratch_shapes=[
            pltpu.VMEM((n, 2 * HD, WINDOW), BF16),
            pltpu.SemaphoreType.DMA((n,)),
        ],
    )(at, w_out)


def dout_kernel(deltas, at_ref, w_ref, pa, pb, *refs):
    shards = refs[:RING]
    near_ref, send_ref, wbuf, fbuf, gbuf, hbuf, far_acc, sem = refs[RING:]
    z, xh, core = at_ref[0], at_ref[1], at_ref[2]
    for i in range(RING):
        chunk = lax.rem(z + deltas[i] + RING, RING)
        half = lax.div(chunk, RING // 2)
        inner = lax.rem(chunk, RING // 2)
        lanes, _ = column_window(2 * chunk + xh)
        far = pltpu.make_async_copy(pa.at[inner], fbuf.at[i], sem.at[i, 1])
        far_too = pltpu.make_async_copy(pb.at[inner], fbuf.at[i], sem.at[i, 1])
        pltpu.make_async_copy(w_ref.at[:, lanes], wbuf.at[i], sem.at[i, 0]).start()

        @pl.when(half == core)
        def _(copy=far):
            copy.start()

        @pl.when(half != core)
        def _(copy=far_too):
            copy.start()

        pltpu.make_async_copy(shards[i], hbuf.at[i, :FEATS], sem.at[i, 2]).start()
        hbuf[i, FEATS:] = jnp.zeros((CHUNK - FEATS, ROWS), BF16)
    near_ref[...] = jnp.zeros(near_ref.shape, F32)
    far_acc[...] = jnp.zeros(far_acc.shape, F32)

    def one_chunk(i, carry):
        pltpu.make_async_copy(w_ref.at[:, :WINDOW], wbuf.at[i], sem.at[i, 0]).wait()
        pltpu.make_async_copy(pa.at[0], fbuf.at[i], sem.at[i, 1]).wait()
        pltpu.make_async_copy(shards[0], hbuf.at[i, :FEATS], sem.at[i, 2]).wait()
        delta = jnp.where(lax.rem(i, 2) == 1, -lax.div(i + 1, 2), lax.div(i, 2))
        chunk = lax.rem(z + delta + RING, RING)
        _, skip = column_window(2 * chunk + xh)
        gbuf[...] = jnp.zeros((WINDOW, ROWS), BF16)
        gbuf[pl.ds(pl.multiple_of(skip, 16), FEATS), :] = hbuf[i, :FEATS]
        far_acc[...] += dot(fbuf[i], hbuf[i])
        near_ref[...] += dot(wbuf[i], gbuf[...])
        return carry

    lax.fori_loop(0, RING, one_chunk, 0)
    send_ref[...] = far_acc[...].astype(BF16)


def dout_parts(at, w_out, far_w, shards):
    deltas = tuple(shards)
    assert deltas == (0, -1, 1, -2, 2, -3, 3, -4)
    half = (2 * HD, ROWS)
    return pl.pallas_call(
        lambda *refs: dout_kernel(deltas, *refs),
        name="dout_parts",
        out_shape=(jax.ShapeDtypeStruct(half, F32), jax.ShapeDtypeStruct(half, BF16)),
        in_specs=[SMEM] + [ANY] * (3 + RING),
        out_specs=(VMEM, VMEM),
        scratch_shapes=[
            pltpu.VMEM((RING, 2 * HD, WINDOW), BF16),
            pltpu.VMEM((RING, 2 * HD, CHUNK), BF16),
            pltpu.VMEM((WINDOW, ROWS), BF16),
            pltpu.VMEM((RING, CHUNK, ROWS), BF16),
            pltpu.VMEM(half, F32),
            pltpu.SemaphoreType.DMA((RING, 3)),
        ],
    )(at, w_out, *far_w, *shards.values())


def join_kernel(core_ref, mine_ref, got_ref, own_ref, *send_refs):
    core = core_ref[0]
    for d in range(HALF + 1):
        at = d - core
        inside = (at >= 0) & (at < HALF)
        other = got_ref[jnp.clip(at, 0, HALF - 1)].astype(F32)
        total = jnp.where(inside, other, 0.0)
        if d < HALF:
            total = total + mine_ref[d].astype(F32)
        if d == 0:
            own_ref[...] = total
        else:
            send_refs[d - 1][...] = total.astype(BF16)


def join_partials(core, mine, got):
    shape = (ROWS, 2 * HD)
    result = pl.pallas_call(
        join_kernel,
        name="join_partials",
        out_shape=(jax.ShapeDtypeStruct(shape, F32),) + (jax.ShapeDtypeStruct(shape, BF16),) * HALF,
        in_specs=[SMEM, VMEM, VMEM],
        out_specs=(VMEM,) * (HALF + 1),
    )(core, mine, got)
    return result[0], result[1:]


def total_kernel(own_ref, *refs):
    total = own_ref[...]
    for ref in refs[:HALF]:
        total = total + ref[...].astype(F32)
    refs[HALF][...] = total.astype(BF16).T


def total_partials(own, parts):
    return pl.pallas_call(
        total_kernel,
        name="total_partials",
        out_shape=jax.ShapeDtypeStruct((2 * HD, ROWS), BF16),
        in_specs=[VMEM] * (HALF + 1),
        out_specs=VMEM,
    )(own, *parts)


def project_kernel(deltas, own_lanes, far, grad_count, more, at_ref, *refs):
    n, k = len(deltas), len(own_lanes)
    weights, refs = refs[:k], refs[k:]
    grads, refs = refs[:grad_count], refs[grad_count:]
    far_refs, refs = (refs[:4], refs[4:]) if far else ((), refs)
    sums, refs = (refs[:n], refs[n:]) if more else ((), refs)
    outs, refs = refs[:n], refs[n:]
    wbuf, gbuf, obuf, sem, g_sem, out_sem, *held = refs
    z, xh, core = at_ref[0], at_ref[1], at_ref[2]
    width = 2 * HD
    g_copies = [
        pltpu.make_async_copy(g, gbuf.at[width * i : width * (i + 1)], g_sem.at[i])
        for i, g in enumerate(grads)
    ]
    for c in g_copies:
        c.start()
    copies = []
    for i, delta in enumerate(deltas):
        chunk = lax.rem(z + delta + RING, RING)
        rows = pl.ds(pl.multiple_of((2 * chunk + xh) * FEATS, 16), FEATS)
        mine = [
            pltpu.make_async_copy(w.at[rows, :], wbuf.at[i, :, lane : lane + size], sem.at[i, j])
            for j, (w, (lane, size)) in enumerate(zip(weights, own_lanes))
        ]
        if more:
            mine.append(pltpu.make_async_copy(sums[i], held[0].at[i], sem.at[i, k + 1]))
        for c in mine:
            c.start()
        if far:
            first, size, lane = far
            other_y = lax.rem(lax.div(chunk, 2), 2) != at_ref[3]
            other = lax.div(chunk, RING // 2) != core
            source = 2 * other.astype(jnp.int32) + other_y.astype(jnp.int32)
            for j, ref in enumerate(far_refs):
                copy = pltpu.make_async_copy(
                    ref.at[lax.rem(chunk, 2), :, first : first + size],
                    wbuf.at[i, :, lane : lane + size],
                    sem.at[i, k],
                )

                @pl.when(source == j)
                def _(copy=copy):
                    copy.start()

            mine.append(copy)
        copies.append(mine)
    for c in g_copies:
        c.wait()
    results = []
    for i in range(n):
        for c in copies[i]:
            c.wait()
        total = dot(wbuf[i], gbuf[...])
        if more:
            total = total + held[0][i]
        obuf[i] = total.astype(obuf.dtype)
        results.append(pltpu.make_async_copy(obuf.at[i], outs[i], out_sem.at[i]))
        results[-1].start()
    for c in results:
        c.wait()


def project(deltas, at, weights, own_lanes, far, far_rows, grads, sums, kind):
    n, k = len(deltas), len(weights)
    more = len(sums) > 0
    depth = 2 * HD * len(grads)
    return pl.pallas_call(
        lambda *refs: project_kernel(deltas, own_lanes, far, len(grads), more, *refs),
        name="project",
        out_shape=(jax.ShapeDtypeStruct((FEATS, ROWS), kind),) * n,
        in_specs=[SMEM] + [ANY] * (k + len(grads) + len(far_rows) + len(sums)),
        out_specs=(ANY,) * n,
        scratch_shapes=[
            pltpu.VMEM((n, FEATS, depth), BF16),
            pltpu.VMEM((depth, ROWS), BF16),
            pltpu.VMEM((n, FEATS, ROWS), kind),
            pltpu.SemaphoreType.DMA((n, k + 2)),
            pltpu.SemaphoreType.DMA((len(grads),)),
            pltpu.SemaphoreType.DMA((n,)),
        ]
        + [pltpu.VMEM((n, FEATS, ROWS), F32)] * more,
    )(at, *weights, *grads, *far_rows, *sums)


def arrive(x):
    return pltpu.with_memory_space_constraint(x, pltpu.VMEM)


def swapped(x, axis):
    return lax.ppermute(x, axis, [(0, 1), (1, 0)])


def next_y(x):
    return lax.ppermute(x, "y", [(0, 1), (1, 0), (2, 3), (3, 2)])


def chip_pairs(d):
    return [(i, i + 2 * d) for i in range(lax.axis_size(AA) - 2 * d) if d < HALF or i % 2]


def chips_on(x, d):
    return lax.ppermute(x, AA, chip_pairs(d))


def chips_back(x, d):
    return arrive(lax.ppermute(x, AA, [(j, i) for i, j in chip_pairs(d)]))


def round_z(x, step):
    return lax.ppermute(x, "z", [(i, (i + step) % RING) for i in range(RING)])


def body(query, keys, values, grad_out, segment_ids, w_query, w_key, w_value, w_out):
    core = lax.axis_index("core")
    z = lax.axis_index("z")
    xh = lax.axis_index("xh")
    own = lax.axis_index(AA)[None]
    pair = lax.axis_index("y") % 2
    at = jnp.stack((z, xh, core, pair))
    shards = {0: grad_out.T}
    for k in range(1, RING // 2 + 1):
        shards[-k] = round_z(shards[1 - k], 1)
        if k < RING // 2:
            shards[k] = round_z(shards[k - 1], -1)
    send_w = split_w_out(at, w_out)
    far_w = swapped(send_w, "xh")
    far_w = (far_w, arrive(swapped(far_w, "core")))
    ids = jnp.pad(
        segment_ids.astype(BF16).reshape(ROWS // HD, HD),
        ((0, SEG_ROWS - ROWS // HD), (0, HD)),
    )
    block = jnp.concatenate((jnp.concatenate((keys, values), axis=1), ids), axis=0)
    twins = [block] + [chips_on(block, d) for d in range(1, HALF + 1)]
    others = [swapped(twins[d], "core") for d in range(HALF + 1)]
    wanted = []
    for w in (w_query, w_key, w_value):
        w = w.reshape(2, 2, 2, 2, FEATS, -1)
        w = lax.dynamic_index_in_dim(w, core, 0, keepdims=False)
        w = lax.dynamic_index_in_dim(w, pair, 0, keepdims=False)
        wanted.append(lax.dynamic_index_in_dim(w, 1 - xh, 1, keepdims=False))
    wanted = jnp.concatenate(wanted, axis=2)
    arrivals = [swapped(wanted, "xh")]
    arrivals.append(next_y(arrivals[0]))
    far_rows = (*arrivals, *(swapped(arrivals[h], "core") for h in range(2)))

    qseg = segment_ids[None, :]
    state = attention_stats(own, qseg, query, twins, others, NEAR, BLOCKS)
    near, send = dout_parts(at, w_out, far_w, shards)
    far = arrive(swapped(send, "xh"))
    stats = attention_stats(own, qseg, query, twins, others, 0, NEAR, state)
    gqt, mine, theirs = attention_grads(own, stats, query, near, far, twins, others)
    got = arrive(swapped(theirs, "core"))
    gqt_far = arrive(swapped(gqt, "xh"))
    own_total, sends = join_partials(core[None], mine, got)
    parts = [chips_back(sends[d - 1], d) for d in range(HALF, 0, -1)]
    gkvt = total_partials(own_total, parts)
    gkvt_far = arrive(swapped(gkvt, "xh"))

    deltas = (4, -3, 3, -2, 2, -1, 1, 0)
    wide = 2 * HD
    q_lanes = ((0, wide),)
    kv_lanes = ((0, HD), (HD, HD))
    kv = (w_key, w_value)
    sums = project(deltas, at, (w_query,), q_lanes, (), (), (gqt,), (), F32)
    first = project(
        deltas[:2], at, kv, kv_lanes, (0, wide, wide), far_rows,
        (gkvt, gqt_far), sums[:2], F32,
    )
    ahead, behind = project(
        deltas[:2], at, (), (), (wide, wide, 0), far_rows,
        (gkvt_far,), first, BF16,
    )
    rest = ()
    for some in (slice(2, 6), slice(6, 8)):
        rest += project(
            deltas[some], at, kv, kv_lanes, (0, 2 * wide, wide), far_rows,
            (gkvt, gqt_far, gkvt_far), sums[some], F32,
        )
    ahead = round_z(ahead, 1)
    behind = round_z(behind, -1)
    for k in (2, 3):
        add_ahead, add_behind = rest[2 * k - 4], rest[2 * k - 3]
        ahead = round_z((ahead.astype(F32) + add_ahead).astype(BF16), 1)
        behind = round_z((behind.astype(F32) + add_behind).astype(BF16), -1)
    ahead = round_z((ahead.astype(F32) + rest[4]).astype(BF16), 1)
    result = (ahead.astype(F32) + behind.astype(F32) + rest[5]).astype(BF16)
    return result.T


def solution(mesh):
    finer = Mesh(mesh.devices.reshape(2, 4, 2, RING, 2), AA + BA)
    return jax.shard_map(
        body,
        mesh=finer,
        in_specs=(
            P(AA, BA),
            P(AA, BA),
            P(AA, BA),
            P(AA, BA),
            P(AA),
            P(None, BA),
            P(None, BA),
            P(None, BA),
            P(BA, None),
        ),
        out_specs=P(AA, BA),
        check_vma=False,
    )
```

```python
import math

import jax
import jax.numpy as jnp
from jax import lax
from jax.experimental import pallas as pl
from jax.experimental.pallas import tpu as pltpu
from jax.sharding import Mesh
from jax.sharding import PartitionSpec as P


D = 5376
HQ = 32
HD = 128
DOCS = 6
ROWS = 384
HALF = 5
BLOCKS = 2 * HALF
SEG_ROWS = 16
PACKED = ROWS + SEG_ROWS
FEATS = 336
CHUNK = 384
WINDOW = 512
BOTH = 2 * ROWS
TILE = 256
STATS_TILE = 128
NEAR = 6
RING = 8
AA = ("xl", "y", "core")
BA = ("z", "xh")
NEG_FILL = -1e30
SCALE = (D / HQ) ** (-0.5)
SCALE2 = SCALE * math.log2(math.e)
F32 = jnp.float32
BF16 = jnp.bfloat16
VMEM = pl.BlockSpec(memory_space=pltpu.VMEM)
SMEM = pl.BlockSpec(memory_space=pltpu.SMEM)
ANY = pl.BlockSpec(memory_space=pl.ANY)


def dot(a, b):
    return lax.dot_general(a, b, (((1,), (0,)), ((), ())), preferred_element_type=F32)


def sources(low, high):
    odd = [d for d in range(HALF) if low <= BLOCKS - 1 - 2 * d < high]
    even = [k for k in range(HALF) if low <= BLOCKS - 2 - 2 * k < high]
    return odd, even, sorted({k for e in even for k in (e, e + 1)})


def load_window(low, high, core, kv_refs, buf, sem):
    odd, even, extra = sources(low, high)
    twin = dict(zip(odd, kv_refs))
    other = dict(zip(extra, kv_refs[len(odd) :]))
    copies = []
    for d in odd:
        at = BLOCKS - 1 - 2 * d - low
        copies.append(pltpu.make_async_copy(twin[d], buf.at[at], sem.at[at]))
        copies[-1].start()
    for k in even:
        at = BLOCKS - 2 - 2 * k - low
        from_low = pltpu.make_async_copy(other[k], buf.at[at], sem.at[at])
        from_high = pltpu.make_async_copy(other[k + 1], buf.at[at], sem.at[at])

        @pl.when(core == 1)
        def _(copy=from_low):
            copy.start()

        @pl.when(core == 0)
        def _(copy=from_high):
            copy.start()

        copies.append(from_low)
    return copies


def window_refs(low, high, twins, others):
    odd, _, extra = sources(low, high)
    return [twins[d] for d in odd] + [others[k] for k in extra]


def side_by_side(x):
    return jnp.concatenate((x[:HD, :], x[HD:, :]), axis=1)


def one_above_other(x):
    return jnp.concatenate((x[:, :HD], x[:, HD:]), axis=0)


def tiles(width):
    return [slice(t, t + width) for t in range(0, BOTH, width)]


def stats_kernel(low, high, own_ref, qseg_ref, q_ref, *refs):
    near = high == BLOCKS
    odd, _, extra = sources(low, high)
    count = len(odd) + len(extra)
    if near:
        kv_refs = refs[:count]
        m_ref, l_ref, out_ref, start_ref, buf, qt_ref, sem = refs[count:]
    else:
        m_in, l_in, out_in, start_in = refs[:4]
        kv_refs = refs[4 : 4 + count]
        lse_ref, out_ref, start_ref, low_ref, buf, qt_ref, m_ref, l_ref, sem = refs[4 + count :]
    own = own_ref[0]
    copies = load_window(low, high, lax.rem(own, 2), kv_refs, buf, sem)
    qt_ref[...] = one_above_other(q_ref[...]).T
    if near:
        m_ref[...] = jnp.full(m_ref.shape, NEG_FILL, F32)
        l_ref[...] = jnp.zeros(l_ref.shape, F32)
        out_ref[...] = jnp.zeros(out_ref.shape, F32)
    else:
        m_ref[...] = m_in[...]
        l_ref[...] = l_in[...]
        out_ref[...] = out_in[...]
    seg = qseg_ref[...]
    seg0 = jnp.min(seg, axis=1, keepdims=True)
    for c in copies:
        c.wait()
    before = jnp.zeros((SEG_ROWS, HD), jnp.int32)
    line = lax.broadcasted_iota(jnp.int32, (SEG_ROWS, HD), 0)
    for b in range(low, min(high, BLOCKS - 1)):
        ids = buf[b - low, ROWS:, :HD].astype(F32).astype(jnp.int32)
        hit = (line < ROWS // HD) & (ids < seg0) & (own + b >= BLOCKS - 1)
        before = before + hit.astype(jnp.int32)
    start0 = jnp.sum(before) + jnp.maximum(own + low - (BLOCKS - 1), 0) * ROWS
    first_next = (own + high - (BLOCKS - 1)) * ROWS
    start = jnp.zeros((1, ROWS), jnp.int32) + start0
    if near:
        for s in range(1, DOCS):
            here = own * ROWS + jnp.sum((seg < s).astype(jnp.int32), axis=1, keepdims=True)
            start = jnp.where((seg == s) & (seg > seg0), here, start)
        start_ref[...] = start
    else:
        start = jnp.where((seg == seg0) & (start0 < first_next), start, start_in[...])
        start_ref[...] = start
        start0 = jnp.min(start)
    lowest = lax.div(start0, ROWS) - own + (BLOCKS - 1)
    latest = jnp.max(start)
    pos = own * ROWS + lax.broadcasted_iota(jnp.int32, (1, ROWS), 1)
    start = jnp.concatenate((start, start), axis=1)
    pos = jnp.concatenate((pos, pos), axis=1)
    key_at = lax.broadcasted_iota(jnp.int32, (ROWS, STATS_TILE), 0)

    def add_block(b, first, whole):
        kb = buf[b - low, :ROWS, :HD]
        vt = buf[b - low, :ROWS, HD:].T
        for t in tiles(STATS_TILE):
            s = dot(kb, qt_ref[:, t]) * SCALE2
            if not whole:
                allowed = (key_at >= start[:, t] - first) & (key_at <= pos[:, t] - first)
                s = jnp.where(allowed, s, NEG_FILL)
            m_old = m_ref[:, t]
            m_new = jnp.maximum(m_old, jnp.max(s, axis=0, keepdims=True))
            p = jnp.exp2(s - m_new)
            back = jnp.exp2(m_old - m_new)
            l_ref[:, t] = l_ref[:, t] * back + jnp.sum(p, axis=0, keepdims=True)
            m_ref[:, t] = m_new
            out_ref[:, t] = out_ref[:, t] * back + dot(vt, p.astype(BF16))

    def one_block(back_to, carry):
        b = high - 1 - back_to
        first = (own + b - (BLOCKS - 1)) * ROWS
        whole = (first >= latest) & (b < BLOCKS - 1)

        @pl.when(whole)
        def _():
            add_block(b, first, True)

        @pl.when(jnp.logical_not(whole))
        def _():
            add_block(b, first, False)

        return carry

    lax.fori_loop(0, high - jnp.clip(lowest, low, high), one_block, 0)
    if not near:
        low_ref[0] = lowest
        lse_ref[...] = m_ref[...] + jnp.log2(l_ref[...])
        out_ref[...] = out_ref[...] / l_ref[...]


def grads_kernel(own_ref, low_ref, *refs):
    given, refs = refs[:6], refs[6:]
    kv_refs, refs = refs[: BLOCKS + 1], refs[BLOCKS + 1 :]
    gqt_ref, mine_ref, theirs_ref = refs[:3]
    start_ref, q_ref, near_ref, far_ref, lse_ref, out_ref = held = refs[3:9]
    buf, qt_ref, qn_ref, dout_ref, doutt_ref, delta_ref, acc_ref, made, sem, in_sem, out_sem = refs[9:]
    own = own_ref[0]
    arrivals = [pltpu.make_async_copy(x, y, in_sem.at[i]) for i, (x, y) in enumerate(zip(given, held))]
    for c in arrivals:
        c.start()
    load_window(0, BLOCKS, lax.rem(own, 2), kv_refs, buf, sem)
    lowest = low_ref[0]
    acc_ref[...] = jnp.zeros(acc_ref.shape, F32)
    key_at = lax.broadcasted_iota(jnp.int32, (ROWS, TILE), 0)
    for c in arrivals:
        c.wait()
    qn_ref[...] = one_above_other(q_ref[...])
    qt_ref[...] = qn_ref[...].T
    doutt_ref[...] = side_by_side((near_ref[...] + far_ref[...].astype(F32)).astype(BF16))
    dout_ref[...] = doutt_ref[...].T
    delta_ref[...] = jnp.sum(doutt_ref[...].astype(F32) * out_ref[...], axis=0, keepdims=True)
    start = start_ref[...]
    latest = jnp.max(start)
    pos = own * ROWS + lax.broadcasted_iota(jnp.int32, (1, ROWS), 1)
    start = jnp.concatenate((start, start), axis=1)
    pos = jnp.concatenate((pos, pos), axis=1)

    def add_block(b, first, whole):
        kb = buf[b, :ROWS, :HD]
        vb = buf[b, :ROWS, HD:]
        kt = kb.T
        gk = gv = None
        for t in tiles(TILE):
            s = dot(kb, qt_ref[:, t]) * SCALE2
            dp = dot(vb, doutt_ref[:, t])
            p = jnp.exp2(s - lse_ref[:, t])
            if not whole:
                allowed = (key_at >= start[:, t] - first) & (key_at <= pos[:, t] - first)
                p = jnp.where(allowed, p, 0.0)
            ds = (p * (dp - delta_ref[:, t])).astype(BF16)
            add_v = dot(p.astype(BF16), dout_ref[t, :])
            add_k = dot(ds, qn_ref[t, :])
            gv = add_v if gv is None else gv + add_v
            gk = add_k if gk is None else gk + add_k
            acc_ref[:, t] += dot(kt, ds)
        made[b, :, :HD] = (gk * SCALE).astype(BF16)
        made[b, :, HD:] = gv.astype(BF16)

    def departure(b, target):
        d = (BLOCKS - 1 - b) // 2 if isinstance(b, int) else lax.div(BLOCKS - 1 - b, 2)
        return pltpu.make_async_copy(made.at[b], target.at[d], out_sem.at[b])

    def one_block(b, carry):
        pltpu.make_async_copy(kv_refs[0], buf.at[b], sem.at[b]).wait()
        first = (own + b - (BLOCKS - 1)) * ROWS
        whole = (first >= latest) & (b < BLOCKS - 1)

        @pl.when((b >= lowest) & whole)
        def _():
            add_block(b, first, True)

        @pl.when((b >= lowest) & jnp.logical_not(whole))
        def _():
            add_block(b, first, False)

        @pl.when(b < lowest)
        def _():
            made[b] = jnp.zeros((ROWS, 2 * HD), BF16)

        odd = lax.rem(b, 2) == 1

        @pl.when(odd)
        def _():
            departure(b, mine_ref).start()

        @pl.when(jnp.logical_not(odd))
        def _():
            departure(b, theirs_ref).start()

        return carry

    lax.fori_loop(0, BLOCKS, one_block, 0)
    gqt_ref[:HD, :] = (acc_ref[:, :ROWS] * SCALE).astype(BF16)
    gqt_ref[HD:, :] = (acc_ref[:, ROWS:] * SCALE).astype(BF16)
    for b in range(BLOCKS):
        departure(b, mine_ref if b % 2 else theirs_ref).wait()


def attention_stats(own, qseg, query, twins, others, low, high, state=()):
    count = high - low
    window = window_refs(low, high, twins, others)
    row = jax.ShapeDtypeStruct((1, BOTH), F32)
    wide = jax.ShapeDtypeStruct((HD, BOTH), F32)
    start = jax.ShapeDtypeStruct((1, ROWS), jnp.int32)
    lowest = jax.ShapeDtypeStruct((1,), jnp.int32)
    scratch = [
        pltpu.VMEM((count, PACKED, 2 * HD), BF16),
        pltpu.VMEM((HD, BOTH), BF16),
    ]
    if state:
        scratch += [pltpu.VMEM((1, BOTH), F32), pltpu.VMEM((1, BOTH), F32)]
    return pl.pallas_call(
        lambda *refs: stats_kernel(low, high, *refs),
        name="stats_far" if state else "stats_near",
        out_shape=(row, wide, start, lowest) if state else (row, row, wide, start),
        in_specs=[SMEM, VMEM, VMEM] + [VMEM] * len(state) + [ANY] * len(window),
        out_specs=(VMEM, VMEM, VMEM, SMEM if state else VMEM),
        scratch_shapes=scratch + [pltpu.SemaphoreType.DMA((count,))],
    )(own, qseg, query, *state, *window)


def attention_grads(own, stats, query, near, far, twins, others):
    lse, out, start, lowest = stats
    window = window_refs(0, BLOCKS, twins, others)
    given = (start, query, near, far, lse, out)
    return pl.pallas_call(
        grads_kernel,
        name="attention_grads",
        out_shape=(
            jax.ShapeDtypeStruct((2 * HD, ROWS), BF16),
            jax.ShapeDtypeStruct((HALF, ROWS, 2 * HD), BF16),
            jax.ShapeDtypeStruct((HALF, ROWS, 2 * HD), BF16),
        ),
        in_specs=[SMEM, SMEM] + [ANY] * (len(given) + len(window)),
        out_specs=(VMEM, ANY, ANY),
        scratch_shapes=[pltpu.VMEM(x.shape, x.dtype) for x in given]
        + [
            pltpu.VMEM((BLOCKS, PACKED, 2 * HD), BF16),
            pltpu.VMEM((HD, BOTH), BF16),
            pltpu.VMEM((BOTH, HD), BF16),
            pltpu.VMEM((BOTH, HD), BF16),
            pltpu.VMEM((HD, BOTH), BF16),
            pltpu.VMEM((1, BOTH), F32),
            pltpu.VMEM((HD, BOTH), F32),
            pltpu.VMEM((BLOCKS, ROWS, 2 * HD), BF16),
            pltpu.SemaphoreType.DMA((BLOCKS,)),
            pltpu.SemaphoreType.DMA((len(given),)),
            pltpu.SemaphoreType.DMA((BLOCKS,)),
        ],
    )(own, lowest, *given, *window)


def column_window(chunk):
    base = jnp.minimum(lax.div(chunk * FEATS, HD) * HD, D - WINDOW)
    return pl.ds(pl.multiple_of(base, HD), WINDOW), chunk * FEATS - base


def split_kernel(at_ref, w_ref, send_ref, buf, sem):
    first = at_ref[2] * (RING // 2)
    other = 1 - at_ref[1]
    copies = []
    for i in range(RING // 2):
        lanes, skip = column_window(2 * (first + i) + other)
        copy = pltpu.make_async_copy(w_ref.at[:, lanes], buf.at[i], sem.at[i])
        copy.start()
        copies.append((copy, skip))
    lane = lax.broadcasted_iota(jnp.int32, (2 * HD, CHUNK), 1)
    for i, (copy, skip) in enumerate(copies):
        copy.wait()
        moved = pltpu.roll(buf[i].astype(F32), lax.rem(WINDOW - skip, WINDOW), 1)[:, :CHUNK]
        send_ref[i] = jnp.where(lane < FEATS, moved, 0.0).astype(BF16)


def split_w_out(at, w_out):
    n = RING // 2
    return pl.pallas_call(
        split_kernel,
        name="split_w_out",
        out_shape=jax.ShapeDtypeStruct((n, 2 * HD, CHUNK), BF16),
        in_specs=[SMEM, ANY],
        out_specs=VMEM,
        scratch_shapes=[
            pltpu.VMEM((n, 2 * HD, WINDOW), BF16),
            pltpu.SemaphoreType.DMA((n,)),
        ],
    )(at, w_out)


def dout_kernel(deltas, at_ref, w_ref, pa, pb, *refs):
    shards = refs[:RING]
    near_ref, send_ref, wbuf, fbuf, gbuf, hbuf, far_acc, sem = refs[RING:]
    z, xh, core = at_ref[0], at_ref[1], at_ref[2]
    for i in range(RING):
        chunk = lax.rem(z + deltas[i] + RING, RING)
        half = lax.div(chunk, RING // 2)
        inner = lax.rem(chunk, RING // 2)
        lanes, _ = column_window(2 * chunk + xh)
        far = pltpu.make_async_copy(pa.at[inner], fbuf.at[i], sem.at[i, 1])
        far_too = pltpu.make_async_copy(pb.at[inner], fbuf.at[i], sem.at[i, 1])
        pltpu.make_async_copy(w_ref.at[:, lanes], wbuf.at[i], sem.at[i, 0]).start()

        @pl.when(half == core)
        def _(copy=far):
            copy.start()

        @pl.when(half != core)
        def _(copy=far_too):
            copy.start()

        pltpu.make_async_copy(shards[i], hbuf.at[i, :FEATS], sem.at[i, 2]).start()
        hbuf[i, FEATS:] = jnp.zeros((CHUNK - FEATS, ROWS), BF16)
    near_ref[...] = jnp.zeros(near_ref.shape, F32)
    far_acc[...] = jnp.zeros(far_acc.shape, F32)

    def one_chunk(i, carry):
        pltpu.make_async_copy(w_ref.at[:, :WINDOW], wbuf.at[i], sem.at[i, 0]).wait()
        pltpu.make_async_copy(pa.at[0], fbuf.at[i], sem.at[i, 1]).wait()
        pltpu.make_async_copy(shards[0], hbuf.at[i, :FEATS], sem.at[i, 2]).wait()
        delta = jnp.where(lax.rem(i, 2) == 1, -lax.div(i + 1, 2), lax.div(i, 2))
        chunk = lax.rem(z + delta + RING, RING)
        _, skip = column_window(2 * chunk + xh)
        gbuf[...] = jnp.zeros((WINDOW, ROWS), BF16)
        gbuf[pl.ds(pl.multiple_of(skip, 16), FEATS), :] = hbuf[i, :FEATS]
        far_acc[...] += dot(fbuf[i], hbuf[i])
        near_ref[...] += dot(wbuf[i], gbuf[...])
        return carry

    lax.fori_loop(0, RING, one_chunk, 0)
    send_ref[...] = far_acc[...].astype(BF16)


def dout_parts(at, w_out, far_w, shards):
    deltas = tuple(shards)
    assert deltas == (0, -1, 1, -2, 2, -3, 3, -4)
    half = (2 * HD, ROWS)
    return pl.pallas_call(
        lambda *refs: dout_kernel(deltas, *refs),
        name="dout_parts",
        out_shape=(jax.ShapeDtypeStruct(half, F32), jax.ShapeDtypeStruct(half, BF16)),
        in_specs=[SMEM] + [ANY] * (3 + RING),
        out_specs=(VMEM, VMEM),
        scratch_shapes=[
            pltpu.VMEM((RING, 2 * HD, WINDOW), BF16),
            pltpu.VMEM((RING, 2 * HD, CHUNK), BF16),
            pltpu.VMEM((WINDOW, ROWS), BF16),
            pltpu.VMEM((RING, CHUNK, ROWS), BF16),
            pltpu.VMEM(half, F32),
            pltpu.SemaphoreType.DMA((RING, 3)),
        ],
    )(at, w_out, *far_w, *shards.values())


def join_kernel(core_ref, mine_ref, got_ref, own_ref, *send_refs):
    core = core_ref[0]
    for d in range(HALF + 1):
        at = d - core
        inside = (at >= 0) & (at < HALF)
        other = got_ref[jnp.clip(at, 0, HALF - 1)].astype(F32)
        total = jnp.where(inside, other, 0.0)
        if d < HALF:
            total = total + mine_ref[d].astype(F32)
        if d == 0:
            own_ref[...] = total
        else:
            send_refs[d - 1][...] = total.astype(BF16)


def join_partials(core, mine, got):
    shape = (ROWS, 2 * HD)
    result = pl.pallas_call(
        join_kernel,
        name="join_partials",
        out_shape=(jax.ShapeDtypeStruct(shape, F32),) + (jax.ShapeDtypeStruct(shape, BF16),) * HALF,
        in_specs=[SMEM, VMEM, VMEM],
        out_specs=(VMEM,) * (HALF + 1),
    )(core, mine, got)
    return result[0], result[1:]


def total_kernel(own_ref, *refs):
    total = own_ref[...]
    for ref in refs[:HALF]:
        total = total + ref[...].astype(F32)
    refs[HALF][...] = total.astype(BF16).T


def total_partials(own, parts):
    return pl.pallas_call(
        total_kernel,
        name="total_partials",
        out_shape=jax.ShapeDtypeStruct((2 * HD, ROWS), BF16),
        in_specs=[VMEM] * (HALF + 1),
        out_specs=VMEM,
    )(own, *parts)


def project_kernel(deltas, own_lanes, far, grad_count, more, at_ref, *refs):
    n, k = len(deltas), len(own_lanes)
    weights, refs = refs[:k], refs[k:]
    grads, refs = refs[:grad_count], refs[grad_count:]
    far_refs, refs = (refs[:RING], refs[RING:]) if far else ((), refs)
    sums, refs = (refs[:n], refs[n:]) if more else ((), refs)
    outs, refs = refs[:n], refs[n:]
    wbuf, gbuf, obuf, sem, g_sem, out_sem, *held = refs
    z, xh, core = at_ref[0], at_ref[1], at_ref[2]
    width = 2 * HD
    g_copies = [
        pltpu.make_async_copy(g, gbuf.at[width * i : width * (i + 1)], g_sem.at[i])
        for i, g in enumerate(grads)
    ]
    for c in g_copies:
        c.start()
    copies = []
    for i, delta in enumerate(deltas):
        chunk = lax.rem(z + delta + RING, RING)
        rows = pl.ds(pl.multiple_of((2 * chunk + xh) * FEATS, 16), FEATS)
        mine = [
            pltpu.make_async_copy(w.at[rows, :], wbuf.at[i, :, lane : lane + size], sem.at[i, j])
            for j, (w, (lane, size)) in enumerate(zip(weights, own_lanes))
        ]
        if more:
            mine.append(pltpu.make_async_copy(sums[i], held[0].at[i], sem.at[i, k + 1]))
        for c in mine:
            c.start()
        if far:
            first, size, lane = far
            other_y = lax.rem(lax.div(chunk, 2), 2) != at_ref[3]
            other = lax.div(chunk, RING // 2) != core
            source = 4 * other.astype(jnp.int32) + 2 * other_y.astype(jnp.int32)
            source = source + lax.rem(chunk, 2)
            for j, ref in enumerate(far_refs):
                copy = pltpu.make_async_copy(
                    ref.at[:, first : first + size],
                    wbuf.at[i, :, lane : lane + size],
                    sem.at[i, k],
                )

                @pl.when(source == j)
                def _(copy=copy):
                    copy.start()

            mine.append(copy)
        copies.append(mine)
    for c in g_copies:
        c.wait()
    results = []
    for i in range(n):
        for c in copies[i]:
            c.wait()
        total = dot(wbuf[i], gbuf[...])
        if more:
            total = total + held[0][i]
        obuf[i] = total.astype(obuf.dtype)
        results.append(pltpu.make_async_copy(obuf.at[i], outs[i], out_sem.at[i]))
        results[-1].start()
    for c in results:
        c.wait()


def project(deltas, at, weights, own_lanes, far, far_rows, grads, sums, kind):
    n, k = len(deltas), len(weights)
    more = len(sums) > 0
    depth = 2 * HD * len(grads)
    return pl.pallas_call(
        lambda *refs: project_kernel(deltas, own_lanes, far, len(grads), more, *refs),
        name="project",
        out_shape=(jax.ShapeDtypeStruct((FEATS, ROWS), kind),) * n,
        in_specs=[SMEM] + [ANY] * (k + len(grads) + len(far_rows) + len(sums)),
        out_specs=(ANY,) * n,
        scratch_shapes=[
            pltpu.VMEM((n, FEATS, depth), BF16),
            pltpu.VMEM((depth, ROWS), BF16),
            pltpu.VMEM((n, FEATS, ROWS), kind),
            pltpu.SemaphoreType.DMA((n, k + 2)),
            pltpu.SemaphoreType.DMA((len(grads),)),
            pltpu.SemaphoreType.DMA((n,)),
        ]
        + [pltpu.VMEM((n, FEATS, ROWS), F32)] * more,
    )(at, *weights, *grads, *far_rows, *sums)


def arrive(x):
    return pltpu.with_memory_space_constraint(x, pltpu.VMEM)


def swapped(x, axis):
    return lax.ppermute(x, axis, [(0, 1), (1, 0)])


def next_y(x):
    return lax.ppermute(x, "y", [(0, 1), (1, 0), (2, 3), (3, 2)])


def chip_pairs(d):
    return [(i, i + 2 * d) for i in range(lax.axis_size(AA) - 2 * d) if d < HALF or i % 2]


def chips_on(x, d):
    return lax.ppermute(x, AA, chip_pairs(d))


def chips_back(x, d):
    return arrive(lax.ppermute(x, AA, [(j, i) for i, j in chip_pairs(d)]))


def round_z(x, step):
    return lax.ppermute(x, "z", [(i, (i + step) % RING) for i in range(RING)])


def body(query, keys, values, grad_out, segment_ids, w_query, w_key, w_value, w_out):
    core = lax.axis_index("core")
    z = lax.axis_index("z")
    xh = lax.axis_index("xh")
    own = lax.axis_index(AA)[None]
    pair = lax.axis_index("y") % 2
    at = jnp.stack((z, xh, core, pair))
    shards = {0: grad_out.T}
    for k in range(1, RING // 2 + 1):
        shards[-k] = round_z(shards[1 - k], 1)
        if k < RING // 2:
            shards[k] = round_z(shards[k - 1], -1)
    send_w = split_w_out(at, w_out)
    far_w = swapped(send_w, "xh")
    far_w = (far_w, arrive(swapped(far_w, "core")))
    ids = jnp.pad(
        segment_ids.astype(BF16).reshape(ROWS // HD, HD),
        ((0, SEG_ROWS - ROWS // HD), (0, HD)),
    )
    block = jnp.concatenate((jnp.concatenate((keys, values), axis=1), ids), axis=0)
    twins = [block] + [chips_on(block, d) for d in range(1, HALF + 1)]
    others = [swapped(twins[d], "core") for d in range(HALF + 1)]
    mine, theirs = [], []
    for k in range(2):
        wanted = []
        for w in (w_query, w_key, w_value):
            w = w.reshape(2, 2, 2, 2, FEATS, -1)
            w = lax.dynamic_index_in_dim(w, core, 0, keepdims=False)
            w = lax.dynamic_index_in_dim(w, pair, 0, keepdims=False)
            wanted.append(lax.dynamic_index_in_dim(w[k], 1 - xh, 0, keepdims=False))
        wanted = jnp.concatenate(wanted, axis=1)
        mine.append(swapped(wanted, "xh"))
        theirs.append(next_y(mine[k]))
    far_rows = (*mine, *theirs)
    far_rows += tuple(swapped(x, "core") for x in far_rows)

    qseg = segment_ids[None, :]
    state = attention_stats(own, qseg, query, twins, others, NEAR, BLOCKS)
    near, send = dout_parts(at, w_out, far_w, shards)
    far = arrive(swapped(send, "xh"))
    stats = attention_stats(own, qseg, query, twins, others, 0, NEAR, state)
    gqt, mine, theirs = attention_grads(own, stats, query, near, far, twins, others)
    got = arrive(swapped(theirs, "core"))
    gqt_far = arrive(swapped(gqt, "xh"))
    own_total, sends = join_partials(core[None], mine, got)
    parts = [chips_back(sends[d - 1], d) for d in range(HALF, 0, -1)]
    gkvt = total_partials(own_total, parts)
    gkvt_far = arrive(swapped(gkvt, "xh"))

    deltas = (4, -3, 3, -2, 2, -1, 1, 0)
    wide = 2 * HD
    q_lanes = ((0, wide),)
    kv_lanes = ((0, HD), (HD, HD))
    kv = (w_key, w_value)
    sums = project(deltas, at, (w_query,), q_lanes, (), (), (gqt,), (), F32)
    first = project(
        deltas[:2], at, kv, kv_lanes, (0, wide, wide), far_rows,
        (gkvt, gqt_far), sums[:2], F32,
    )
    ahead, behind = project(
        deltas[:2], at, (), (), (wide, wide, 0), far_rows,
        (gkvt_far,), first, BF16,
    )
    rest = ()
    for some in (slice(2, 6), slice(6, 8)):
        rest += project(
            deltas[some], at, kv, kv_lanes, (0, 2 * wide, wide), far_rows,
            (gkvt, gqt_far, gkvt_far), sums[some], F32,
        )
    ahead = round_z(ahead, 1)
    behind = round_z(behind, -1)
    for k in (2, 3):
        add_ahead, add_behind = rest[2 * k - 4], rest[2 * k - 3]
        ahead = round_z((ahead.astype(F32) + add_ahead).astype(BF16), 1)
        behind = round_z((behind.astype(F32) + add_behind).astype(BF16), -1)
    ahead = round_z((ahead.astype(F32) + rest[4]).astype(BF16), 1)
    result = (ahead.astype(F32) + behind.astype(F32) + rest[5]).astype(BF16)
    return result.T


def solution(mesh):
    finer = Mesh(mesh.devices.reshape(2, 4, 2, RING, 2), AA + BA)
    return jax.shard_map(
        body,
        mesh=finer,
        in_specs=(
            P(AA, BA),
            P(AA, BA),
            P(AA, BA),
            P(AA, BA),
            P(AA),
            P(None, BA),
            P(None, BA),
            P(None, BA),
            P(BA, None),
        ),
        out_specs=P(AA, BA),
        check_vma=False,
    )
```

```python
import math

import jax
import jax.numpy as jnp
from jax import lax
from jax.experimental import pallas as pl
from jax.experimental.pallas import tpu as pltpu
from jax.sharding import Mesh
from jax.sharding import PartitionSpec as P


D = 5376
HQ = 32
HD = 128
DOCS = 6
ROWS = 384
HALF = 5
BLOCKS = 2 * HALF
SEG_ROWS = 16
PACKED = ROWS + SEG_ROWS
FEATS = 336
CHUNK = 384
WINDOW = 512
BOTH = 2 * ROWS
TILE = 256
STATS_TILE = 128
NEAR = 6
RING = 8
AA = ("xl", "y", "core")
BA = ("z", "xh")
NEG_FILL = -1e30
SCALE = (D / HQ) ** (-0.5)
SCALE2 = SCALE * math.log2(math.e)
F32 = jnp.float32
BF16 = jnp.bfloat16
VMEM = pl.BlockSpec(memory_space=pltpu.VMEM)
SMEM = pl.BlockSpec(memory_space=pltpu.SMEM)
ANY = pl.BlockSpec(memory_space=pl.ANY)


def dot(a, b):
    return lax.dot_general(a, b, (((1,), (0,)), ((), ())), preferred_element_type=F32)


def sources(low, high):
    odd = [d for d in range(HALF) if low <= BLOCKS - 1 - 2 * d < high]
    even = [k for k in range(HALF) if low <= BLOCKS - 2 - 2 * k < high]
    return odd, even, sorted({k for e in even for k in (e, e + 1)})


def load_window(low, high, core, kv_refs, buf, sem):
    odd, even, extra = sources(low, high)
    twin = dict(zip(odd, kv_refs))
    other = dict(zip(extra, kv_refs[len(odd) :]))
    copies = []
    for d in odd:
        at = BLOCKS - 1 - 2 * d - low
        copies.append(pltpu.make_async_copy(twin[d], buf.at[at], sem.at[at]))
        copies[-1].start()
    for k in even:
        at = BLOCKS - 2 - 2 * k - low
        from_low = pltpu.make_async_copy(other[k], buf.at[at], sem.at[at])
        from_high = pltpu.make_async_copy(other[k + 1], buf.at[at], sem.at[at])

        @pl.when(core == 1)
        def _(copy=from_low):
            copy.start()

        @pl.when(core == 0)
        def _(copy=from_high):
            copy.start()

        copies.append(from_low)
    return copies


def window_refs(low, high, twins, others):
    odd, _, extra = sources(low, high)
    return [twins[d] for d in odd] + [others[k] for k in extra]


def side_by_side(x):
    return jnp.concatenate((x[:HD, :], x[HD:, :]), axis=1)


def one_above_other(x):
    return jnp.concatenate((x[:, :HD], x[:, HD:]), axis=0)


def tiles(width):
    return [slice(t, t + width) for t in range(0, BOTH, width)]


def stats_kernel(low, high, own_ref, qseg_ref, q_ref, *refs):
    near = high == BLOCKS
    odd, _, extra = sources(low, high)
    count = len(odd) + len(extra)
    if near:
        kv_refs = refs[:count]
        m_ref, l_ref, out_ref, start_ref, buf, qt_ref, sem = refs[count:]
    else:
        m_in, l_in, out_in, start_in = refs[:4]
        kv_refs = refs[4 : 4 + count]
        lse_ref, out_ref, start_ref, low_ref, buf, qt_ref, m_ref, l_ref, sem = refs[4 + count :]
    own = own_ref[0]
    copies = load_window(low, high, lax.rem(own, 2), kv_refs, buf, sem)
    qt_ref[...] = one_above_other(q_ref[...]).T
    if near:
        m_ref[...] = jnp.full(m_ref.shape, NEG_FILL, F32)
        l_ref[...] = jnp.zeros(l_ref.shape, F32)
        out_ref[...] = jnp.zeros(out_ref.shape, F32)
    else:
        m_ref[...] = m_in[...]
        l_ref[...] = l_in[...]
        out_ref[...] = out_in[...]
    seg = qseg_ref[...]
    seg0 = jnp.min(seg, axis=1, keepdims=True)
    for c in copies:
        c.wait()
    before = jnp.zeros((SEG_ROWS, HD), jnp.int32)
    line = lax.broadcasted_iota(jnp.int32, (SEG_ROWS, HD), 0)
    for b in range(low, min(high, BLOCKS - 1)):
        ids = buf[b - low, ROWS:, :HD].astype(F32).astype(jnp.int32)
        hit = (line < ROWS // HD) & (ids < seg0) & (own + b >= BLOCKS - 1)
        before = before + hit.astype(jnp.int32)
    start0 = jnp.sum(before) + jnp.maximum(own + low - (BLOCKS - 1), 0) * ROWS
    first_next = (own + high - (BLOCKS - 1)) * ROWS
    start = jnp.zeros((1, ROWS), jnp.int32) + start0
    if near:
        for s in range(1, DOCS):
            here = own * ROWS + jnp.sum((seg < s).astype(jnp.int32), axis=1, keepdims=True)
            start = jnp.where((seg == s) & (seg > seg0), here, start)
        start_ref[...] = start
    else:
        start = jnp.where((seg == seg0) & (start0 < first_next), start, start_in[...])
        start_ref[...] = start
        start0 = jnp.min(start)
    lowest = lax.div(start0, ROWS) - own + (BLOCKS - 1)
    latest = jnp.max(start)
    pos = own * ROWS + lax.broadcasted_iota(jnp.int32, (1, ROWS), 1)
    start = jnp.concatenate((start, start), axis=1)
    pos = jnp.concatenate((pos, pos), axis=1)
    key_at = lax.broadcasted_iota(jnp.int32, (ROWS, STATS_TILE), 0)

    def add_block(b, first, whole):
        kb = buf[b - low, :ROWS, :HD]
        vt = buf[b - low, :ROWS, HD:].T
        for t in tiles(STATS_TILE):
            s = dot(kb, qt_ref[:, t]) * SCALE2
            if not whole:
                allowed = (key_at >= start[:, t] - first) & (key_at <= pos[:, t] - first)
                s = jnp.where(allowed, s, NEG_FILL)
            m_old = m_ref[:, t]
            m_new = jnp.maximum(m_old, jnp.max(s, axis=0, keepdims=True))
            p = jnp.exp2(s - m_new)
            back = jnp.exp2(m_old - m_new)
            l_ref[:, t] = l_ref[:, t] * back + jnp.sum(p, axis=0, keepdims=True)
            m_ref[:, t] = m_new
            out_ref[:, t] = out_ref[:, t] * back + dot(vt, p.astype(BF16))

    def one_block(back_to, carry):
        b = high - 1 - back_to
        first = (own + b - (BLOCKS - 1)) * ROWS
        whole = (first >= latest) & (b < BLOCKS - 1)

        @pl.when(whole)
        def _():
            add_block(b, first, True)

        @pl.when(jnp.logical_not(whole))
        def _():
            add_block(b, first, False)

        return carry

    lax.fori_loop(0, high - jnp.clip(lowest, low, high), one_block, 0)
    if not near:
        low_ref[0] = lowest
        lse_ref[...] = m_ref[...] + jnp.log2(l_ref[...])
        out_ref[...] = out_ref[...] / l_ref[...]


def grads_kernel(own_ref, low_ref, *refs):
    given, refs = refs[:6], refs[6:]
    kv_refs, refs = refs[: BLOCKS + 1], refs[BLOCKS + 1 :]
    gqt_ref, mine_ref, theirs_ref = refs[:3]
    start_ref, q_ref, near_ref, far_ref, lse_ref, out_ref = held = refs[3:9]
    buf, qt_ref, qn_ref, dout_ref, doutt_ref, delta_ref, acc_ref, made, sem, in_sem, out_sem = refs[9:]
    own = own_ref[0]
    arrivals = [pltpu.make_async_copy(x, y, in_sem.at[i]) for i, (x, y) in enumerate(zip(given, held))]
    for c in arrivals:
        c.start()
    load_window(0, BLOCKS, lax.rem(own, 2), kv_refs, buf, sem)
    lowest = low_ref[0]
    acc_ref[...] = jnp.zeros(acc_ref.shape, F32)
    key_at = lax.broadcasted_iota(jnp.int32, (ROWS, TILE), 0)
    for c in arrivals:
        c.wait()
    qn_ref[...] = one_above_other(q_ref[...])
    qt_ref[...] = qn_ref[...].T
    doutt_ref[...] = side_by_side((near_ref[...] + far_ref[...].astype(F32)).astype(BF16))
    dout_ref[...] = doutt_ref[...].T
    delta_ref[...] = jnp.sum(doutt_ref[...].astype(F32) * out_ref[...], axis=0, keepdims=True)
    start = start_ref[...]
    latest = jnp.max(start)
    pos = own * ROWS + lax.broadcasted_iota(jnp.int32, (1, ROWS), 1)
    start = jnp.concatenate((start, start), axis=1)
    pos = jnp.concatenate((pos, pos), axis=1)

    def add_block(b, first, whole):
        kb = buf[b, :ROWS, :HD]
        vb = buf[b, :ROWS, HD:]
        kt = kb.T
        gk = gv = None
        for t in tiles(TILE):
            s = dot(kb, qt_ref[:, t]) * SCALE2
            dp = dot(vb, doutt_ref[:, t])
            p = jnp.exp2(s - lse_ref[:, t])
            if not whole:
                allowed = (key_at >= start[:, t] - first) & (key_at <= pos[:, t] - first)
                p = jnp.where(allowed, p, 0.0)
            ds = (p * (dp - delta_ref[:, t])).astype(BF16)
            add_v = dot(p.astype(BF16), dout_ref[t, :])
            add_k = dot(ds, qn_ref[t, :])
            gv = add_v if gv is None else gv + add_v
            gk = add_k if gk is None else gk + add_k
            acc_ref[:, t] += dot(kt, ds)
        made[b, :, :HD] = (gk * SCALE).astype(BF16)
        made[b, :, HD:] = gv.astype(BF16)

    def departure(b, target):
        d = (BLOCKS - 1 - b) // 2 if isinstance(b, int) else lax.div(BLOCKS - 1 - b, 2)
        return pltpu.make_async_copy(made.at[b], target.at[d], out_sem.at[b])

    def one_block(b, carry):
        pltpu.make_async_copy(kv_refs[0], buf.at[b], sem.at[b]).wait()
        first = (own + b - (BLOCKS - 1)) * ROWS
        whole = (first >= latest) & (b < BLOCKS - 1)

        @pl.when((b >= lowest) & whole)
        def _():
            add_block(b, first, True)

        @pl.when((b >= lowest) & jnp.logical_not(whole))
        def _():
            add_block(b, first, False)

        @pl.when(b < lowest)
        def _():
            made[b] = jnp.zeros((ROWS, 2 * HD), BF16)

        odd = lax.rem(b, 2) == 1

        @pl.when(odd)
        def _():
            departure(b, mine_ref).start()

        @pl.when(jnp.logical_not(odd))
        def _():
            departure(b, theirs_ref).start()

        return carry

    lax.fori_loop(0, BLOCKS, one_block, 0)
    gqt_ref[:HD, :] = (acc_ref[:, :ROWS] * SCALE).astype(BF16)
    gqt_ref[HD:, :] = (acc_ref[:, ROWS:] * SCALE).astype(BF16)
    for b in range(BLOCKS):
        departure(b, mine_ref if b % 2 else theirs_ref).wait()


def attention_stats(own, qseg, query, twins, others, low, high, state=()):
    count = high - low
    window = window_refs(low, high, twins, others)
    row = jax.ShapeDtypeStruct((1, BOTH), F32)
    wide = jax.ShapeDtypeStruct((HD, BOTH), F32)
    start = jax.ShapeDtypeStruct((1, ROWS), jnp.int32)
    lowest = jax.ShapeDtypeStruct((1,), jnp.int32)
    scratch = [
        pltpu.VMEM((count, PACKED, 2 * HD), BF16),
        pltpu.VMEM((HD, BOTH), BF16),
    ]
    if state:
        scratch += [pltpu.VMEM((1, BOTH), F32), pltpu.VMEM((1, BOTH), F32)]
    return pl.pallas_call(
        lambda *refs: stats_kernel(low, high, *refs),
        name="stats_far" if state else "stats_near",
        out_shape=(row, wide, start, lowest) if state else (row, row, wide, start),
        in_specs=[SMEM, VMEM, VMEM] + [VMEM] * len(state) + [ANY] * len(window),
        out_specs=(VMEM, VMEM, VMEM, SMEM if state else VMEM),
        scratch_shapes=scratch + [pltpu.SemaphoreType.DMA((count,))],
    )(own, qseg, query, *state, *window)


def attention_grads(own, stats, query, near, far, twins, others):
    lse, out, start, lowest = stats
    window = window_refs(0, BLOCKS, twins, others)
    given = (start, query, near, far, lse, out)
    return pl.pallas_call(
        grads_kernel,
        name="attention_grads",
        out_shape=(
            jax.ShapeDtypeStruct((2 * HD, ROWS), BF16),
            jax.ShapeDtypeStruct((HALF, ROWS, 2 * HD), BF16),
            jax.ShapeDtypeStruct((HALF, ROWS, 2 * HD), BF16),
        ),
        in_specs=[SMEM, SMEM] + [ANY] * (len(given) + len(window)),
        out_specs=(VMEM, ANY, ANY),
        scratch_shapes=[pltpu.VMEM(x.shape, x.dtype) for x in given]
        + [
            pltpu.VMEM((BLOCKS, PACKED, 2 * HD), BF16),
            pltpu.VMEM((HD, BOTH), BF16),
            pltpu.VMEM((BOTH, HD), BF16),
            pltpu.VMEM((BOTH, HD), BF16),
            pltpu.VMEM((HD, BOTH), BF16),
            pltpu.VMEM((1, BOTH), F32),
            pltpu.VMEM((HD, BOTH), F32),
            pltpu.VMEM((BLOCKS, ROWS, 2 * HD), BF16),
            pltpu.SemaphoreType.DMA((BLOCKS,)),
            pltpu.SemaphoreType.DMA((len(given),)),
            pltpu.SemaphoreType.DMA((BLOCKS,)),
        ],
    )(own, lowest, *given, *window)


def column_window(chunk):
    base = jnp.minimum(lax.div(chunk * FEATS, HD) * HD, D - WINDOW)
    return pl.ds(pl.multiple_of(base, HD), WINDOW), chunk * FEATS - base


def split_kernel(at_ref, w_ref, send_ref, buf, sem):
    first = at_ref[2] * (RING // 2)
    other = 1 - at_ref[1]
    copies = []
    for i in range(RING // 2):
        lanes, skip = column_window(2 * (first + i) + other)
        copy = pltpu.make_async_copy(w_ref.at[:, lanes], buf.at[i], sem.at[i])
        copy.start()
        copies.append((copy, skip))
    lane = lax.broadcasted_iota(jnp.int32, (2 * HD, CHUNK), 1)
    for i, (copy, skip) in enumerate(copies):
        copy.wait()
        moved = pltpu.roll(buf[i].astype(F32), lax.rem(WINDOW - skip, WINDOW), 1)[:, :CHUNK]
        send_ref[i] = jnp.where(lane < FEATS, moved, 0.0).astype(BF16)


def split_w_out(at, w_out):
    n = RING // 2
    return pl.pallas_call(
        split_kernel,
        name="split_w_out",
        out_shape=jax.ShapeDtypeStruct((n, 2 * HD, CHUNK), BF16),
        in_specs=[SMEM, ANY],
        out_specs=VMEM,
        scratch_shapes=[
            pltpu.VMEM((n, 2 * HD, WINDOW), BF16),
            pltpu.SemaphoreType.DMA((n,)),
        ],
    )(at, w_out)


def dout_kernel(deltas, at_ref, w_ref, pa, pb, *refs):
    shards = refs[:RING]
    near_ref, send_ref, wbuf, fbuf, gbuf, hbuf, far_acc, sem = refs[RING:]
    z, xh, core = at_ref[0], at_ref[1], at_ref[2]
    for i in range(RING):
        chunk = lax.rem(z + deltas[i] + RING, RING)
        half = lax.div(chunk, RING // 2)
        inner = lax.rem(chunk, RING // 2)
        lanes, _ = column_window(2 * chunk + xh)
        far = pltpu.make_async_copy(pa.at[inner], fbuf.at[i], sem.at[i, 1])
        far_too = pltpu.make_async_copy(pb.at[inner], fbuf.at[i], sem.at[i, 1])
        pltpu.make_async_copy(w_ref.at[:, lanes], wbuf.at[i], sem.at[i, 0]).start()

        @pl.when(half == core)
        def _(copy=far):
            copy.start()

        @pl.when(half != core)
        def _(copy=far_too):
            copy.start()

        pltpu.make_async_copy(shards[i], hbuf.at[i, :FEATS], sem.at[i, 2]).start()
        hbuf[i, FEATS:] = jnp.zeros((CHUNK - FEATS, ROWS), BF16)
    near_ref[...] = jnp.zeros(near_ref.shape, F32)
    far_acc[...] = jnp.zeros(far_acc.shape, F32)

    def one_chunk(i, carry):
        pltpu.make_async_copy(w_ref.at[:, :WINDOW], wbuf.at[i], sem.at[i, 0]).wait()
        pltpu.make_async_copy(pa.at[0], fbuf.at[i], sem.at[i, 1]).wait()
        pltpu.make_async_copy(shards[0], hbuf.at[i, :FEATS], sem.at[i, 2]).wait()
        delta = jnp.where(lax.rem(i, 2) == 1, -lax.div(i + 1, 2), lax.div(i, 2))
        chunk = lax.rem(z + delta + RING, RING)
        _, skip = column_window(2 * chunk + xh)
        gbuf[...] = jnp.zeros((WINDOW, ROWS), BF16)
        gbuf[pl.ds(pl.multiple_of(skip, 16), FEATS), :] = hbuf[i, :FEATS]
        far_acc[...] += dot(fbuf[i], hbuf[i])
        near_ref[...] += dot(wbuf[i], gbuf[...])
        return carry

    lax.fori_loop(0, RING, one_chunk, 0)
    send_ref[...] = far_acc[...].astype(BF16)


def dout_parts(at, w_out, far_w, shards):
    deltas = tuple(shards)
    assert deltas == (0, -1, 1, -2, 2, -3, 3, -4)
    half = (2 * HD, ROWS)
    return pl.pallas_call(
        lambda *refs: dout_kernel(deltas, *refs),
        name="dout_parts",
        out_shape=(jax.ShapeDtypeStruct(half, F32), pltpu.VMEM(half, BF16)),
        in_specs=[SMEM] + [ANY] * (3 + RING),
        out_specs=(VMEM, VMEM),
        scratch_shapes=[
            pltpu.VMEM((RING, 2 * HD, WINDOW), BF16),
            pltpu.VMEM((RING, 2 * HD, CHUNK), BF16),
            pltpu.VMEM((WINDOW, ROWS), BF16),
            pltpu.VMEM((RING, CHUNK, ROWS), BF16),
            pltpu.VMEM(half, F32),
            pltpu.SemaphoreType.DMA((RING, 3)),
        ],
    )(at, w_out, *far_w, *shards.values())


def join_kernel(core_ref, mine_ref, got_ref, own_ref, *send_refs):
    core = core_ref[0]
    for d in range(HALF + 1):
        at = d - core
        inside = (at >= 0) & (at < HALF)
        other = got_ref[jnp.clip(at, 0, HALF - 1)].astype(F32)
        total = jnp.where(inside, other, 0.0)
        if d < HALF:
            total = total + mine_ref[d].astype(F32)
        if d == 0:
            own_ref[...] = total
        else:
            send_refs[d - 1][...] = total.astype(BF16)


def join_partials(core, mine, got):
    shape = (ROWS, 2 * HD)
    result = pl.pallas_call(
        join_kernel,
        name="join_partials",
        out_shape=(jax.ShapeDtypeStruct(shape, F32),) + (pltpu.VMEM(shape, BF16),) * HALF,
        in_specs=[SMEM, VMEM, VMEM],
        out_specs=(VMEM,) * (HALF + 1),
    )(core, mine, got)
    return result[0], result[1:]


def total_kernel(own_ref, *refs):
    total = own_ref[...]
    for ref in refs[:HALF]:
        total = total + ref[...].astype(F32)
    refs[HALF][...] = total.astype(BF16).T


def total_partials(own, parts):
    return pl.pallas_call(
        total_kernel,
        name="total_partials",
        out_shape=jax.ShapeDtypeStruct((2 * HD, ROWS), BF16),
        in_specs=[VMEM] * (HALF + 1),
        out_specs=VMEM,
    )(own, *parts)


def project_kernel(deltas, own_lanes, far, grad_count, more, at_ref, *refs):
    n, k = len(deltas), len(own_lanes)
    weights, refs = refs[:k], refs[k:]
    grads, refs = refs[:grad_count], refs[grad_count:]
    far_refs, refs = (refs[:RING], refs[RING:]) if far else ((), refs)
    sums, refs = (refs[:n], refs[n:]) if more else ((), refs)
    outs, refs = refs[:n], refs[n:]
    wbuf, gbuf, obuf, sem, g_sem, out_sem, *held = refs
    z, xh, core = at_ref[0], at_ref[1], at_ref[2]
    width = 2 * HD
    g_copies = [
        pltpu.make_async_copy(g, gbuf.at[width * i : width * (i + 1)], g_sem.at[i])
        for i, g in enumerate(grads)
    ]
    for c in g_copies:
        c.start()
    copies = []
    for i, delta in enumerate(deltas):
        chunk = lax.rem(z + delta + RING, RING)
        rows = pl.ds(pl.multiple_of((2 * chunk + xh) * FEATS, 16), FEATS)
        mine = [
            pltpu.make_async_copy(w.at[rows, :], wbuf.at[i, :, lane : lane + size], sem.at[i, j])
            for j, (w, (lane, size)) in enumerate(zip(weights, own_lanes))
        ]
        if more:
            mine.append(pltpu.make_async_copy(sums[i], held[0].at[i], sem.at[i, k + 1]))
        for c in mine:
            c.start()
        if far:
            first, size, lane = far
            other_y = lax.rem(lax.div(chunk, 2), 2) != at_ref[3]
            other = lax.div(chunk, RING // 2) != core
            source = 4 * other.astype(jnp.int32) + 2 * other_y.astype(jnp.int32)
            source = source + lax.rem(chunk, 2)
            for j, ref in enumerate(far_refs):
                copy = pltpu.make_async_copy(
                    ref.at[:, first : first + size],
                    wbuf.at[i, :, lane : lane + size],
                    sem.at[i, k],
                )

                @pl.when(source == j)
                def _(copy=copy):
                    copy.start()

            mine.append(copy)
        copies.append(mine)
    for c in g_copies:
        c.wait()
    results = []
    for i in range(n):
        for c in copies[i]:
            c.wait()
        total = dot(wbuf[i], gbuf[...])
        if more:
            total = total + held[0][i]
        obuf[i] = total.astype(obuf.dtype)
        results.append(pltpu.make_async_copy(obuf.at[i], outs[i], out_sem.at[i]))
        results[-1].start()
    for c in results:
        c.wait()


def project(deltas, at, weights, own_lanes, far, far_rows, grads, sums, kind):
    n, k = len(deltas), len(weights)
    more = len(sums) > 0
    depth = 2 * HD * len(grads)
    return pl.pallas_call(
        lambda *refs: project_kernel(deltas, own_lanes, far, len(grads), more, *refs),
        name="project",
        out_shape=((jax.ShapeDtypeStruct if kind == F32 else pltpu.VMEM)((FEATS, ROWS), kind),) * n,
        in_specs=[SMEM] + [ANY] * (k + len(grads) + len(far_rows) + len(sums)),
        out_specs=(ANY,) * n,
        scratch_shapes=[
            pltpu.VMEM((n, FEATS, depth), BF16),
            pltpu.VMEM((depth, ROWS), BF16),
            pltpu.VMEM((n, FEATS, ROWS), kind),
            pltpu.SemaphoreType.DMA((n, k + 2)),
            pltpu.SemaphoreType.DMA((len(grads),)),
            pltpu.SemaphoreType.DMA((n,)),
        ]
        + [pltpu.VMEM((n, FEATS, ROWS), F32)] * more,
    )(at, *weights, *grads, *far_rows, *sums)


def arrive(x):
    return pltpu.with_memory_space_constraint(x, pltpu.VMEM)


def swapped(x, axis):
    return lax.ppermute(x, axis, [(0, 1), (1, 0)])


def next_y(x):
    return lax.ppermute(x, "y", [(0, 1), (1, 0), (2, 3), (3, 2)])


def chip_pairs(d):
    return [(i, i + 2 * d) for i in range(lax.axis_size(AA) - 2 * d) if d < HALF or i % 2]


def chips_on(x, d):
    return lax.ppermute(x, AA, chip_pairs(d))


def chips_back(x, d):
    return arrive(lax.ppermute(x, AA, [(j, i) for i, j in chip_pairs(d)]))


def round_z(x, step):
    return lax.ppermute(x, "z", [(i, (i + step) % RING) for i in range(RING)])


def body(query, keys, values, grad_out, segment_ids, w_query, w_key, w_value, w_out):
    core = lax.axis_index("core")
    z = lax.axis_index("z")
    xh = lax.axis_index("xh")
    own = lax.axis_index(AA)[None]
    pair = lax.axis_index("y") % 2
    at = jnp.stack((z, xh, core, pair))
    shards = {0: grad_out.T}
    for k in range(1, RING // 2 + 1):
        shards[-k] = round_z(shards[1 - k], 1)
        if k < RING // 2:
            shards[k] = round_z(shards[k - 1], -1)
    send_w = split_w_out(at, w_out)
    far_w = swapped(send_w, "xh")
    far_w = (far_w, arrive(swapped(far_w, "core")))
    ids = jnp.pad(
        segment_ids.astype(BF16).reshape(ROWS // HD, HD),
        ((0, SEG_ROWS - ROWS // HD), (0, HD)),
    )
    block = jnp.concatenate((jnp.concatenate((keys, values), axis=1), ids), axis=0)
    twins = [block] + [chips_on(block, d) for d in range(1, HALF + 1)]
    others = [swapped(twins[d], "core") for d in range(HALF + 1)]
    mine, theirs = [], []
    for k in range(2):
        wanted = []
        for w in (w_query, w_key, w_value):
            w = w.reshape(2, 2, 2, 2, FEATS, -1)
            w = lax.dynamic_index_in_dim(w, core, 0, keepdims=False)
            w = lax.dynamic_index_in_dim(w, pair, 0, keepdims=False)
            wanted.append(lax.dynamic_index_in_dim(w[k], 1 - xh, 0, keepdims=False))
        wanted = jnp.concatenate(wanted, axis=1)
        mine.append(swapped(wanted, "xh"))
        theirs.append(next_y(mine[k]))
    far_rows = (*mine, *theirs)
    far_rows += tuple(swapped(x, "core") for x in far_rows)

    qseg = segment_ids[None, :]
    state = attention_stats(own, qseg, query, twins, others, NEAR, BLOCKS)
    near, send = dout_parts(at, w_out, far_w, shards)
    far = arrive(swapped(send, "xh"))
    stats = attention_stats(own, qseg, query, twins, others, 0, NEAR, state)
    gqt, mine, theirs = attention_grads(own, stats, query, near, far, twins, others)
    got = arrive(swapped(theirs, "core"))
    gqt_far = arrive(swapped(gqt, "xh"))
    own_total, sends = join_partials(core[None], mine, got)
    parts = [chips_back(sends[d - 1], d) for d in range(HALF, 0, -1)]
    gkvt = total_partials(own_total, parts)
    gkvt_far = arrive(swapped(gkvt, "xh"))

    deltas = (4, -3, 3, -2, 2, -1, 1, 0)
    wide = 2 * HD
    q_lanes = ((0, wide),)
    kv_lanes = ((0, HD), (HD, HD))
    kv = (w_key, w_value)
    sums = project(deltas, at, (w_query,), q_lanes, (), (), (gqt,), (), F32)
    first = project(
        deltas[:2], at, kv, kv_lanes, (0, wide, wide), far_rows,
        (gkvt, gqt_far), sums[:2], F32,
    )
    ahead, behind = project(
        deltas[:2], at, (), (), (wide, wide, 0), far_rows,
        (gkvt_far,), first, BF16,
    )
    rest = ()
    for some in (slice(2, 6), slice(6, 8)):
        rest += project(
            deltas[some], at, kv, kv_lanes, (0, 2 * wide, wide), far_rows,
            (gkvt, gqt_far, gkvt_far), sums[some], F32,
        )
    ahead = round_z(ahead, 1)
    behind = round_z(behind, -1)
    for k in (2, 3):
        add_ahead, add_behind = rest[2 * k - 4], rest[2 * k - 3]
        ahead = round_z((ahead.astype(F32) + add_ahead).astype(BF16), 1)
        behind = round_z((behind.astype(F32) + add_behind).astype(BF16), -1)
    ahead = round_z((ahead.astype(F32) + rest[4]).astype(BF16), 1)
    result = (ahead.astype(F32) + behind.astype(F32) + rest[5]).astype(BF16)
    return result.T


def solution(mesh):
    finer = Mesh(mesh.devices.reshape(2, 4, 2, RING, 2), AA + BA)
    return jax.shard_map(
        body,
        mesh=finer,
        in_specs=(
            P(AA, BA),
            P(AA, BA),
            P(AA, BA),
            P(AA, BA),
            P(AA),
            P(None, BA),
            P(None, BA),
            P(None, BA),
            P(BA, None),
        ),
        out_specs=P(AA, BA),
        check_vma=False,
    )
```

```python
import math

import jax
import jax.numpy as jnp
from jax import lax
from jax.experimental import pallas as pl
from jax.experimental.pallas import tpu as pltpu
from jax.sharding import Mesh
from jax.sharding import PartitionSpec as P


D = 5376
HQ = 32
HD = 128
DOCS = 6
ROWS = 384
HALF = 5
BLOCKS = 2 * HALF
SEG_ROWS = 16
PACKED = ROWS + SEG_ROWS
FEATS = 336
CHUNK = 384
WINDOW = 512
BOTH = 2 * ROWS
TILE = 256
STATS_TILE = 128
NEAR = 6
RING = 8
AA = ("xl", "y", "core")
BA = ("z", "xh")
NEG_FILL = -1e30
SCALE = (D / HQ) ** (-0.5)
SCALE2 = SCALE * math.log2(math.e)
F32 = jnp.float32
BF16 = jnp.bfloat16
VMEM = pl.BlockSpec(memory_space=pltpu.VMEM)
SMEM = pl.BlockSpec(memory_space=pltpu.SMEM)
ANY = pl.BlockSpec(memory_space=pl.ANY)


def dot(a, b):
    return lax.dot_general(a, b, (((1,), (0,)), ((), ())), preferred_element_type=F32)


def sources(low, high):
    odd = [d for d in range(HALF) if low <= BLOCKS - 1 - 2 * d < high]
    even = [k for k in range(HALF) if low <= BLOCKS - 2 - 2 * k < high]
    return odd, even, sorted({k for e in even for k in (e, e + 1)})


def load_window(low, high, core, kv_refs, buf, sem):
    odd, even, extra = sources(low, high)
    twin = dict(zip(odd, kv_refs))
    other = dict(zip(extra, kv_refs[len(odd) :]))
    copies = []
    for d in odd:
        at = BLOCKS - 1 - 2 * d - low
        copies.append(pltpu.make_async_copy(twin[d], buf.at[at], sem.at[at]))
        copies[-1].start()
    for k in even:
        at = BLOCKS - 2 - 2 * k - low
        from_low = pltpu.make_async_copy(other[k], buf.at[at], sem.at[at])
        from_high = pltpu.make_async_copy(other[k + 1], buf.at[at], sem.at[at])

        @pl.when(core == 1)
        def _(copy=from_low):
            copy.start()

        @pl.when(core == 0)
        def _(copy=from_high):
            copy.start()

        copies.append(from_low)
    return copies


def window_refs(low, high, twins, others):
    odd, _, extra = sources(low, high)
    return [twins[d] for d in odd] + [others[k] for k in extra]


def side_by_side(x):
    return jnp.concatenate((x[:HD, :], x[HD:, :]), axis=1)


def one_above_other(x):
    return jnp.concatenate((x[:, :HD], x[:, HD:]), axis=0)


def tiles(width):
    return [slice(t, t + width) for t in range(0, BOTH, width)]


def stats_kernel(low, high, own_ref, qseg_ref, q_ref, *refs):
    near = high == BLOCKS
    odd, _, extra = sources(low, high)
    count = len(odd) + len(extra)
    if near:
        kv_refs = refs[:count]
        m_ref, l_ref, out_ref, start_ref, buf, qt_ref, sem = refs[count:]
    else:
        m_in, l_in, out_in, start_in = refs[:4]
        kv_refs = refs[4 : 4 + count]
        lse_ref, out_ref, start_ref, low_ref, buf, qt_ref, m_ref, l_ref, sem = refs[4 + count :]
    own = own_ref[0]
    copies = load_window(low, high, lax.rem(own, 2), kv_refs, buf, sem)
    qt_ref[...] = one_above_other(q_ref[...]).T
    if near:
        m_ref[...] = jnp.full(m_ref.shape, NEG_FILL, F32)
        l_ref[...] = jnp.zeros(l_ref.shape, F32)
        out_ref[...] = jnp.zeros(out_ref.shape, F32)
    else:
        m_ref[...] = m_in[...]
        l_ref[...] = l_in[...]
        out_ref[...] = out_in[...]
    seg = qseg_ref[...]
    seg0 = jnp.min(seg, axis=1, keepdims=True)
    for c in copies:
        c.wait()
    before = jnp.zeros((SEG_ROWS, HD), jnp.int32)
    line = lax.broadcasted_iota(jnp.int32, (SEG_ROWS, HD), 0)
    for b in range(low, min(high, BLOCKS - 1)):
        ids = buf[b - low, ROWS:, :HD].astype(F32).astype(jnp.int32)
        hit = (line < ROWS // HD) & (ids < seg0) & (own + b >= BLOCKS - 1)
        before = before + hit.astype(jnp.int32)
    start0 = jnp.sum(before) + jnp.maximum(own + low - (BLOCKS - 1), 0) * ROWS
    first_next = (own + high - (BLOCKS - 1)) * ROWS
    start = jnp.zeros((1, ROWS), jnp.int32) + start0
    if near:
        for s in range(1, DOCS):
            here = own * ROWS + jnp.sum((seg < s).astype(jnp.int32), axis=1, keepdims=True)
            start = jnp.where((seg == s) & (seg > seg0), here, start)
        start_ref[...] = start
    else:
        start = jnp.where((seg == seg0) & (start0 < first_next), start, start_in[...])
        start_ref[...] = start
        start0 = jnp.min(start)
    lowest = lax.div(start0, ROWS) - own + (BLOCKS - 1)
    latest = jnp.max(start)
    pos = own * ROWS + lax.broadcasted_iota(jnp.int32, (1, ROWS), 1)
    start = jnp.concatenate((start, start), axis=1)
    pos = jnp.concatenate((pos, pos), axis=1)
    key_at = lax.broadcasted_iota(jnp.int32, (ROWS, STATS_TILE), 0)

    def add_block(b, first, whole):
        kb = buf[b - low, :ROWS, :HD]
        vt = buf[b - low, :ROWS, HD:].T
        for t in tiles(STATS_TILE):
            s = dot(kb, qt_ref[:, t]) * SCALE2
            if not whole:
                allowed = (key_at >= start[:, t] - first) & (key_at <= pos[:, t] - first)
                s = jnp.where(allowed, s, NEG_FILL)
            m_old = m_ref[:, t]
            m_new = jnp.maximum(m_old, jnp.max(s, axis=0, keepdims=True))
            p = jnp.exp2(s - m_new)
            back = jnp.exp2(m_old - m_new)
            l_ref[:, t] = l_ref[:, t] * back + jnp.sum(p, axis=0, keepdims=True)
            m_ref[:, t] = m_new
            out_ref[:, t] = out_ref[:, t] * back + dot(vt, p.astype(BF16))

    def one_block(back_to, carry):
        b = high - 1 - back_to
        first = (own + b - (BLOCKS - 1)) * ROWS
        whole = (first >= latest) & (b < BLOCKS - 1)

        @pl.when(whole)
        def _():
            add_block(b, first, True)

        @pl.when(jnp.logical_not(whole))
        def _():
            add_block(b, first, False)

        return carry

    lax.fori_loop(0, high - jnp.clip(lowest, low, high), one_block, 0)
    if not near:
        low_ref[0] = lowest
        lse_ref[...] = m_ref[...] + jnp.log2(l_ref[...])
        out_ref[...] = out_ref[...] / l_ref[...]


def grads_kernel(own_ref, low_ref, *refs):
    given, refs = refs[:6], refs[6:]
    kv_refs, refs = refs[: BLOCKS + 1], refs[BLOCKS + 1 :]
    gqt_ref, mine_ref, theirs_ref = refs[:3]
    start_ref, q_ref, near_ref, far_ref, lse_ref, out_ref = held = refs[3:9]
    buf, qt_ref, qn_ref, dout_ref, doutt_ref, delta_ref, acc_ref, made, sem, in_sem, out_sem = refs[9:]
    own = own_ref[0]
    arrivals = [pltpu.make_async_copy(x, y, in_sem.at[i]) for i, (x, y) in enumerate(zip(given, held))]
    for c in arrivals:
        c.start()
    load_window(0, BLOCKS, lax.rem(own, 2), kv_refs, buf, sem)
    lowest = low_ref[0]
    acc_ref[...] = jnp.zeros(acc_ref.shape, F32)
    key_at = lax.broadcasted_iota(jnp.int32, (ROWS, TILE), 0)
    for c in arrivals:
        c.wait()
    qn_ref[...] = one_above_other(q_ref[...])
    qt_ref[...] = qn_ref[...].T
    doutt_ref[...] = side_by_side((near_ref[...] + far_ref[...].astype(F32)).astype(BF16))
    dout_ref[...] = doutt_ref[...].T
    delta_ref[...] = jnp.sum(doutt_ref[...].astype(F32) * out_ref[...], axis=0, keepdims=True)
    start = start_ref[...]
    latest = jnp.max(start)
    pos = own * ROWS + lax.broadcasted_iota(jnp.int32, (1, ROWS), 1)
    start = jnp.concatenate((start, start), axis=1)
    pos = jnp.concatenate((pos, pos), axis=1)

    def add_block(b, first, whole):
        kb = buf[b, :ROWS, :HD]
        vb = buf[b, :ROWS, HD:]
        kt = kb.T
        gk = gv = None
        for t in tiles(TILE):
            s = dot(kb, qt_ref[:, t]) * SCALE2
            dp = dot(vb, doutt_ref[:, t])
            p = jnp.exp2(s - lse_ref[:, t])
            if not whole:
                allowed = (key_at >= start[:, t] - first) & (key_at <= pos[:, t] - first)
                p = jnp.where(allowed, p, 0.0)
            ds = (p * (dp - delta_ref[:, t])).astype(BF16)
            add_v = dot(p.astype(BF16), dout_ref[t, :])
            add_k = dot(ds, qn_ref[t, :])
            gv = add_v if gv is None else gv + add_v
            gk = add_k if gk is None else gk + add_k
            acc_ref[:, t] += dot(kt, ds)
        made[b, :, :HD] = (gk * SCALE).astype(BF16)
        made[b, :, HD:] = gv.astype(BF16)

    def departure(b, target):
        d = (BLOCKS - 1 - b) // 2 if isinstance(b, int) else lax.div(BLOCKS - 1 - b, 2)
        return pltpu.make_async_copy(made.at[b], target.at[d], out_sem.at[b])

    def one_block(b, carry):
        pltpu.make_async_copy(kv_refs[0], buf.at[b], sem.at[b]).wait()
        first = (own + b - (BLOCKS - 1)) * ROWS
        whole = (first >= latest) & (b < BLOCKS - 1)

        @pl.when((b >= lowest) & whole)
        def _():
            add_block(b, first, True)

        @pl.when((b >= lowest) & jnp.logical_not(whole))
        def _():
            add_block(b, first, False)

        @pl.when(b < lowest)
        def _():
            made[b] = jnp.zeros((ROWS, 2 * HD), BF16)

        odd = lax.rem(b, 2) == 1

        @pl.when(odd)
        def _():
            departure(b, mine_ref).start()

        @pl.when(jnp.logical_not(odd))
        def _():
            departure(b, theirs_ref).start()

        return carry

    lax.fori_loop(0, BLOCKS, one_block, 0)
    gqt_ref[:HD, :] = (acc_ref[:, :ROWS] * SCALE).astype(BF16)
    gqt_ref[HD:, :] = (acc_ref[:, ROWS:] * SCALE).astype(BF16)
    for b in range(BLOCKS):
        departure(b, mine_ref if b % 2 else theirs_ref).wait()


def attention_stats(own, qseg, query, twins, others, low, high, state=()):
    count = high - low
    window = window_refs(low, high, twins, others)
    row = jax.ShapeDtypeStruct((1, BOTH), F32)
    wide = jax.ShapeDtypeStruct((HD, BOTH), F32)
    start = jax.ShapeDtypeStruct((1, ROWS), jnp.int32)
    lowest = jax.ShapeDtypeStruct((1,), jnp.int32)
    scratch = [
        pltpu.VMEM((count, PACKED, 2 * HD), BF16),
        pltpu.VMEM((HD, BOTH), BF16),
    ]
    if state:
        scratch += [pltpu.VMEM((1, BOTH), F32), pltpu.VMEM((1, BOTH), F32)]
    return pl.pallas_call(
        lambda *refs: stats_kernel(low, high, *refs),
        name="stats_far" if state else "stats_near",
        out_shape=(row, wide, start, lowest) if state else (row, row, wide, start),
        in_specs=[SMEM, VMEM, VMEM] + [VMEM] * len(state) + [ANY] * len(window),
        out_specs=(VMEM, VMEM, VMEM, SMEM if state else VMEM),
        scratch_shapes=scratch + [pltpu.SemaphoreType.DMA((count,))],
    )(own, qseg, query, *state, *window)


def attention_grads(own, stats, query, near, far, twins, others):
    lse, out, start, lowest = stats
    window = window_refs(0, BLOCKS, twins, others)
    given = (start, query, near, far, lse, out)
    return pl.pallas_call(
        grads_kernel,
        name="attention_grads",
        out_shape=(
            jax.ShapeDtypeStruct((2 * HD, ROWS), BF16),
            jax.ShapeDtypeStruct((HALF, ROWS, 2 * HD), BF16),
            jax.ShapeDtypeStruct((HALF, ROWS, 2 * HD), BF16),
        ),
        in_specs=[SMEM, SMEM] + [ANY] * (len(given) + len(window)),
        out_specs=(VMEM, ANY, ANY),
        scratch_shapes=[pltpu.VMEM(x.shape, x.dtype) for x in given]
        + [
            pltpu.VMEM((BLOCKS, PACKED, 2 * HD), BF16),
            pltpu.VMEM((HD, BOTH), BF16),
            pltpu.VMEM((BOTH, HD), BF16),
            pltpu.VMEM((BOTH, HD), BF16),
            pltpu.VMEM((HD, BOTH), BF16),
            pltpu.VMEM((1, BOTH), F32),
            pltpu.VMEM((HD, BOTH), F32),
            pltpu.VMEM((BLOCKS, ROWS, 2 * HD), BF16),
            pltpu.SemaphoreType.DMA((BLOCKS,)),
            pltpu.SemaphoreType.DMA((len(given),)),
            pltpu.SemaphoreType.DMA((BLOCKS,)),
        ],
    )(own, lowest, *given, *window)


def column_window(chunk):
    base = jnp.minimum(lax.div(chunk * FEATS, HD) * HD, D - WINDOW)
    return pl.ds(pl.multiple_of(base, HD), WINDOW), chunk * FEATS - base


def split_kernel(at_ref, w_ref, send_ref, buf, sem):
    first = at_ref[2] * (RING // 2)
    other = 1 - at_ref[1]
    copies = []
    for i in range(RING // 2):
        lanes, skip = column_window(2 * (first + i) + other)
        copy = pltpu.make_async_copy(w_ref.at[:, lanes], buf.at[i], sem.at[i])
        copy.start()
        copies.append((copy, skip))
    lane = lax.broadcasted_iota(jnp.int32, (2 * HD, CHUNK), 1)
    for i, (copy, skip) in enumerate(copies):
        copy.wait()
        moved = pltpu.roll(buf[i].astype(F32), lax.rem(WINDOW - skip, WINDOW), 1)[:, :CHUNK]
        send_ref[i] = jnp.where(lane < FEATS, moved, 0.0).astype(BF16)


def split_w_out(at, w_out):
    n = RING // 2
    return pl.pallas_call(
        split_kernel,
        name="split_w_out",
        out_shape=jax.ShapeDtypeStruct((n, 2 * HD, CHUNK), BF16),
        in_specs=[SMEM, ANY],
        out_specs=VMEM,
        scratch_shapes=[
            pltpu.VMEM((n, 2 * HD, WINDOW), BF16),
            pltpu.SemaphoreType.DMA((n,)),
        ],
    )(at, w_out)


def dout_kernel(deltas, at_ref, w_ref, pa, pb, *refs):
    shards = refs[:RING]
    near_ref, send_ref, wbuf, fbuf, gbuf, hbuf, far_acc, sem = refs[RING:]
    z, xh, core = at_ref[0], at_ref[1], at_ref[2]
    for i in range(RING):
        chunk = lax.rem(z + deltas[i] + RING, RING)
        half = lax.div(chunk, RING // 2)
        inner = lax.rem(chunk, RING // 2)
        lanes, _ = column_window(2 * chunk + xh)
        far = pltpu.make_async_copy(pa.at[inner], fbuf.at[i], sem.at[i, 1])
        far_too = pltpu.make_async_copy(pb.at[inner], fbuf.at[i], sem.at[i, 1])
        pltpu.make_async_copy(w_ref.at[:, lanes], wbuf.at[i], sem.at[i, 0]).start()

        @pl.when(half == core)
        def _(copy=far):
            copy.start()

        @pl.when(half != core)
        def _(copy=far_too):
            copy.start()

        pltpu.make_async_copy(shards[i], hbuf.at[i, :FEATS], sem.at[i, 2]).start()
        hbuf[i, FEATS:] = jnp.zeros((CHUNK - FEATS, ROWS), BF16)
    near_ref[...] = jnp.zeros(near_ref.shape, F32)
    far_acc[...] = jnp.zeros(far_acc.shape, F32)

    def one_chunk(i, carry):
        pltpu.make_async_copy(w_ref.at[:, :WINDOW], wbuf.at[i], sem.at[i, 0]).wait()
        pltpu.make_async_copy(pa.at[0], fbuf.at[i], sem.at[i, 1]).wait()
        pltpu.make_async_copy(shards[0], hbuf.at[i, :FEATS], sem.at[i, 2]).wait()
        delta = jnp.where(lax.rem(i, 2) == 1, -lax.div(i + 1, 2), lax.div(i, 2))
        chunk = lax.rem(z + delta + RING, RING)
        _, skip = column_window(2 * chunk + xh)
        gbuf[...] = jnp.zeros((WINDOW, ROWS), BF16)
        gbuf[pl.ds(pl.multiple_of(skip, 16), FEATS), :] = hbuf[i, :FEATS]
        far_acc[...] += dot(fbuf[i], hbuf[i])
        near_ref[...] += dot(wbuf[i], gbuf[...])
        return carry

    lax.fori_loop(0, RING, one_chunk, 0)
    send_ref[...] = far_acc[...].astype(BF16)


def dout_parts(at, w_out, far_w, shards):
    deltas = tuple(shards)
    assert deltas == (0, -1, 1, -2, 2, -3, 3, -4)
    half = (2 * HD, ROWS)
    return pl.pallas_call(
        lambda *refs: dout_kernel(deltas, *refs),
        name="dout_parts",
        out_shape=(jax.ShapeDtypeStruct(half, F32), pltpu.VMEM(half, BF16)),
        in_specs=[SMEM] + [ANY] * (3 + RING),
        out_specs=(VMEM, VMEM),
        scratch_shapes=[
            pltpu.VMEM((RING, 2 * HD, WINDOW), BF16),
            pltpu.VMEM((RING, 2 * HD, CHUNK), BF16),
            pltpu.VMEM((WINDOW, ROWS), BF16),
            pltpu.VMEM((RING, CHUNK, ROWS), BF16),
            pltpu.VMEM(half, F32),
            pltpu.SemaphoreType.DMA((RING, 3)),
        ],
    )(at, w_out, *far_w, *shards.values())


def join_kernel(core_ref, mine_ref, got_ref, own_ref, *send_refs):
    core = core_ref[0]
    for d in range(HALF + 1):
        at = d - core
        inside = (at >= 0) & (at < HALF)
        other = got_ref[jnp.clip(at, 0, HALF - 1)].astype(F32)
        total = jnp.where(inside, other, 0.0)
        if d < HALF:
            total = total + mine_ref[d].astype(F32)
        if d == 0:
            own_ref[...] = total
        else:
            send_refs[d - 1][...] = total.astype(BF16)


def join_partials(core, mine, got):
    shape = (ROWS, 2 * HD)
    result = pl.pallas_call(
        join_kernel,
        name="join_partials",
        out_shape=(jax.ShapeDtypeStruct(shape, F32),) + (pltpu.VMEM(shape, BF16),) * HALF,
        in_specs=[SMEM, VMEM, VMEM],
        out_specs=(VMEM,) * (HALF + 1),
    )(core, mine, got)
    return result[0], result[1:]


def total_kernel(own_ref, *refs):
    total = own_ref[...]
    for ref in refs[:HALF]:
        total = total + ref[...].astype(F32)
    refs[HALF][...] = total.astype(BF16).T


def total_partials(own, parts):
    return pl.pallas_call(
        total_kernel,
        name="total_partials",
        out_shape=jax.ShapeDtypeStruct((2 * HD, ROWS), BF16),
        in_specs=[VMEM] * (HALF + 1),
        out_specs=VMEM,
    )(own, *parts)


def project_kernel(deltas, own_lanes, far, grad_count, more, at_ref, *refs):
    n, k = len(deltas), len(own_lanes)
    weights, refs = refs[:k], refs[k:]
    grads, refs = refs[:grad_count], refs[grad_count:]
    far_refs, refs = (refs[:RING], refs[RING:]) if far else ((), refs)
    sums, refs = (refs[:n], refs[n:]) if more else ((), refs)
    outs, refs = refs[:n], refs[n:]
    wbuf, gbuf, obuf, sem, g_sem, out_sem, *held = refs
    z, xh, core = at_ref[0], at_ref[1], at_ref[2]
    width = 2 * HD
    g_copies = [
        pltpu.make_async_copy(g, gbuf.at[width * i : width * (i + 1)], g_sem.at[i])
        for i, g in enumerate(grads)
    ]
    for c in g_copies:
        c.start()
    copies = []
    for i, delta in enumerate(deltas):
        chunk = lax.rem(z + delta + RING, RING)
        rows = pl.ds(pl.multiple_of((2 * chunk + xh) * FEATS, 16), FEATS)
        mine = [
            pltpu.make_async_copy(w.at[rows, :], wbuf.at[i, :, lane : lane + size], sem.at[i, j])
            for j, (w, (lane, size)) in enumerate(zip(weights, own_lanes))
        ]
        if more:
            mine.append(pltpu.make_async_copy(sums[i], held[0].at[i], sem.at[i, k + 1]))
        for c in mine:
            c.start()
        if far:
            first, size, lane = far
            other_y = lax.rem(lax.div(chunk, 2), 2) != at_ref[3]
            other = lax.div(chunk, RING // 2) != core
            source = 4 * other.astype(jnp.int32) + 2 * other_y.astype(jnp.int32)
            source = source + lax.rem(chunk, 2)
            for j, ref in enumerate(far_refs):
                copy = pltpu.make_async_copy(
                    ref.at[:, first : first + size],
                    wbuf.at[i, :, lane : lane + size],
                    sem.at[i, k],
                )

                @pl.when(source == j)
                def _(copy=copy):
                    copy.start()

            mine.append(copy)
        copies.append(mine)
    for c in g_copies:
        c.wait()
    results = []
    for i in range(n):
        for c in copies[i]:
            c.wait()
        total = dot(wbuf[i], gbuf[...])
        if more:
            total = total + held[0][i]
        obuf[i] = total.astype(obuf.dtype)
        results.append(pltpu.make_async_copy(obuf.at[i], outs[i], out_sem.at[i]))
        results[-1].start()
    for c in results:
        c.wait()


def project(deltas, at, weights, own_lanes, far, far_rows, grads, sums, kind):
    n, k = len(deltas), len(weights)
    more = len(sums) > 0
    depth = 2 * HD * len(grads)
    return pl.pallas_call(
        lambda *refs: project_kernel(deltas, own_lanes, far, len(grads), more, *refs),
        name="project",
        out_shape=((jax.ShapeDtypeStruct if kind == F32 else pltpu.VMEM)((FEATS, ROWS), kind),) * n,
        in_specs=[SMEM] + [ANY] * (k + len(grads) + len(far_rows) + len(sums)),
        out_specs=(ANY,) * n,
        scratch_shapes=[
            pltpu.VMEM((n, FEATS, depth), BF16),
            pltpu.VMEM((depth, ROWS), BF16),
            pltpu.VMEM((n, FEATS, ROWS), kind),
            pltpu.SemaphoreType.DMA((n, k + 2)),
            pltpu.SemaphoreType.DMA((len(grads),)),
            pltpu.SemaphoreType.DMA((n,)),
        ]
        + [pltpu.VMEM((n, FEATS, ROWS), F32)] * more,
    )(at, *weights, *grads, *far_rows, *sums)


def add_kernel(ahead_ref, up_ref, behind_ref, down_ref, ahead_out, behind_out):
    ahead_out[...] = (ahead_ref[...].astype(F32) + up_ref[...]).astype(BF16)
    behind_out[...] = (behind_ref[...].astype(F32) + down_ref[...]).astype(BF16)


def add_both(ahead, up, behind, down):
    return pl.pallas_call(
        add_kernel,
        name="add_both",
        out_shape=(pltpu.VMEM((FEATS, ROWS), BF16),) * 2,
        in_specs=[VMEM] * 4,
        out_specs=(VMEM, VMEM),
    )(arrive(ahead), arrive(up), arrive(behind), arrive(down))


def arrive(x):
    return pltpu.with_memory_space_constraint(x, pltpu.VMEM)


def swapped(x, axis):
    return lax.ppermute(x, axis, [(0, 1), (1, 0)])


def next_y(x):
    return lax.ppermute(x, "y", [(0, 1), (1, 0), (2, 3), (3, 2)])


def chip_pairs(d):
    return [(i, i + 2 * d) for i in range(lax.axis_size(AA) - 2 * d) if d < HALF or i % 2]


def chips_on(x, d):
    return lax.ppermute(x, AA, chip_pairs(d))


def chips_back(x, d):
    return arrive(lax.ppermute(x, AA, [(j, i) for i, j in chip_pairs(d)]))


def round_z(x, step):
    return lax.ppermute(x, "z", [(i, (i + step) % RING) for i in range(RING)])


def body(query, keys, values, grad_out, segment_ids, w_query, w_key, w_value, w_out):
    core = lax.axis_index("core")
    z = lax.axis_index("z")
    xh = lax.axis_index("xh")
    own = lax.axis_index(AA)[None]
    pair = lax.axis_index("y") % 2
    at = jnp.stack((z, xh, core, pair))
    shards = {0: grad_out.T}
    for k in range(1, RING // 2 + 1):
        shards[-k] = round_z(shards[1 - k], 1)
        if k < RING // 2:
            shards[k] = round_z(shards[k - 1], -1)
    send_w = split_w_out(at, w_out)
    far_w = swapped(send_w, "xh")
    far_w = (far_w, arrive(swapped(far_w, "core")))
    ids = jnp.pad(
        segment_ids.astype(BF16).reshape(ROWS // HD, HD),
        ((0, SEG_ROWS - ROWS // HD), (0, HD)),
    )
    block = jnp.concatenate((jnp.concatenate((keys, values), axis=1), ids), axis=0)
    twins = [block] + [chips_on(block, d) for d in range(1, HALF + 1)]
    others = [swapped(twins[d], "core") for d in range(HALF + 1)]
    mine, theirs = [], []
    for k in range(2):
        wanted = []
        for w in (w_query, w_key, w_value):
            w = w.reshape(2, 2, 2, 2, FEATS, -1)
            w = lax.dynamic_index_in_dim(w, core, 0, keepdims=False)
            w = lax.dynamic_index_in_dim(w, pair, 0, keepdims=False)
            wanted.append(lax.dynamic_index_in_dim(w[k], 1 - xh, 0, keepdims=False))
        wanted = jnp.concatenate(wanted, axis=1)
        mine.append(swapped(wanted, "xh"))
        theirs.append(next_y(mine[k]))
    far_rows = (*mine, *theirs)
    far_rows += tuple(swapped(x, "core") for x in far_rows)

    qseg = segment_ids[None, :]
    state = attention_stats(own, qseg, query, twins, others, NEAR, BLOCKS)
    near, send = dout_parts(at, w_out, far_w, shards)
    far = arrive(swapped(send, "xh"))
    stats = attention_stats(own, qseg, query, twins, others, 0, NEAR, state)
    gqt, mine, theirs = attention_grads(own, stats, query, near, far, twins, others)
    got = arrive(swapped(theirs, "core"))
    gqt_far = arrive(swapped(gqt, "xh"))
    own_total, sends = join_partials(core[None], mine, got)
    parts = [chips_back(sends[d - 1], d) for d in range(HALF, 0, -1)]
    gkvt = total_partials(own_total, parts)
    gkvt_far = arrive(swapped(gkvt, "xh"))

    deltas = (4, -3, 3, -2, 2, -1, 1, 0)
    wide = 2 * HD
    q_lanes = ((0, wide),)
    kv_lanes = ((0, HD), (HD, HD))
    kv = (w_key, w_value)
    sums = project(deltas, at, (w_query,), q_lanes, (), (), (gqt,), (), F32)
    first = project(
        deltas[:2], at, kv, kv_lanes, (0, wide, wide), far_rows,
        (gkvt, gqt_far), sums[:2], F32,
    )
    ahead, behind = project(
        deltas[:2], at, (), (), (wide, wide, 0), far_rows,
        (gkvt_far,), first, BF16,
    )
    rest = ()
    for some in (slice(2, 6), slice(6, 8)):
        rest += project(
            deltas[some], at, kv, kv_lanes, (0, 2 * wide, wide), far_rows,
            (gkvt, gqt_far, gkvt_far), sums[some], F32,
        )
    ahead = round_z(ahead, 1)
    behind = round_z(behind, -1)
    for k in (2, 3):
        up, down = rest[2 * k - 4], rest[2 * k - 3]
        if k == 2:
            ahead = (ahead.astype(F32) + up).astype(BF16)
            behind = (behind.astype(F32) + down).astype(BF16)
        else:
            ahead, behind = add_both(ahead, up, behind, down)
        ahead = round_z(ahead, 1)
        behind = round_z(behind, -1)
    ahead = round_z((ahead.astype(F32) + rest[4]).astype(BF16), 1)
    result = (ahead.astype(F32) + behind.astype(F32) + rest[5]).astype(BF16)
    return result.T


def solution(mesh):
    finer = Mesh(mesh.devices.reshape(2, 4, 2, RING, 2), AA + BA)
    return jax.shard_map(
        body,
        mesh=finer,
        in_specs=(
            P(AA, BA),
            P(AA, BA),
            P(AA, BA),
            P(AA, BA),
            P(AA),
            P(None, BA),
            P(None, BA),
            P(None, BA),
            P(BA, None),
        ),
        out_specs=P(AA, BA),
        check_vma=False,
    )
```
